256 devices in a mesh: view: 16 (over z, core), blk: 16 (over y, x).
Axes of the slice: x: 4, y: 4, z: 8, core: 2. Of those that a mesh axis runs over, the one named last changes fastest.
Arguments:
- estimate: float32 [256, 128, 128], P('blk'), may hold values from 0.5 to 2
- images: bfloat16 [16, 256, 64, 128], P('view', 'blk'), may hold values from 0.5 to 2
- point_spread: float32 [8, 9, 7, 25], replicated, may hold values from 0.01 to 1
- covered: int32 [8, 16, 4], P(None, 'blk'), may hold values from 0 to 1, as said below
Outputs:
- estimate_next: float32 [256, 128, 128], P('blk')
The draws below stay inside these ranges and needn't reach their ends.
Inputs may be any that keep to these rules, and one draw needn't show every extreme that they name: For each view and each block layer along the first dimension, the covered blocks are consecutive along the second dimension and at most 3; for every view some block layer has exactly 3.
All inputs are finite; a program needn't handle non-finite values.
Results may differ from the reference program's by a relative error of at most 0.0003.
Values may be sent and summed in bfloat16 or wider, within the bound.
A program may use at most 64 MiB of HBM per device.

```python
import math
import jax
import jax.numpy as jnp
from jax import lax

VIEWS = 8
KX = 9
KY = 7
KZ = 25
SX = 16
BY = 32
NBY = 4
SHARES = 2
CAP = 3
NBX = 16
NX = 256
NY = 128
NZ = 128
N_VIEW = 16


def draw_covered(key, part):
    key_count = jax.random.fold_in(key, 11)
    key_pick = jax.random.fold_in(key, 12)
    key_start = jax.random.fold_in(key, 13)
    counts = jax.random.randint(key_count, (VIEWS, NBX), 0, CAP + 1)
    chosen = jax.random.randint(key_pick, (VIEWS,), 0, NBX)
    layer_index = jnp.arange(NBX, dtype=jnp.int32)
    counts = jnp.where(layer_index[None, :] == chosen[:, None], CAP, counts)
    starts = jax.random.randint(key_start, (VIEWS, NBX), 0, NBY - counts + 1)
    position = jnp.arange(NBY, dtype=jnp.int32)[None, None, :]
    inside = (position >= starts[:, :, None]) & (position < starts[:, :, None] + counts[:, :, None])
    return inside.astype(jnp.int32)


def block_levels(stream_key, dims, shards, low, high):
    level = 1.0
    for axis_at, blocks in shards:
        heights = jax.random.uniform(jax.random.fold_in(jax.random.fold_in(stream_key, 6), axis_at), (blocks,), jnp.float32, low / len(shards), high / len(shards))
        level = level * jnp.repeat(jnp.exp(heights), dims[axis_at] // blocks).reshape((-1,) + (1,) * (len(dims) - 1 - axis_at))
    return level


def setup_inputs(seed: int = 0) -> dict:
    streams_of = jax.random.split(jax.random.key(seed), 5)
    return {
        "estimate": jnp.clip(0.5 + 1.5 * jax.random.uniform(streams_of[0], (NX, NY, NZ), jnp.float32) ** block_levels(streams_of[0], (NX, NY, NZ), ((0, 16),), -0.2, 0.2), 0.5, 2.0),
        "images": jnp.clip(jnp.exp(math.log(2.0) - 1.3862944 * jax.random.uniform(streams_of[1], (N_VIEW, NX, NY // SHARES, NZ), jnp.float32) ** block_levels(streams_of[1], (N_VIEW, NX, NY // SHARES, NZ), ((0, 16), (1, 16)), -0.2, 0.2)), 0.5, 2.0).astype(jnp.bfloat16),
        "point_spread": jnp.clip(jnp.exp(jax.random.uniform(streams_of[2], (VIEWS, KX, KY, KZ), jnp.float32, math.log(0.01), math.log(1.0))), 0.01, 1.0),
        "covered": draw_covered(jax.random.fold_in(streams_of[4], 71), 0),
    }


def correlate(volume, kernel):
    rims = [((KX - 1) // 2, (KX - 1) // 2), ((KY - 1) // 2, (KY - 1) // 2), ((KZ - 1) // 2, (KZ - 1) // 2)]
    output = lax.conv_general_dilated(volume[None, None].astype(jnp.float32), kernel[None, None].astype(jnp.float32), (1, 1, 1), rims, dimension_numbers=("NCDHW", "OIDHW", "NCDHW"), precision=lax.Precision.HIGHEST)
    return output[0, 0]


def reference(estimate, images, point_spread, covered):
    source = estimate.astype(jnp.bfloat16)
    product_all = jnp.ones(estimate.shape, jnp.float32)
    for view_id in range(VIEWS):
        kernel = (point_spread[view_id] / jnp.sum(point_spread[view_id])).astype(jnp.bfloat16)
        image = jnp.concatenate([images[view_id * SHARES + share] for share in range(SHARES)], axis=1)
        coverage = jnp.repeat(jnp.repeat(covered[view_id], SX, axis=0), BY, axis=1)[:, :, None] > 0
        blurred = correlate(source, kernel)
        quotient = jnp.where(coverage, image.astype(jnp.float32) / blurred, 0.0).astype(jnp.bfloat16)
        correction = correlate(quotient, kernel[::-1, ::-1, ::-1])
        product_all = product_all * jnp.where(coverage, correction, 1.0)
    return estimate * product_all
```

```python
import jax
import jax.numpy as jnp
from jax import lax
from jax.sharding import PartitionSpec as P

BY = 32


def with_halo(cells, sides, width):
    for axis, dim in sides:
        count = lax.axis_size(axis)
        ends = count - 1
        head = lax.slice_in_dim(cells, 0, width, axis=dim)
        tail = lax.slice_in_dim(cells, cells.shape[dim] - width, cells.shape[dim], axis=dim)
        cells = jnp.concatenate(
            [
                lax.ppermute(tail, axis, [(i, (i + 1) % count) for i in range(ends)]),
                cells,
                lax.ppermute(head, axis, [((i + 1) % count, i) for i in range(ends)]),
            ],
            axis=dim,
        )
    return cells


def swapped(block, axis, stride):
    count = lax.axis_size(axis)
    route = []
    for low in range(count):
        high = low | 1 << stride
        if high != low and high < count:
            route += [(low, high), (high, low)]
    return lax.ppermute(block, axis, route)


def merged(part, axis, combine):
    gathered = lax.all_gather(part, axis)

    def take(source):
        return lax.dynamic_index_in_dim(gathered, source, 0, False)

    return lax.fori_loop(
        1, lax.axis_size(axis), lambda source, state: combine(state, take(source)), take(0)
    )


def band_table(kernel, depth):
    taps_x, taps_y, taps_z = kernel.shape
    span_z = depth + taps_z - 1
    shape_three = (taps_z, span_z, depth)
    offset = lax.broadcasted_iota(jnp.int32, shape_three, 1) - lax.broadcasted_iota(
        jnp.int32, shape_three, 2
    )
    onehot = (offset == lax.broadcasted_iota(jnp.int32, shape_three, 0)).astype(jnp.bfloat16)
    banded = jnp.einsum("abt,tpz->abpz", kernel, onehot, preferred_element_type=jnp.float32).astype(
        jnp.bfloat16
    )
    inner_width = taps_y * span_z
    padded_width = -(-inner_width // 128) * 128
    banded = banded.reshape(taps_x, inner_width, depth)
    return jnp.pad(banded, ((0, 0), (0, padded_width - inner_width), (0, 0)))


def convolve(padded_part, banded, rows_x, rows_y):
    taps_x = padded_part.shape[0] - rows_x + 1
    taps_y = padded_part.shape[1] - rows_y + 1
    columns = jnp.concatenate(
        [padded_part[:, step_y : step_y + rows_y, :] for step_y in range(taps_y)], axis=2
    )
    columns = jnp.pad(columns, ((0, 0), (0, 0), (0, banded.shape[1] - columns.shape[2])))
    output = None
    for shift_x in range(taps_x):
        partial_sum = jnp.dot(
            columns[shift_x : shift_x + rows_x].reshape(rows_x * rows_y, -1),
            banded[shift_x],
            preferred_element_type=jnp.float32,
        )
        output = partial_sum if output is None else output + partial_sum
    return output.reshape(rows_x, rows_y, -1)


def local(estimate, images, point_spread, covered):
    slab_x, width_y, depth = estimate.shape
    share_w = images.shape[2]
    view_count, taps_x, taps_y, taps_z = point_spread.shape
    rim_x, rim_y, rim_z = ((taps_x - 1) // 2, (taps_y - 1) // 2, (taps_z - 1) // 2)
    shares = width_y // share_w
    share_blocks = share_w // BY
    group = lax.axis_index("view")
    view_id = group // shares
    part = group % shares
    y_start = part * share_w
    source = estimate.astype(jnp.bfloat16)
    rimmed = with_halo(source, (("blk", 0),), rim_x)
    padded = jnp.pad(rimmed, ((0, 0), (rim_y, rim_y), (rim_z, rim_z)))
    spread = lax.dynamic_index_in_dim(point_spread, view_id, 0, keepdims=False)
    kernel = (spread / jnp.sum(spread)).astype(jnp.bfloat16)
    forward = band_table(kernel, depth)
    backward = band_table(kernel[::-1, ::-1, ::-1], depth)
    coverage_row = lax.dynamic_index_in_dim(covered[:, 0, :], view_id, 0, keepdims=False) > 0
    share_cover = lax.dynamic_slice_in_dim(coverage_row, part * share_blocks, share_blocks)
    cell_cover = jnp.repeat(share_cover, BY)[None, :, None]
    image = images[0]
    region = lax.dynamic_slice(
        padded, (0, y_start, 0), (slab_x + 2 * rim_x, share_w + 2 * rim_y, depth + 2 * rim_z)
    )
    blurred = convolve(region, forward, slab_x, share_w)
    quotient = jnp.where(cell_cover, image.astype(jnp.float32) / blurred, 0.0).astype(jnp.bfloat16)
    rim_zeros = jnp.zeros((slab_x, rim_y, depth), jnp.bfloat16)
    edge_rows = jnp.where(part == 0, quotient[:, share_w - rim_y :, :], quotient[:, :rim_y, :])
    partner = swapped(edge_rows, "view", 0)
    lower_rim = jnp.where(part > 0, partner, rim_zeros)
    upper_rim = jnp.where(part < shares - 1, partner, rim_zeros)
    extended = jnp.concatenate([lower_rim, quotient, upper_rim], axis=1)
    quotient_rimmed = with_halo(extended, (("blk", 0),), rim_x)
    padded_quotient = jnp.pad(quotient_rimmed, ((0, 0), (0, 0), (rim_z, rim_z)))
    correction = convolve(padded_quotient, backward, slab_x, share_w)
    share_factor = jnp.where(cell_cover, correction, 1.0)
    n_view = lax.axis_size("view")
    step_x = slab_x // n_view
    rows = share_factor.reshape(n_view, step_x, share_w, depth)
    got = lax.all_to_all(rows, "view", 0, 0)
    got = got.reshape(n_view // shares, shares, step_x, share_w, depth)
    product_rows = jnp.prod(got, axis=0)
    product_rows = jnp.transpose(product_rows, (1, 0, 2, 3)).reshape(step_x, width_y, depth)
    mine = lax.dynamic_slice_in_dim(estimate, group * step_x, step_x, axis=0)
    return lax.all_gather(mine * product_rows, "view", axis=0, tiled=True)


def solution(mesh):
    in_specs = (P("blk", None, None), P("view", "blk", None, None), P(), P(None, "blk", None))
    out_specs = P("blk", None, None)
    return jax.shard_map(local, mesh=mesh, in_specs=in_specs, out_specs=out_specs, check_vma=False)
```

```python
import jax
import jax.numpy as jnp
from jax import lax
from jax.sharding import PartitionSpec as P

BY = 32


def with_halo(cells, sides, width):
    for axis, dim in sides:
        count = lax.axis_size(axis)
        ends = count - 1
        head = lax.slice_in_dim(cells, 0, width, axis=dim)
        tail = lax.slice_in_dim(cells, cells.shape[dim] - width, cells.shape[dim], axis=dim)
        cells = jnp.concatenate(
            [
                lax.ppermute(tail, axis, [(i, (i + 1) % count) for i in range(ends)]),
                cells,
                lax.ppermute(head, axis, [((i + 1) % count, i) for i in range(ends)]),
            ],
            axis=dim,
        )
    return cells


def swapped(block, axis, stride):
    count = lax.axis_size(axis)
    route = []
    for low in range(count):
        high = low | 1 << stride
        if high != low and high < count:
            route += [(low, high), (high, low)]
    return lax.ppermute(block, axis, route)


def merged(part, axis, combine):
    gathered = lax.all_gather(part, axis)

    def take(source):
        return lax.dynamic_index_in_dim(gathered, source, 0, False)

    return lax.fori_loop(
        1, lax.axis_size(axis), lambda source, state: combine(state, take(source)), take(0)
    )


def band_table(kernel, depth):
    taps_x, taps_y, taps_z = kernel.shape
    rim_z = (taps_z - 1) // 2
    shape_three = (taps_z, depth, depth)
    offset = lax.broadcasted_iota(jnp.int32, shape_three, 1) - lax.broadcasted_iota(
        jnp.int32, shape_three, 2
    )
    onehot = (offset + rim_z == lax.broadcasted_iota(jnp.int32, shape_three, 0)).astype(
        jnp.bfloat16
    )
    banded = jnp.einsum("abt,tpz->abpz", kernel, onehot, preferred_element_type=jnp.float32).astype(
        jnp.bfloat16
    )
    return banded.reshape(taps_x, taps_y * depth, depth)


def convolve(padded_part, banded, rows_x, rows_y):
    taps_x = padded_part.shape[0] - rows_x + 1
    taps_y = padded_part.shape[1] - rows_y + 1
    columns = jnp.concatenate(
        [padded_part[:, step_y : step_y + rows_y, :] for step_y in range(taps_y)], axis=2
    )
    output = None
    for shift_x in range(taps_x):
        partial_sum = jnp.dot(
            columns[shift_x : shift_x + rows_x].reshape(rows_x * rows_y, -1),
            banded[shift_x],
            preferred_element_type=jnp.float32,
        )
        output = partial_sum if output is None else output + partial_sum
    return output.reshape(rows_x, rows_y, -1)


def local(estimate, images, point_spread, covered):
    slab_x, width_y, depth = estimate.shape
    share_w = images.shape[2]
    view_count, taps_x, taps_y, taps_z = point_spread.shape
    rim_x, rim_y, rim_z = ((taps_x - 1) // 2, (taps_y - 1) // 2, (taps_z - 1) // 2)
    shares = width_y // share_w
    share_blocks = share_w // BY
    group = lax.axis_index("view")
    view_id = group // shares
    part = group % shares
    y_start = part * share_w
    source = estimate.astype(jnp.bfloat16)
    rimmed = with_halo(source, (("blk", 0),), rim_x)
    padded = jnp.pad(rimmed, ((0, 0), (rim_y, rim_y), (0, 0)))
    spread = lax.dynamic_index_in_dim(point_spread, view_id, 0, keepdims=False)
    kernel = (spread / jnp.sum(spread)).astype(jnp.bfloat16)
    forward = band_table(kernel, depth)
    backward = band_table(kernel[::-1, ::-1, ::-1], depth)
    coverage_row = lax.dynamic_index_in_dim(covered[:, 0, :], view_id, 0, keepdims=False) > 0
    share_cover = lax.dynamic_slice_in_dim(coverage_row, part * share_blocks, share_blocks)
    cell_cover = jnp.repeat(share_cover, BY)[None, :, None]
    image = images[0]
    region = lax.dynamic_slice(
        padded, (0, y_start, 0), (slab_x + 2 * rim_x, share_w + 2 * rim_y, depth)
    )
    blurred = convolve(region, forward, slab_x, share_w)
    quotient = jnp.where(cell_cover, image.astype(jnp.float32) / blurred, 0.0).astype(jnp.bfloat16)
    rim_zeros = jnp.zeros((slab_x, rim_y, depth), jnp.bfloat16)
    edge_rows = jnp.where(part == 0, quotient[:, share_w - rim_y :, :], quotient[:, :rim_y, :])
    partner = swapped(edge_rows, "view", 0)
    lower_rim = jnp.where(part > 0, partner, rim_zeros)
    upper_rim = jnp.where(part < shares - 1, partner, rim_zeros)
    extended = jnp.concatenate([lower_rim, quotient, upper_rim], axis=1)
    quotient_rimmed = with_halo(extended, (("blk", 0),), rim_x)
    correction = convolve(quotient_rimmed, backward, slab_x, share_w)
    share_factor = jnp.where(cell_cover, correction, 1.0)
    n_view = lax.axis_size("view")
    step_x = slab_x // n_view
    rows = share_factor.reshape(n_view, step_x, share_w, depth)
    got = lax.all_to_all(rows, "view", 0, 0)
    got = got.reshape(n_view // shares, shares, step_x, share_w, depth)
    product_rows = jnp.prod(got, axis=0)
    product_rows = jnp.transpose(product_rows, (1, 0, 2, 3)).reshape(step_x, width_y, depth)
    mine = lax.dynamic_slice_in_dim(estimate, group * step_x, step_x, axis=0)
    return lax.all_gather(mine * product_rows, "view", axis=0, tiled=True)


def solution(mesh):
    in_specs = (P("blk", None, None), P("view", "blk", None, None), P(), P(None, "blk", None))
    out_specs = P("blk", None, None)
    return jax.shard_map(local, mesh=mesh, in_specs=in_specs, out_specs=out_specs, check_vma=False)
```

```python
import functools

import jax
import jax.numpy as jnp
from jax import lax
from jax.experimental import pallas as pl
from jax.experimental.pallas import tpu as pltpu
from jax.sharding import PartitionSpec as P

BY = 32


def with_halo(cells, sides, width):
    for axis, dim in sides:
        count = lax.axis_size(axis)
        ends = count - 1
        head = lax.slice_in_dim(cells, 0, width, axis=dim)
        tail = lax.slice_in_dim(cells, cells.shape[dim] - width, cells.shape[dim], axis=dim)
        cells = jnp.concatenate(
            [
                lax.ppermute(tail, axis, [(i, (i + 1) % count) for i in range(ends)]),
                cells,
                lax.ppermute(head, axis, [((i + 1) % count, i) for i in range(ends)]),
            ],
            axis=dim,
        )
    return cells


def swapped(block, axis, stride):
    count = lax.axis_size(axis)
    route = []
    for low in range(count):
        high = low | 1 << stride
        if high != low and high < count:
            route += [(low, high), (high, low)]
    return lax.ppermute(block, axis, route)


def merged(part, axis, combine):
    gathered = lax.all_gather(part, axis)

    def take(source):
        return lax.dynamic_index_in_dim(gathered, source, 0, False)

    return lax.fori_loop(
        1, lax.axis_size(axis), lambda source, state: combine(state, take(source)), take(0)
    )


def product_kernel(n, shares, factor_ref, est_ref, out_ref, held, send1, recv1, send2, recv2):
    groups = n // shares
    step, share_w, depth = held.shape[1:]
    me = lax.axis_index("view")
    view_id = me // shares
    part = me % shares
    mesh_kind = pl.DeviceIdType.MESH
    outgoing = []
    for d in range(1, groups):
        target = (view_id + d) % groups
        copy = pltpu.make_async_remote_copy(
            src_ref=factor_ref.at[pl.ds(target * step, step)],
            dst_ref=held.at[view_id],
            send_sem=send1.at[d],
            recv_sem=recv1.at[d],
            device_id={"view": target * shares + part},
            device_id_type=mesh_kind,
        )
        copy.start()
        outgoing.append(copy)
    acc = factor_ref[pl.ds(view_id * step, step)]
    for d in range(1, groups):
        source = (view_id - d + groups) % groups
        pltpu.make_async_remote_copy(
            src_ref=factor_ref.at[pl.ds(0, step)],
            dst_ref=held.at[source],
            send_sem=send1.at[d],
            recv_sem=recv1.at[d],
            device_id={"view": source * shares + part},
            device_id_type=mesh_kind,
        ).wait_recv()
        acc = acc * held[source]
    for copy in outgoing:
        copy.wait_send()
    rows = pl.ds(view_id * step, step)
    cols = pl.ds(part * share_w, share_w)
    out_ref[rows, cols, :] = acc * est_ref[rows, cols, :]
    outgoing = []
    for d in range(1, n):
        target = (me + d) % n
        copy = pltpu.make_async_remote_copy(
            src_ref=out_ref.at[rows, cols],
            dst_ref=out_ref.at[rows, cols],
            send_sem=send2.at[d],
            recv_sem=recv2.at[d],
            device_id={"view": target},
            device_id_type=mesh_kind,
        )
        copy.start()
        outgoing.append(copy)
    for d in range(1, n):
        source = (me - d + n) % n
        src_rows = pl.ds((source // shares) * step, step)
        src_cols = pl.ds((source % shares) * share_w, share_w)
        pltpu.make_async_remote_copy(
            src_ref=out_ref.at[src_rows, src_cols],
            dst_ref=out_ref.at[src_rows, src_cols],
            send_sem=send2.at[d],
            recv_sem=recv2.at[d],
            device_id={"view": source},
            device_id_type=mesh_kind,
        ).wait_recv()
    for copy in outgoing:
        copy.wait_send()


def product_gather(share_factor, estimate, shares):
    n = lax.axis_size("view")
    groups = n // shares
    slab_x, share_w, depth = share_factor.shape
    step = slab_x // groups
    vmem = pl.BlockSpec(memory_space=pltpu.VMEM)
    return pl.pallas_call(
        functools.partial(product_kernel, n, shares),
        out_shape=jax.ShapeDtypeStruct(estimate.shape, jnp.float32),
        in_specs=[vmem, vmem],
        out_specs=vmem,
        scratch_shapes=[
            pltpu.VMEM((groups, step, share_w, depth), jnp.float32),
            pltpu.SemaphoreType.DMA((groups,)),
            pltpu.SemaphoreType.DMA((groups,)),
            pltpu.SemaphoreType.DMA((n,)),
            pltpu.SemaphoreType.DMA((n,)),
        ],
        compiler_params=pltpu.CompilerParams(has_side_effects=True),
    )(share_factor, estimate)


def band_table(kernel, depth):
    taps_x, taps_y, taps_z = kernel.shape
    rim_z = (taps_z - 1) // 2
    shape_three = (taps_z, depth, depth)
    offset = lax.broadcasted_iota(jnp.int32, shape_three, 1) - lax.broadcasted_iota(
        jnp.int32, shape_three, 2
    )
    onehot = (offset + rim_z == lax.broadcasted_iota(jnp.int32, shape_three, 0)).astype(
        jnp.bfloat16
    )
    banded = jnp.einsum("abt,tpz->abpz", kernel, onehot, preferred_element_type=jnp.float32).astype(
        jnp.bfloat16
    )
    return banded.reshape(taps_x, taps_y * depth, depth)


def convolve(padded_part, banded, rows_x, rows_y):
    taps_x = padded_part.shape[0] - rows_x + 1
    taps_y = padded_part.shape[1] - rows_y + 1
    columns = jnp.concatenate(
        [padded_part[:, step_y : step_y + rows_y, :] for step_y in range(taps_y)], axis=2
    )
    output = None
    for shift_x in range(taps_x):
        partial_sum = jnp.dot(
            columns[shift_x : shift_x + rows_x].reshape(rows_x * rows_y, -1),
            banded[shift_x],
            preferred_element_type=jnp.float32,
        )
        output = partial_sum if output is None else output + partial_sum
    return output.reshape(rows_x, rows_y, -1)


def local(estimate, images, point_spread, covered):
    slab_x, width_y, depth = estimate.shape
    share_w = images.shape[2]
    view_count, taps_x, taps_y, taps_z = point_spread.shape
    rim_x, rim_y, rim_z = ((taps_x - 1) // 2, (taps_y - 1) // 2, (taps_z - 1) // 2)
    shares = width_y // share_w
    share_blocks = share_w // BY
    group = lax.axis_index("view")
    view_id = group // shares
    part = group % shares
    y_start = part * share_w
    source = estimate.astype(jnp.bfloat16)
    rimmed = with_halo(source, (("blk", 0),), rim_x)
    padded = jnp.pad(rimmed, ((0, 0), (rim_y, rim_y), (0, 0)))
    spread = lax.dynamic_index_in_dim(point_spread, view_id, 0, keepdims=False)
    kernel = (spread / jnp.sum(spread)).astype(jnp.bfloat16)
    forward = band_table(kernel, depth)
    backward = band_table(kernel[::-1, ::-1, ::-1], depth)
    coverage_row = lax.dynamic_index_in_dim(covered[:, 0, :], view_id, 0, keepdims=False) > 0
    share_cover = lax.dynamic_slice_in_dim(coverage_row, part * share_blocks, share_blocks)
    cell_cover = jnp.repeat(share_cover, BY)[None, :, None]
    image = images[0]
    region = lax.dynamic_slice(
        padded, (0, y_start, 0), (slab_x + 2 * rim_x, share_w + 2 * rim_y, depth)
    )
    blurred = convolve(region, forward, slab_x, share_w)
    quotient = jnp.where(cell_cover, image.astype(jnp.float32) / blurred, 0.0).astype(jnp.bfloat16)
    rim_zeros = jnp.zeros((slab_x, rim_y, depth), jnp.bfloat16)
    edge_rows = jnp.where(part == 0, quotient[:, share_w - rim_y :, :], quotient[:, :rim_y, :])
    partner = swapped(edge_rows, "view", 0)
    lower_rim = jnp.where(part > 0, partner, rim_zeros)
    upper_rim = jnp.where(part < shares - 1, partner, rim_zeros)
    extended = jnp.concatenate([lower_rim, quotient, upper_rim], axis=1)
    quotient_rimmed = with_halo(extended, (("blk", 0),), rim_x)
    correction = convolve(quotient_rimmed, backward, slab_x, share_w)
    share_factor = jnp.where(cell_cover, correction, 1.0)
    return product_gather(share_factor, estimate, shares)


def solution(mesh):
    in_specs = (P("blk", None, None), P("view", "blk", None, None), P(), P(None, "blk", None))
    out_specs = P("blk", None, None)
    return jax.shard_map(local, mesh=mesh, in_specs=in_specs, out_specs=out_specs, check_vma=False)
```

```python
import functools

import jax
import jax.numpy as jnp
from jax import lax
from jax.experimental import pallas as pl
from jax.experimental.pallas import tpu as pltpu
from jax.sharding import PartitionSpec as P

BY = 32


def with_halo(cells, sides, width):
    for axis, dim in sides:
        count = lax.axis_size(axis)
        ends = count - 1
        head = lax.slice_in_dim(cells, 0, width, axis=dim)
        tail = lax.slice_in_dim(cells, cells.shape[dim] - width, cells.shape[dim], axis=dim)
        cells = jnp.concatenate(
            [
                lax.ppermute(tail, axis, [(i, (i + 1) % count) for i in range(ends)]),
                cells,
                lax.ppermute(head, axis, [((i + 1) % count, i) for i in range(ends)]),
            ],
            axis=dim,
        )
    return cells


def swapped(block, axis, stride):
    count = lax.axis_size(axis)
    route = []
    for low in range(count):
        high = low | 1 << stride
        if high != low and high < count:
            route += [(low, high), (high, low)]
    return lax.ppermute(block, axis, route)


def merged(part, axis, combine):
    gathered = lax.all_gather(part, axis)

    def take(source):
        return lax.dynamic_index_in_dim(gathered, source, 0, False)

    return lax.fori_loop(
        1, lax.axis_size(axis), lambda source, state: combine(state, take(source)), take(0)
    )


def product_kernel(n, shares, factor_ref, est_ref, out_ref, held, send1, recv1, send2, recv2):
    groups = n // shares
    step, share_w, depth = held.shape[1:]
    me = lax.axis_index("view")
    view_id = me // shares
    part = me % shares
    mesh_kind = pl.DeviceIdType.MESH
    outgoing = []
    for d in range(1, groups):
        target = (view_id + d) % groups
        copy = pltpu.make_async_remote_copy(
            src_ref=factor_ref.at[pl.ds(target * step, step)],
            dst_ref=held.at[view_id],
            send_sem=send1.at[d],
            recv_sem=recv1.at[d],
            device_id={"view": target * shares + part},
            device_id_type=mesh_kind,
        )
        copy.start()
        outgoing.append(copy)
    acc = factor_ref[pl.ds(view_id * step, step)]
    for d in range(1, groups):
        source = (view_id - d + groups) % groups
        pltpu.make_async_remote_copy(
            src_ref=factor_ref.at[pl.ds(0, step)],
            dst_ref=held.at[source],
            send_sem=send1.at[d],
            recv_sem=recv1.at[d],
            device_id={"view": source * shares + part},
            device_id_type=mesh_kind,
        ).wait_recv()
        acc = acc * held[source]
    for copy in outgoing:
        copy.wait_send()
    rows = pl.ds(view_id * step, step)
    cols = pl.ds(part * share_w, share_w)
    out_ref[rows, cols, :] = acc * est_ref[rows, cols, :]
    outgoing = []
    for d in range(1, groups):
        target = (view_id + d) % groups
        copy = pltpu.make_async_remote_copy(
            src_ref=out_ref.at[rows, cols],
            dst_ref=out_ref.at[rows, cols],
            send_sem=send2.at[d],
            recv_sem=recv2.at[d],
            device_id={"view": target * shares + part},
            device_id_type=mesh_kind,
        )
        copy.start()
        outgoing.append(copy)
    for d in range(1, groups):
        source = (view_id - d + groups) % groups
        src_rows = pl.ds(source * step, step)
        pltpu.make_async_remote_copy(
            src_ref=out_ref.at[src_rows, cols],
            dst_ref=out_ref.at[src_rows, cols],
            send_sem=send2.at[d],
            recv_sem=recv2.at[d],
            device_id={"view": source * shares + part},
            device_id_type=mesh_kind,
        ).wait_recv()
    for copy in outgoing:
        copy.wait_send()
    outgoing = []
    for d in range(1, shares):
        other = (part + d) % shares
        copy = pltpu.make_async_remote_copy(
            src_ref=out_ref.at[:, cols],
            dst_ref=out_ref.at[:, cols],
            send_sem=send2.at[groups + d],
            recv_sem=recv2.at[groups + d],
            device_id={"view": view_id * shares + other},
            device_id_type=mesh_kind,
        )
        copy.start()
        outgoing.append(copy)
    for d in range(1, shares):
        other = (part - d + shares) % shares
        other_cols = pl.ds(other * share_w, share_w)
        pltpu.make_async_remote_copy(
            src_ref=out_ref.at[:, other_cols],
            dst_ref=out_ref.at[:, other_cols],
            send_sem=send2.at[groups + d],
            recv_sem=recv2.at[groups + d],
            device_id={"view": view_id * shares + other},
            device_id_type=mesh_kind,
        ).wait_recv()
    for copy in outgoing:
        copy.wait_send()


def product_gather(share_factor, estimate, shares):
    n = lax.axis_size("view")
    groups = n // shares
    slab_x, share_w, depth = share_factor.shape
    step = slab_x // groups
    vmem = pl.BlockSpec(memory_space=pltpu.VMEM)
    return pl.pallas_call(
        functools.partial(product_kernel, n, shares),
        out_shape=jax.ShapeDtypeStruct(estimate.shape, jnp.float32),
        in_specs=[vmem, vmem],
        out_specs=vmem,
        scratch_shapes=[
            pltpu.VMEM((groups, step, share_w, depth), jnp.float32),
            pltpu.SemaphoreType.DMA((groups,)),
            pltpu.SemaphoreType.DMA((groups,)),
            pltpu.SemaphoreType.DMA((groups + shares,)),
            pltpu.SemaphoreType.DMA((groups + shares,)),
        ],
        compiler_params=pltpu.CompilerParams(has_side_effects=True),
    )(share_factor, estimate)


def band_table(kernel, depth):
    taps_x, taps_y, taps_z = kernel.shape
    rim_z = (taps_z - 1) // 2
    shape_three = (taps_z, depth, depth)
    offset = lax.broadcasted_iota(jnp.int32, shape_three, 1) - lax.broadcasted_iota(
        jnp.int32, shape_three, 2
    )
    onehot = (offset + rim_z == lax.broadcasted_iota(jnp.int32, shape_three, 0)).astype(
        jnp.bfloat16
    )
    banded = jnp.einsum("abt,tpz->abpz", kernel, onehot, preferred_element_type=jnp.float32).astype(
        jnp.bfloat16
    )
    return banded.reshape(taps_x, taps_y * depth, depth)


def convolve(padded_part, banded, rows_x, rows_y):
    taps_x = padded_part.shape[0] - rows_x + 1
    taps_y = padded_part.shape[1] - rows_y + 1
    columns = jnp.concatenate(
        [padded_part[:, step_y : step_y + rows_y, :] for step_y in range(taps_y)], axis=2
    )
    output = None
    for shift_x in range(taps_x):
        partial_sum = jnp.dot(
            columns[shift_x : shift_x + rows_x].reshape(rows_x * rows_y, -1),
            banded[shift_x],
            preferred_element_type=jnp.float32,
        )
        output = partial_sum if output is None else output + partial_sum
    return output.reshape(rows_x, rows_y, -1)


def local(estimate, images, point_spread, covered):
    slab_x, width_y, depth = estimate.shape
    share_w = images.shape[2]
    view_count, taps_x, taps_y, taps_z = point_spread.shape
    rim_x, rim_y, rim_z = ((taps_x - 1) // 2, (taps_y - 1) // 2, (taps_z - 1) // 2)
    shares = width_y // share_w
    share_blocks = share_w // BY
    group = lax.axis_index("view")
    view_id = group // shares
    part = group % shares
    y_start = part * share_w
    source = estimate.astype(jnp.bfloat16)
    rimmed = with_halo(source, (("blk", 0),), rim_x)
    padded = jnp.pad(rimmed, ((0, 0), (rim_y, rim_y), (0, 0)))
    spread = lax.dynamic_index_in_dim(point_spread, view_id, 0, keepdims=False)
    kernel = (spread / jnp.sum(spread)).astype(jnp.bfloat16)
    forward = band_table(kernel, depth)
    backward = band_table(kernel[::-1, ::-1, ::-1], depth)
    coverage_row = lax.dynamic_index_in_dim(covered[:, 0, :], view_id, 0, keepdims=False) > 0
    share_cover = lax.dynamic_slice_in_dim(coverage_row, part * share_blocks, share_blocks)
    cell_cover = jnp.repeat(share_cover, BY)[None, :, None]
    image = images[0]
    region = lax.dynamic_slice(
        padded, (0, y_start, 0), (slab_x + 2 * rim_x, share_w + 2 * rim_y, depth)
    )
    blurred = convolve(region, forward, slab_x, share_w)
    quotient = jnp.where(cell_cover, image.astype(jnp.float32) / blurred, 0.0).astype(jnp.bfloat16)
    rim_zeros = jnp.zeros((slab_x, rim_y, depth), jnp.bfloat16)
    edge_rows = jnp.where(part == 0, quotient[:, share_w - rim_y :, :], quotient[:, :rim_y, :])
    partner = swapped(edge_rows, "view", 0)
    lower_rim = jnp.where(part > 0, partner, rim_zeros)
    upper_rim = jnp.where(part < shares - 1, partner, rim_zeros)
    extended = jnp.concatenate([lower_rim, quotient, upper_rim], axis=1)
    quotient_rimmed = with_halo(extended, (("blk", 0),), rim_x)
    correction = convolve(quotient_rimmed, backward, slab_x, share_w)
    share_factor = jnp.where(cell_cover, correction, 1.0)
    return product_gather(share_factor, estimate, shares)


def solution(mesh):
    in_specs = (P("blk", None, None), P("view", "blk", None, None), P(), P(None, "blk", None))
    out_specs = P("blk", None, None)
    return jax.shard_map(local, mesh=mesh, in_specs=in_specs, out_specs=out_specs, check_vma=False)
```

```python
import functools

import jax
import jax.numpy as jnp
from jax import lax
from jax.experimental import pallas as pl
from jax.experimental.pallas import tpu as pltpu
from jax.sharding import PartitionSpec as P

BY = 32


def with_halo(cells, sides, width):
    for axis, dim in sides:
        count = lax.axis_size(axis)
        ends = count - 1
        head = lax.slice_in_dim(cells, 0, width, axis=dim)
        tail = lax.slice_in_dim(cells, cells.shape[dim] - width, cells.shape[dim], axis=dim)
        cells = jnp.concatenate(
            [
                lax.ppermute(tail, axis, [(i, (i + 1) % count) for i in range(ends)]),
                cells,
                lax.ppermute(head, axis, [((i + 1) % count, i) for i in range(ends)]),
            ],
            axis=dim,
        )
    return cells


def swapped(block, axis, stride):
    count = lax.axis_size(axis)
    route = []
    for low in range(count):
        high = low | 1 << stride
        if high != low and high < count:
            route += [(low, high), (high, low)]
    return lax.ppermute(block, axis, route)


def merged(part, axis, combine):
    gathered = lax.all_gather(part, axis)

    def take(source):
        return lax.dynamic_index_in_dim(gathered, source, 0, False)

    return lax.fori_loop(
        1, lax.axis_size(axis), lambda source, state: combine(state, take(source)), take(0)
    )


def product_kernel(n, shares, factor_ref, est_ref, out_ref, held, send1, recv1, send2, recv2):
    groups = n // shares
    step, share_w, depth = held.shape[1:]
    me = lax.axis_index("view")
    view_id = me // shares
    part = me % shares
    mesh_kind = pl.DeviceIdType.MESH
    barrier = pltpu.get_barrier_semaphore()
    for d in range(1, groups):
        pl.semaphore_signal(
            barrier, inc=1, device_id={"view": ((view_id + d) % groups) * shares + part},
            device_id_type=mesh_kind,
        )
    for d in range(1, shares):
        pl.semaphore_signal(
            barrier, inc=1, device_id={"view": view_id * shares + (part + d) % shares},
            device_id_type=mesh_kind,
        )
    pl.semaphore_wait(barrier, groups + shares - 2)
    outgoing = []
    for d in range(1, groups):
        target = (view_id + d) % groups
        copy = pltpu.make_async_remote_copy(
            src_ref=factor_ref.at[pl.ds(target * step, step)],
            dst_ref=held.at[view_id],
            send_sem=send1.at[d],
            recv_sem=recv1.at[d],
            device_id={"view": target * shares + part},
            device_id_type=mesh_kind,
        )
        copy.start()
        outgoing.append(copy)
    acc = factor_ref[pl.ds(view_id * step, step)]
    for d in range(1, groups):
        source = (view_id - d + groups) % groups
        pltpu.make_async_remote_copy(
            src_ref=factor_ref.at[pl.ds(0, step)],
            dst_ref=held.at[source],
            send_sem=send1.at[d],
            recv_sem=recv1.at[d],
            device_id={"view": source * shares + part},
            device_id_type=mesh_kind,
        ).wait_recv()
        acc = acc * held[source]
    for copy in outgoing:
        copy.wait_send()
    rows = pl.ds(view_id * step, step)
    cols = pl.ds(part * share_w, share_w)
    out_ref[rows, cols, :] = acc * est_ref[rows, cols, :]
    outgoing = []
    for d in range(1, groups):
        target = (view_id + d) % groups
        copy = pltpu.make_async_remote_copy(
            src_ref=out_ref.at[rows, cols],
            dst_ref=out_ref.at[rows, cols],
            send_sem=send2.at[d],
            recv_sem=recv2.at[d],
            device_id={"view": target * shares + part},
            device_id_type=mesh_kind,
        )
        copy.start()
        outgoing.append(copy)
    for d in range(1, groups):
        source = (view_id - d + groups) % groups
        src_rows = pl.ds(source * step, step)
        pltpu.make_async_remote_copy(
            src_ref=out_ref.at[src_rows, cols],
            dst_ref=out_ref.at[src_rows, cols],
            send_sem=send2.at[d],
            recv_sem=recv2.at[d],
            device_id={"view": source * shares + part},
            device_id_type=mesh_kind,
        ).wait_recv()
    for copy in outgoing:
        copy.wait_send()
    outgoing = []
    for d in range(1, shares):
        other = (part + d) % shares
        copy = pltpu.make_async_remote_copy(
            src_ref=out_ref.at[:, cols],
            dst_ref=out_ref.at[:, cols],
            send_sem=send2.at[groups + d],
            recv_sem=recv2.at[groups + d],
            device_id={"view": view_id * shares + other},
            device_id_type=mesh_kind,
        )
        copy.start()
        outgoing.append(copy)
    for d in range(1, shares):
        other = (part - d + shares) % shares
        other_cols = pl.ds(other * share_w, share_w)
        pltpu.make_async_remote_copy(
            src_ref=out_ref.at[:, other_cols],
            dst_ref=out_ref.at[:, other_cols],
            send_sem=send2.at[groups + d],
            recv_sem=recv2.at[groups + d],
            device_id={"view": view_id * shares + other},
            device_id_type=mesh_kind,
        ).wait_recv()
    for copy in outgoing:
        copy.wait_send()


def product_gather(share_factor, estimate, shares):
    n = lax.axis_size("view")
    groups = n // shares
    slab_x, share_w, depth = share_factor.shape
    step = slab_x // groups
    vmem = pl.BlockSpec(memory_space=pltpu.VMEM)
    return pl.pallas_call(
        functools.partial(product_kernel, n, shares),
        out_shape=jax.ShapeDtypeStruct(estimate.shape, jnp.float32),
        in_specs=[vmem, vmem],
        out_specs=vmem,
        scratch_shapes=[
            pltpu.VMEM((groups, step, share_w, depth), jnp.float32),
            pltpu.SemaphoreType.DMA((groups,)),
            pltpu.SemaphoreType.DMA((groups,)),
            pltpu.SemaphoreType.DMA((groups + shares,)),
            pltpu.SemaphoreType.DMA((groups + shares,)),
        ],
        compiler_params=pltpu.CompilerParams(collective_id=0, has_side_effects=True),
    )(share_factor, estimate)


def band_table(kernel, depth):
    taps_x, taps_y, taps_z = kernel.shape
    rim_z = (taps_z - 1) // 2
    shape_three = (taps_z, depth, depth)
    offset = lax.broadcasted_iota(jnp.int32, shape_three, 1) - lax.broadcasted_iota(
        jnp.int32, shape_three, 2
    )
    onehot = (offset + rim_z == lax.broadcasted_iota(jnp.int32, shape_three, 0)).astype(
        jnp.bfloat16
    )
    banded = jnp.einsum("abt,tpz->abpz", kernel, onehot, preferred_element_type=jnp.float32).astype(
        jnp.bfloat16
    )
    return banded.reshape(taps_x, taps_y * depth, depth)


def convolve(padded_part, banded, rows_x, rows_y):
    taps_x = padded_part.shape[0] - rows_x + 1
    taps_y = padded_part.shape[1] - rows_y + 1
    columns = jnp.concatenate(
        [padded_part[:, step_y : step_y + rows_y, :] for step_y in range(taps_y)], axis=2
    )
    output = None
    for shift_x in range(taps_x):
        partial_sum = jnp.dot(
            columns[shift_x : shift_x + rows_x].reshape(rows_x * rows_y, -1),
            banded[shift_x],
            preferred_element_type=jnp.float32,
        )
        output = partial_sum if output is None else output + partial_sum
    return output.reshape(rows_x, rows_y, -1)


def local(estimate, images, point_spread, covered):
    slab_x, width_y, depth = estimate.shape
    share_w = images.shape[2]
    view_count, taps_x, taps_y, taps_z = point_spread.shape
    rim_x, rim_y, rim_z = ((taps_x - 1) // 2, (taps_y - 1) // 2, (taps_z - 1) // 2)
    shares = width_y // share_w
    share_blocks = share_w // BY
    group = lax.axis_index("view")
    view_id = group // shares
    part = group % shares
    y_start = part * share_w
    source = estimate.astype(jnp.bfloat16)
    rimmed = with_halo(source, (("blk", 0),), rim_x)
    padded = jnp.pad(rimmed, ((0, 0), (rim_y, rim_y), (0, 0)))
    spread = lax.dynamic_index_in_dim(point_spread, view_id, 0, keepdims=False)
    kernel = (spread / jnp.sum(spread)).astype(jnp.bfloat16)
    forward = band_table(kernel, depth)
    backward = band_table(kernel[::-1, ::-1, ::-1], depth)
    coverage_row = lax.dynamic_index_in_dim(covered[:, 0, :], view_id, 0, keepdims=False) > 0
    share_cover = lax.dynamic_slice_in_dim(coverage_row, part * share_blocks, share_blocks)
    cell_cover = jnp.repeat(share_cover, BY)[None, :, None]
    image = images[0]
    region = lax.dynamic_slice(
        padded, (0, y_start, 0), (slab_x + 2 * rim_x, share_w + 2 * rim_y, depth)
    )
    blurred = convolve(region, forward, slab_x, share_w)
    quotient = jnp.where(cell_cover, image.astype(jnp.float32) / blurred, 0.0).astype(jnp.bfloat16)
    rim_zeros = jnp.zeros((slab_x, rim_y, depth), jnp.bfloat16)
    edge_rows = jnp.where(part == 0, quotient[:, share_w - rim_y :, :], quotient[:, :rim_y, :])
    partner = swapped(edge_rows, "view", 0)
    lower_rim = jnp.where(part > 0, partner, rim_zeros)
    upper_rim = jnp.where(part < shares - 1, partner, rim_zeros)
    extended = jnp.concatenate([lower_rim, quotient, upper_rim], axis=1)
    quotient_rimmed = with_halo(extended, (("blk", 0),), rim_x)
    correction = convolve(quotient_rimmed, backward, slab_x, share_w)
    share_factor = jnp.where(cell_cover, correction, 1.0)
    return product_gather(share_factor, estimate, shares)


def solution(mesh):
    in_specs = (P("blk", None, None), P("view", "blk", None, None), P(), P(None, "blk", None))
    out_specs = P("blk", None, None)
    return jax.shard_map(local, mesh=mesh, in_specs=in_specs, out_specs=out_specs, check_vma=False)
```

```python
import functools

import jax
import jax.numpy as jnp
from jax import lax
from jax.experimental import pallas as pl
from jax.experimental.pallas import tpu as pltpu
from jax.sharding import PartitionSpec as P

BY = 32


def with_halo(cells, sides, width):
    for axis, dim in sides:
        count = lax.axis_size(axis)
        ends = count - 1
        head = lax.slice_in_dim(cells, 0, width, axis=dim)
        tail = lax.slice_in_dim(cells, cells.shape[dim] - width, cells.shape[dim], axis=dim)
        cells = jnp.concatenate(
            [
                lax.ppermute(tail, axis, [(i, (i + 1) % count) for i in range(ends)]),
                cells,
                lax.ppermute(head, axis, [((i + 1) % count, i) for i in range(ends)]),
            ],
            axis=dim,
        )
    return cells


def swapped(block, axis, stride):
    count = lax.axis_size(axis)
    route = []
    for low in range(count):
        high = low | 1 << stride
        if high != low and high < count:
            route += [(low, high), (high, low)]
    return lax.ppermute(block, axis, route)


def merged(part, axis, combine):
    gathered = lax.all_gather(part, axis)

    def take(source):
        return lax.dynamic_index_in_dim(gathered, source, 0, False)

    return lax.fori_loop(
        1, lax.axis_size(axis), lambda source, state: combine(state, take(source)), take(0)
    )


def product_kernel(n, shares, factor_ref, est_ref, out_ref, held, send1, recv1, send2, recv2):
    groups = n // shares
    step, share_w, depth = held.shape[1:]
    me = lax.axis_index("view")
    view_id = me // shares
    part = me % shares
    mesh_kind = pl.DeviceIdType.MESH
    barrier = pltpu.get_barrier_semaphore()
    for d in range(1, groups):
        pl.semaphore_signal(
            barrier, inc=1, device_id={"view": ((view_id + d) % groups) * shares + part},
            device_id_type=mesh_kind,
        )
    for d in range(1, shares):
        pl.semaphore_signal(
            barrier, inc=1, device_id={"view": view_id * shares + (part + d) % shares},
            device_id_type=mesh_kind,
        )
    pl.semaphore_wait(barrier, groups + shares - 2)
    outgoing = []
    for d in range(1, groups):
        target = (view_id + d) % groups
        copy = pltpu.make_async_remote_copy(
            src_ref=factor_ref.at[pl.ds(target * step, step)],
            dst_ref=held.at[view_id],
            send_sem=send1.at[d],
            recv_sem=recv1.at[d],
            device_id={"view": target * shares + part},
            device_id_type=mesh_kind,
        )
        copy.start()
        outgoing.append(copy)
    acc = factor_ref[pl.ds(view_id * step, step)]
    for d in range(1, groups):
        source = (view_id - d + groups) % groups
        pltpu.make_async_remote_copy(
            src_ref=factor_ref.at[pl.ds(0, step)],
            dst_ref=held.at[source],
            send_sem=send1.at[d],
            recv_sem=recv1.at[d],
            device_id={"view": source * shares + part},
            device_id_type=mesh_kind,
        ).wait_recv()
        acc = acc * held[source]
    for copy in outgoing:
        copy.wait_send()
    rows = pl.ds(view_id * step, step)
    cols = pl.ds(part * share_w, share_w)
    out_ref[rows, cols, :] = acc * est_ref[rows, cols, :]
    outgoing = []
    for d in range(1, groups):
        target = (view_id + d) % groups
        copy = pltpu.make_async_remote_copy(
            src_ref=out_ref.at[rows, cols],
            dst_ref=out_ref.at[rows, cols],
            send_sem=send2.at[d],
            recv_sem=recv2.at[d],
            device_id={"view": target * shares + part},
            device_id_type=mesh_kind,
        )
        copy.start()
        outgoing.append(copy)
    for d in range(1, groups):
        source = (view_id - d + groups) % groups
        src_rows = pl.ds(source * step, step)
        pltpu.make_async_remote_copy(
            src_ref=out_ref.at[src_rows, cols],
            dst_ref=out_ref.at[src_rows, cols],
            send_sem=send2.at[d],
            recv_sem=recv2.at[d],
            device_id={"view": source * shares + part},
            device_id_type=mesh_kind,
        ).wait_recv()
    for copy in outgoing:
        copy.wait_send()
    outgoing = []
    for d in range(1, shares):
        other = (part + d) % shares
        copy = pltpu.make_async_remote_copy(
            src_ref=out_ref.at[:, cols],
            dst_ref=out_ref.at[:, cols],
            send_sem=send2.at[groups + d],
            recv_sem=recv2.at[groups + d],
            device_id={"view": view_id * shares + other},
            device_id_type=mesh_kind,
        )
        copy.start()
        outgoing.append(copy)
    for d in range(1, shares):
        other = (part - d + shares) % shares
        other_cols = pl.ds(other * share_w, share_w)
        pltpu.make_async_remote_copy(
            src_ref=out_ref.at[:, other_cols],
            dst_ref=out_ref.at[:, other_cols],
            send_sem=send2.at[groups + d],
            recv_sem=recv2.at[groups + d],
            device_id={"view": view_id * shares + other},
            device_id_type=mesh_kind,
        ).wait_recv()
    for copy in outgoing:
        copy.wait_send()


def product_gather(share_factor, estimate, shares):
    n = lax.axis_size("view")
    groups = n // shares
    slab_x, share_w, depth = share_factor.shape
    step = slab_x // groups
    vmem = pl.BlockSpec(memory_space=pltpu.VMEM)
    return pl.pallas_call(
        functools.partial(product_kernel, n, shares),
        out_shape=jax.ShapeDtypeStruct(estimate.shape, jnp.float32),
        in_specs=[vmem, vmem],
        out_specs=vmem,
        scratch_shapes=[
            pltpu.VMEM((groups, step, share_w, depth), jnp.float32),
            pltpu.SemaphoreType.DMA((groups,)),
            pltpu.SemaphoreType.DMA((groups,)),
            pltpu.SemaphoreType.DMA((groups + shares,)),
            pltpu.SemaphoreType.DMA((groups + shares,)),
        ],
        compiler_params=pltpu.CompilerParams(collective_id=0, has_side_effects=True),
    )(share_factor, estimate)


def band_table(kernel, depth):
    taps_x, taps_y, taps_z = kernel.shape
    rim_z = (taps_z - 1) // 2
    shape_three = (taps_z, depth, depth)
    offset = lax.broadcasted_iota(jnp.int32, shape_three, 1) - lax.broadcasted_iota(
        jnp.int32, shape_three, 2
    )
    onehot = (offset + rim_z == lax.broadcasted_iota(jnp.int32, shape_three, 0)).astype(
        jnp.bfloat16
    )
    banded = jnp.einsum("abt,tpz->abpz", kernel, onehot, preferred_element_type=jnp.float32).astype(
        jnp.bfloat16
    )
    return banded.reshape(taps_x, taps_y * depth, depth)


def conv_kernel(tile_x, src_ref, band_ref, out_ref, cols_ref):
    rows_x, rows_y, depth = out_ref.shape
    taps_x = src_ref.shape[0] - rows_x + 1
    taps_y = src_ref.shape[1] - rows_y + 1
    for step_y in range(taps_y):
        cols_ref[:, :, step_y * depth : (step_y + 1) * depth] = src_ref[:, step_y : step_y + rows_y, :]
    for start in range(0, rows_x, tile_x):
        acc = None
        for shift_x in range(taps_x):
            lhs = cols_ref[start + shift_x : start + shift_x + tile_x].reshape(tile_x * rows_y, -1)
            part = jnp.dot(lhs, band_ref[shift_x], preferred_element_type=jnp.float32)
            acc = part if acc is None else acc + part
        out_ref[start : start + tile_x] = acc.reshape(tile_x, rows_y, depth)


def convolve(padded_part, banded, rows_x, rows_y):
    depth = padded_part.shape[2]
    vmem = pl.BlockSpec(memory_space=pltpu.VMEM)
    return pl.pallas_call(
        functools.partial(conv_kernel, 4),
        out_shape=jax.ShapeDtypeStruct((rows_x, rows_y, depth), jnp.float32),
        in_specs=[vmem, vmem],
        out_specs=vmem,
        scratch_shapes=[pltpu.VMEM((padded_part.shape[0], rows_y, banded.shape[1]), jnp.bfloat16)],
    )(padded_part, banded)


def local(estimate, images, point_spread, covered):
    slab_x, width_y, depth = estimate.shape
    share_w = images.shape[2]
    view_count, taps_x, taps_y, taps_z = point_spread.shape
    rim_x, rim_y, rim_z = ((taps_x - 1) // 2, (taps_y - 1) // 2, (taps_z - 1) // 2)
    shares = width_y // share_w
    share_blocks = share_w // BY
    group = lax.axis_index("view")
    view_id = group // shares
    part = group % shares
    y_start = part * share_w
    source = estimate.astype(jnp.bfloat16)
    rimmed = with_halo(source, (("blk", 0),), rim_x)
    padded = jnp.pad(rimmed, ((0, 0), (rim_y, rim_y), (0, 0)))
    spread = lax.dynamic_index_in_dim(point_spread, view_id, 0, keepdims=False)
    kernel = (spread / jnp.sum(spread)).astype(jnp.bfloat16)
    forward = band_table(kernel, depth)
    backward = band_table(kernel[::-1, ::-1, ::-1], depth)
    coverage_row = lax.dynamic_index_in_dim(covered[:, 0, :], view_id, 0, keepdims=False) > 0
    share_cover = lax.dynamic_slice_in_dim(coverage_row, part * share_blocks, share_blocks)
    cell_cover = jnp.repeat(share_cover, BY)[None, :, None]
    image = images[0]
    region = lax.dynamic_slice(
        padded, (0, y_start, 0), (slab_x + 2 * rim_x, share_w + 2 * rim_y, depth)
    )
    blurred = convolve(region, forward, slab_x, share_w)
    quotient = jnp.where(cell_cover, image.astype(jnp.float32) / blurred, 0.0).astype(jnp.bfloat16)
    rim_zeros = jnp.zeros((slab_x, rim_y, depth), jnp.bfloat16)
    edge_rows = jnp.where(part == 0, quotient[:, share_w - rim_y :, :], quotient[:, :rim_y, :])
    partner = swapped(edge_rows, "view", 0)
    lower_rim = jnp.where(part > 0, partner, rim_zeros)
    upper_rim = jnp.where(part < shares - 1, partner, rim_zeros)
    extended = jnp.concatenate([lower_rim, quotient, upper_rim], axis=1)
    quotient_rimmed = with_halo(extended, (("blk", 0),), rim_x)
    correction = convolve(quotient_rimmed, backward, slab_x, share_w)
    share_factor = jnp.where(cell_cover, correction, 1.0)
    return product_gather(share_factor, estimate, shares)


def solution(mesh):
    in_specs = (P("blk", None, None), P("view", "blk", None, None), P(), P(None, "blk", None))
    out_specs = P("blk", None, None)
    return jax.shard_map(local, mesh=mesh, in_specs=in_specs, out_specs=out_specs, check_vma=False)
```

```python
import functools

import jax
import jax.numpy as jnp
from jax import lax
from jax.experimental import pallas as pl
from jax.experimental.pallas import tpu as pltpu
from jax.sharding import PartitionSpec as P

BY = 32


def with_halo(cells, sides, width):
    for axis, dim in sides:
        count = lax.axis_size(axis)
        ends = count - 1
        head = lax.slice_in_dim(cells, 0, width, axis=dim)
        tail = lax.slice_in_dim(cells, cells.shape[dim] - width, cells.shape[dim], axis=dim)
        cells = jnp.concatenate(
            [
                lax.ppermute(tail, axis, [(i, (i + 1) % count) for i in range(ends)]),
                cells,
                lax.ppermute(head, axis, [((i + 1) % count, i) for i in range(ends)]),
            ],
            axis=dim,
        )
    return cells


def swapped(block, axis, stride):
    count = lax.axis_size(axis)
    route = []
    for low in range(count):
        high = low | 1 << stride
        if high != low and high < count:
            route += [(low, high), (high, low)]
    return lax.ppermute(block, axis, route)


def merged(part, axis, combine):
    gathered = lax.all_gather(part, axis)

    def take(source):
        return lax.dynamic_index_in_dim(gathered, source, 0, False)

    return lax.fori_loop(
        1, lax.axis_size(axis), lambda source, state: combine(state, take(source)), take(0)
    )


def product_kernel(
    n, shares, quot_ref, band_ref, cover_ref, est_ref, out_ref, cols_ref, factor_ref, held,
    send1, recv1, send2, recv2,
):
    groups = n // shares
    step, share_w, depth = held.shape[1:]
    taps_x = band_ref.shape[0]
    taps_y = quot_ref.shape[1] - share_w + 1
    me = lax.axis_index("view")
    view_id = me // shares
    part = me % shares
    mesh_kind = pl.DeviceIdType.MESH
    barrier = pltpu.get_barrier_semaphore()
    for d in range(1, groups):
        pl.semaphore_signal(
            barrier, inc=1, device_id={"view": ((view_id + d) % groups) * shares + part},
            device_id_type=mesh_kind,
        )
    for d in range(1, shares):
        pl.semaphore_signal(
            barrier, inc=1, device_id={"view": view_id * shares + (part + d) % shares},
            device_id_type=mesh_kind,
        )
    for step_y in range(taps_y):
        cols_ref[:, :, step_y * depth : (step_y + 1) * depth] = quot_ref[:, step_y : step_y + share_w, :]
    keep = cover_ref[...] > 0

    def factor_rows(target):
        acc = None
        for shift_x in range(taps_x):
            lhs = cols_ref[pl.ds(target * step + shift_x, step)].reshape(step * share_w, -1)
            part_sum = jnp.dot(lhs, band_ref[shift_x], preferred_element_type=jnp.float32)
            acc = part_sum if acc is None else acc + part_sum
        acc = acc.reshape(step, share_w, depth)
        factor_ref[pl.ds(target * step, step)] = jnp.where(keep[None], acc, 1.0)

    factor_rows(view_id)
    pl.semaphore_wait(barrier, groups + shares - 2)
    outgoing = []
    for d in range(1, groups):
        target = (view_id + d) % groups
        factor_rows(target)
        copy = pltpu.make_async_remote_copy(
            src_ref=factor_ref.at[pl.ds(target * step, step)],
            dst_ref=held.at[view_id],
            send_sem=send1.at[d],
            recv_sem=recv1.at[d],
            device_id={"view": target * shares + part},
            device_id_type=mesh_kind,
        )
        copy.start()
        outgoing.append(copy)
    acc = factor_ref[pl.ds(view_id * step, step)]
    for d in range(1, groups):
        source = (view_id - d + groups) % groups
        pltpu.make_async_remote_copy(
            src_ref=factor_ref.at[pl.ds(0, step)],
            dst_ref=held.at[source],
            send_sem=send1.at[d],
            recv_sem=recv1.at[d],
            device_id={"view": source * shares + part},
            device_id_type=mesh_kind,
        ).wait_recv()
        acc = acc * held[source]
    for copy in outgoing:
        copy.wait_send()
    rows = pl.ds(view_id * step, step)
    cols = pl.ds(part * share_w, share_w)
    out_ref[rows, cols, :] = acc * est_ref[rows, cols, :]
    outgoing = []
    for d in range(1, groups):
        target = (view_id + d) % groups
        copy = pltpu.make_async_remote_copy(
            src_ref=out_ref.at[rows, cols],
            dst_ref=out_ref.at[rows, cols],
            send_sem=send2.at[d],
            recv_sem=recv2.at[d],
            device_id={"view": target * shares + part},
            device_id_type=mesh_kind,
        )
        copy.start()
        outgoing.append(copy)
    for d in range(1, groups):
        source = (view_id - d + groups) % groups
        src_rows = pl.ds(source * step, step)
        pltpu.make_async_remote_copy(
            src_ref=out_ref.at[src_rows, cols],
            dst_ref=out_ref.at[src_rows, cols],
            send_sem=send2.at[d],
            recv_sem=recv2.at[d],
            device_id={"view": source * shares + part},
            device_id_type=mesh_kind,
        ).wait_recv()
    for copy in outgoing:
        copy.wait_send()
    outgoing = []
    for d in range(1, shares):
        other = (part + d) % shares
        copy = pltpu.make_async_remote_copy(
            src_ref=out_ref.at[:, cols],
            dst_ref=out_ref.at[:, cols],
            send_sem=send2.at[groups + d],
            recv_sem=recv2.at[groups + d],
            device_id={"view": view_id * shares + other},
            device_id_type=mesh_kind,
        )
        copy.start()
        outgoing.append(copy)
    for d in range(1, shares):
        other = (part - d + shares) % shares
        other_cols = pl.ds(other * share_w, share_w)
        pltpu.make_async_remote_copy(
            src_ref=out_ref.at[:, other_cols],
            dst_ref=out_ref.at[:, other_cols],
            send_sem=send2.at[groups + d],
            recv_sem=recv2.at[groups + d],
            device_id={"view": view_id * shares + other},
            device_id_type=mesh_kind,
        ).wait_recv()
    for copy in outgoing:
        copy.wait_send()


def product_gather(quotient_rimmed, banded, cover_plane, estimate, shares):
    n = lax.axis_size("view")
    groups = n // shares
    slab_x, width_y, depth = estimate.shape
    share_w = cover_plane.shape[0]
    step = slab_x // groups
    vmem = pl.BlockSpec(memory_space=pltpu.VMEM)
    return pl.pallas_call(
        functools.partial(product_kernel, n, shares),
        out_shape=jax.ShapeDtypeStruct(estimate.shape, jnp.float32),
        in_specs=[vmem] * 4,
        out_specs=vmem,
        scratch_shapes=[
            pltpu.VMEM((quotient_rimmed.shape[0], share_w, banded.shape[1]), jnp.bfloat16),
            pltpu.VMEM((slab_x, share_w, depth), jnp.float32),
            pltpu.VMEM((groups, step, share_w, depth), jnp.float32),
            pltpu.SemaphoreType.DMA((groups,)),
            pltpu.SemaphoreType.DMA((groups,)),
            pltpu.SemaphoreType.DMA((groups + shares,)),
            pltpu.SemaphoreType.DMA((groups + shares,)),
        ],
        compiler_params=pltpu.CompilerParams(collective_id=0, has_side_effects=True),
    )(quotient_rimmed, banded, cover_plane, estimate)


def band_table(kernel, depth):
    taps_x, taps_y, taps_z = kernel.shape
    rim_z = (taps_z - 1) // 2
    shape_three = (taps_z, depth, depth)
    offset = lax.broadcasted_iota(jnp.int32, shape_three, 1) - lax.broadcasted_iota(
        jnp.int32, shape_three, 2
    )
    onehot = (offset + rim_z == lax.broadcasted_iota(jnp.int32, shape_three, 0)).astype(
        jnp.bfloat16
    )
    banded = jnp.einsum("abt,tpz->abpz", kernel, onehot, preferred_element_type=jnp.float32).astype(
        jnp.bfloat16
    )
    return banded.reshape(taps_x, taps_y * depth, depth)


def conv_kernel(tile_x, src_ref, band_ref, out_ref, cols_ref):
    rows_x, rows_y, depth = out_ref.shape
    taps_x = src_ref.shape[0] - rows_x + 1
    taps_y = src_ref.shape[1] - rows_y + 1
    for step_y in range(taps_y):
        cols_ref[:, :, step_y * depth : (step_y + 1) * depth] = src_ref[:, step_y : step_y + rows_y, :]
    for start in range(0, rows_x, tile_x):
        acc = None
        for shift_x in range(taps_x):
            lhs = cols_ref[start + shift_x : start + shift_x + tile_x].reshape(tile_x * rows_y, -1)
            part = jnp.dot(lhs, band_ref[shift_x], preferred_element_type=jnp.float32)
            acc = part if acc is None else acc + part
        out_ref[start : start + tile_x] = acc.reshape(tile_x, rows_y, depth)


def convolve(padded_part, banded, rows_x, rows_y):
    depth = padded_part.shape[2]
    vmem = pl.BlockSpec(memory_space=pltpu.VMEM)
    return pl.pallas_call(
        functools.partial(conv_kernel, 4),
        out_shape=jax.ShapeDtypeStruct((rows_x, rows_y, depth), jnp.float32),
        in_specs=[vmem, vmem],
        out_specs=vmem,
        scratch_shapes=[pltpu.VMEM((padded_part.shape[0], rows_y, banded.shape[1]), jnp.bfloat16)],
    )(padded_part, banded)


def local(estimate, images, point_spread, covered):
    slab_x, width_y, depth = estimate.shape
    share_w = images.shape[2]
    view_count, taps_x, taps_y, taps_z = point_spread.shape
    rim_x, rim_y, rim_z = ((taps_x - 1) // 2, (taps_y - 1) // 2, (taps_z - 1) // 2)
    shares = width_y // share_w
    share_blocks = share_w // BY
    group = lax.axis_index("view")
    view_id = group // shares
    part = group % shares
    y_start = part * share_w
    source = estimate.astype(jnp.bfloat16)
    rimmed = with_halo(source, (("blk", 0),), rim_x)
    padded = jnp.pad(rimmed, ((0, 0), (rim_y, rim_y), (0, 0)))
    spread = lax.dynamic_index_in_dim(point_spread, view_id, 0, keepdims=False)
    kernel = (spread / jnp.sum(spread)).astype(jnp.bfloat16)
    forward = band_table(kernel, depth)
    backward = band_table(kernel[::-1, ::-1, ::-1], depth)
    coverage_row = lax.dynamic_index_in_dim(covered[:, 0, :], view_id, 0, keepdims=False) > 0
    share_cover = lax.dynamic_slice_in_dim(coverage_row, part * share_blocks, share_blocks)
    cell_cover = jnp.repeat(share_cover, BY)[None, :, None]
    image = images[0]
    region = lax.dynamic_slice(
        padded, (0, y_start, 0), (slab_x + 2 * rim_x, share_w + 2 * rim_y, depth)
    )
    blurred = convolve(region, forward, slab_x, share_w)
    quotient = jnp.where(cell_cover, image.astype(jnp.float32) / blurred, 0.0).astype(jnp.bfloat16)
    rim_zeros = jnp.zeros((slab_x, rim_y, depth), jnp.bfloat16)
    edge_rows = jnp.where(part == 0, quotient[:, share_w - rim_y :, :], quotient[:, :rim_y, :])
    partner = swapped(edge_rows, "view", 0)
    lower_rim = jnp.where(part > 0, partner, rim_zeros)
    upper_rim = jnp.where(part < shares - 1, partner, rim_zeros)
    extended = jnp.concatenate([lower_rim, quotient, upper_rim], axis=1)
    quotient_rimmed = with_halo(extended, (("blk", 0),), rim_x)
    cover_plane = jnp.broadcast_to(cell_cover[0].astype(jnp.float32), (share_w, depth))
    return product_gather(quotient_rimmed, backward, cover_plane, estimate, shares)


def solution(mesh):
    in_specs = (P("blk", None, None), P("view", "blk", None, None), P(), P(None, "blk", None))
    out_specs = P("blk", None, None)
    return jax.shard_map(local, mesh=mesh, in_specs=in_specs, out_specs=out_specs, check_vma=False)
```

```python
import functools

import jax
import jax.numpy as jnp
from jax import lax
from jax.experimental import pallas as pl
from jax.experimental.pallas import tpu as pltpu
from jax.sharding import PartitionSpec as P

BY = 32


def with_halo(cells, sides, width):
    for axis, dim in sides:
        count = lax.axis_size(axis)
        ends = count - 1
        head = lax.slice_in_dim(cells, 0, width, axis=dim)
        tail = lax.slice_in_dim(cells, cells.shape[dim] - width, cells.shape[dim], axis=dim)
        cells = jnp.concatenate(
            [
                lax.ppermute(tail, axis, [(i, (i + 1) % count) for i in range(ends)]),
                cells,
                lax.ppermute(head, axis, [((i + 1) % count, i) for i in range(ends)]),
            ],
            axis=dim,
        )
    return cells


def swapped(block, axis, stride):
    count = lax.axis_size(axis)
    route = []
    for low in range(count):
        high = low | 1 << stride
        if high != low and high < count:
            route += [(low, high), (high, low)]
    return lax.ppermute(block, axis, route)


def merged(part, axis, combine):
    gathered = lax.all_gather(part, axis)

    def take(source):
        return lax.dynamic_index_in_dim(gathered, source, 0, False)

    return lax.fori_loop(
        1, lax.axis_size(axis), lambda source, state: combine(state, take(source)), take(0)
    )


def product_kernel(
    n, shares, quot_ref, band_ref, cover_ref, est_ref, out_ref, cols_ref, factor_ref, held,
    send1, recv1, send2, recv2,
):
    groups = n // shares
    step, share_w, depth = held.shape[1:]
    taps_x = band_ref.shape[0]
    taps_y = quot_ref.shape[1] - share_w + 1
    me = lax.axis_index("view")
    view_id = me // shares
    part = me % shares
    mesh_kind = pl.DeviceIdType.MESH
    barrier = pltpu.get_barrier_semaphore()
    for d in range(1, groups):
        pl.semaphore_signal(
            barrier, inc=1, device_id={"view": ((view_id + d) % groups) * shares + part},
            device_id_type=mesh_kind,
        )
    for d in range(1, shares):
        pl.semaphore_signal(
            barrier, inc=1, device_id={"view": view_id * shares + (part + d) % shares},
            device_id_type=mesh_kind,
        )
    for step_y in range(taps_y):
        cols_ref[:, :, step_y * depth : (step_y + 1) * depth] = quot_ref[:, step_y : step_y + share_w, :]
    keep = cover_ref[...] > 0

    def factor_rows(target):
        acc = None
        for shift_x in range(taps_x):
            lhs = cols_ref[pl.ds(target * step + shift_x, step)].reshape(step * share_w, -1)
            part_sum = jnp.dot(lhs, band_ref[shift_x], preferred_element_type=jnp.float32)
            acc = part_sum if acc is None else acc + part_sum
        acc = acc.reshape(step, share_w, depth)
        factor_ref[pl.ds(target * step, step)] = jnp.where(keep[None], acc, 1.0)

    factor_rows(view_id)
    pl.semaphore_wait(barrier, groups + shares - 2)
    outgoing = []
    for d in range(1, groups):
        target = (view_id + d) % groups
        factor_rows(target)
        copy = pltpu.make_async_remote_copy(
            src_ref=factor_ref.at[pl.ds(target * step, step)],
            dst_ref=held.at[view_id],
            send_sem=send1.at[d],
            recv_sem=recv1.at[d],
            device_id={"view": target * shares + part},
            device_id_type=mesh_kind,
        )
        copy.start()
        outgoing.append(copy)
    acc = factor_ref[pl.ds(view_id * step, step)]
    for d in range(1, groups):
        source = (view_id - d + groups) % groups
        pltpu.make_async_remote_copy(
            src_ref=factor_ref.at[pl.ds(0, step)],
            dst_ref=held.at[source],
            send_sem=send1.at[d],
            recv_sem=recv1.at[d],
            device_id={"view": source * shares + part},
            device_id_type=mesh_kind,
        ).wait_recv()
        acc = acc * held[source]
    for copy in outgoing:
        copy.wait_send()
    rows = pl.ds(view_id * step, step)
    cols = pl.ds(part * share_w, share_w)
    out_ref[rows, cols, :] = acc * est_ref[rows, cols, :]
    outgoing = []
    for d in range(1, groups):
        target = (view_id + d) % groups
        copy = pltpu.make_async_remote_copy(
            src_ref=out_ref.at[rows, cols],
            dst_ref=out_ref.at[rows, cols],
            send_sem=send2.at[d],
            recv_sem=recv2.at[d],
            device_id={"view": target * shares + part},
            device_id_type=mesh_kind,
        )
        copy.start()
        outgoing.append(copy)
    for d in range(1, groups):
        source = (view_id - d + groups) % groups
        src_rows = pl.ds(source * step, step)
        pltpu.make_async_remote_copy(
            src_ref=out_ref.at[src_rows, cols],
            dst_ref=out_ref.at[src_rows, cols],
            send_sem=send2.at[d],
            recv_sem=recv2.at[d],
            device_id={"view": source * shares + part},
            device_id_type=mesh_kind,
        ).wait_recv()
    for copy in outgoing:
        copy.wait_send()
    outgoing = []
    for d in range(1, shares):
        other = (part + d) % shares
        copy = pltpu.make_async_remote_copy(
            src_ref=out_ref.at[:, cols],
            dst_ref=out_ref.at[:, cols],
            send_sem=send2.at[groups + d],
            recv_sem=recv2.at[groups + d],
            device_id={"view": view_id * shares + other},
            device_id_type=mesh_kind,
        )
        copy.start()
        outgoing.append(copy)
    for d in range(1, shares):
        other = (part - d + shares) % shares
        other_cols = pl.ds(other * share_w, share_w)
        pltpu.make_async_remote_copy(
            src_ref=out_ref.at[:, other_cols],
            dst_ref=out_ref.at[:, other_cols],
            send_sem=send2.at[groups + d],
            recv_sem=recv2.at[groups + d],
            device_id={"view": view_id * shares + other},
            device_id_type=mesh_kind,
        ).wait_recv()
    for copy in outgoing:
        copy.wait_send()


def product_gather(quotient_rimmed, banded, cover_plane, estimate, shares):
    n = lax.axis_size("view")
    groups = n // shares
    slab_x, width_y, depth = estimate.shape
    share_w = cover_plane.shape[0]
    step = slab_x // groups
    vmem = pl.BlockSpec(memory_space=pltpu.VMEM)
    return pl.pallas_call(
        functools.partial(product_kernel, n, shares),
        out_shape=jax.ShapeDtypeStruct(estimate.shape, jnp.float32),
        in_specs=[vmem] * 4,
        out_specs=vmem,
        scratch_shapes=[
            pltpu.VMEM((quotient_rimmed.shape[0], share_w, banded.shape[1]), jnp.bfloat16),
            pltpu.VMEM((slab_x, share_w, depth), jnp.float32),
            pltpu.VMEM((groups, step, share_w, depth), jnp.float32),
            pltpu.SemaphoreType.DMA((groups,)),
            pltpu.SemaphoreType.DMA((groups,)),
            pltpu.SemaphoreType.DMA((groups + shares,)),
            pltpu.SemaphoreType.DMA((groups + shares,)),
        ],
        compiler_params=pltpu.CompilerParams(collective_id=0, has_side_effects=True),
    )(quotient_rimmed, banded, cover_plane, estimate)


def halo_kernel(width, cells_ref, out_ref, send_sem, recv_sem):
    n = lax.axis_size("blk")
    me = lax.axis_index("blk")
    rows = cells_ref.shape[0]
    up = (me + 1) % n
    down = (me + n - 1) % n
    mesh_kind = pl.DeviceIdType.MESH
    barrier = pltpu.get_barrier_semaphore()
    for other in (up, down):
        pl.semaphore_signal(barrier, inc=1, device_id={"blk": other}, device_id_type=mesh_kind)
    pl.semaphore_wait(barrier, 2)
    to_up = pltpu.make_async_remote_copy(
        src_ref=cells_ref.at[pl.ds(rows - width, width)],
        dst_ref=out_ref.at[pl.ds(0, width)],
        send_sem=send_sem.at[0],
        recv_sem=recv_sem.at[0],
        device_id={"blk": up},
        device_id_type=mesh_kind,
    )
    to_down = pltpu.make_async_remote_copy(
        src_ref=cells_ref.at[pl.ds(0, width)],
        dst_ref=out_ref.at[pl.ds(rows + width, width)],
        send_sem=send_sem.at[1],
        recv_sem=recv_sem.at[1],
        device_id={"blk": down},
        device_id_type=mesh_kind,
    )
    to_up.start()
    to_down.start()
    out_ref[pl.ds(width, rows)] = cells_ref[...]
    to_up.wait()
    to_down.wait()

    @pl.when(me == 0)
    def _():
        out_ref[pl.ds(0, width)] = jnp.zeros((width,) + cells_ref.shape[1:], cells_ref.dtype)

    @pl.when(me == n - 1)
    def _():
        out_ref[pl.ds(rows + width, width)] = jnp.zeros((width,) + cells_ref.shape[1:], cells_ref.dtype)


def halo_exchange(cells, width, kernel_id):
    vmem = pl.BlockSpec(memory_space=pltpu.VMEM)
    shape = (cells.shape[0] + 2 * width,) + cells.shape[1:]
    return pl.pallas_call(
        functools.partial(halo_kernel, width),
        out_shape=jax.ShapeDtypeStruct(shape, cells.dtype),
        in_specs=[vmem],
        out_specs=vmem,
        scratch_shapes=[pltpu.SemaphoreType.DMA((2,)), pltpu.SemaphoreType.DMA((2,))],
        compiler_params=pltpu.CompilerParams(collective_id=kernel_id, has_side_effects=True),
    )(cells)


def band_table(kernel, depth):
    taps_x, taps_y, taps_z = kernel.shape
    rim_z = (taps_z - 1) // 2
    shape_three = (taps_z, depth, depth)
    offset = lax.broadcasted_iota(jnp.int32, shape_three, 1) - lax.broadcasted_iota(
        jnp.int32, shape_three, 2
    )
    onehot = (offset + rim_z == lax.broadcasted_iota(jnp.int32, shape_three, 0)).astype(
        jnp.bfloat16
    )
    banded = jnp.einsum("abt,tpz->abpz", kernel, onehot, preferred_element_type=jnp.float32).astype(
        jnp.bfloat16
    )
    return banded.reshape(taps_x, taps_y * depth, depth)


def conv_kernel(tile_x, src_ref, band_ref, out_ref, cols_ref):
    rows_x, rows_y, depth = out_ref.shape
    taps_x = src_ref.shape[0] - rows_x + 1
    taps_y = src_ref.shape[1] - rows_y + 1
    for step_y in range(taps_y):
        cols_ref[:, :, step_y * depth : (step_y + 1) * depth] = src_ref[:, step_y : step_y + rows_y, :]
    for start in range(0, rows_x, tile_x):
        acc = None
        for shift_x in range(taps_x):
            lhs = cols_ref[start + shift_x : start + shift_x + tile_x].reshape(tile_x * rows_y, -1)
            part = jnp.dot(lhs, band_ref[shift_x], preferred_element_type=jnp.float32)
            acc = part if acc is None else acc + part
        out_ref[start : start + tile_x] = acc.reshape(tile_x, rows_y, depth)


def convolve(padded_part, banded, rows_x, rows_y):
    depth = padded_part.shape[2]
    vmem = pl.BlockSpec(memory_space=pltpu.VMEM)
    return pl.pallas_call(
        functools.partial(conv_kernel, 4),
        out_shape=jax.ShapeDtypeStruct((rows_x, rows_y, depth), jnp.float32),
        in_specs=[vmem, vmem],
        out_specs=vmem,
        scratch_shapes=[pltpu.VMEM((padded_part.shape[0], rows_y, banded.shape[1]), jnp.bfloat16)],
    )(padded_part, banded)


def local(estimate, images, point_spread, covered):
    slab_x, width_y, depth = estimate.shape
    share_w = images.shape[2]
    view_count, taps_x, taps_y, taps_z = point_spread.shape
    rim_x, rim_y, rim_z = ((taps_x - 1) // 2, (taps_y - 1) // 2, (taps_z - 1) // 2)
    shares = width_y // share_w
    share_blocks = share_w // BY
    group = lax.axis_index("view")
    view_id = group // shares
    part = group % shares
    y_start = part * share_w
    source = estimate.astype(jnp.bfloat16)
    rimmed = halo_exchange(source, rim_x, 1)
    padded = jnp.pad(rimmed, ((0, 0), (rim_y, rim_y), (0, 0)))
    spread = lax.dynamic_index_in_dim(point_spread, view_id, 0, keepdims=False)
    kernel = (spread / jnp.sum(spread)).astype(jnp.bfloat16)
    forward = band_table(kernel, depth)
    backward = band_table(kernel[::-1, ::-1, ::-1], depth)
    coverage_row = lax.dynamic_index_in_dim(covered[:, 0, :], view_id, 0, keepdims=False) > 0
    share_cover = lax.dynamic_slice_in_dim(coverage_row, part * share_blocks, share_blocks)
    cell_cover = jnp.repeat(share_cover, BY)[None, :, None]
    image = images[0]
    region = lax.dynamic_slice(
        padded, (0, y_start, 0), (slab_x + 2 * rim_x, share_w + 2 * rim_y, depth)
    )
    blurred = convolve(region, forward, slab_x, share_w)
    quotient = jnp.where(cell_cover, image.astype(jnp.float32) / blurred, 0.0).astype(jnp.bfloat16)
    rim_zeros = jnp.zeros((slab_x, rim_y, depth), jnp.bfloat16)
    edge_rows = jnp.where(part == 0, quotient[:, share_w - rim_y :, :], quotient[:, :rim_y, :])
    partner = swapped(edge_rows, "view", 0)
    lower_rim = jnp.where(part > 0, partner, rim_zeros)
    upper_rim = jnp.where(part < shares - 1, partner, rim_zeros)
    extended = jnp.concatenate([lower_rim, quotient, upper_rim], axis=1)
    quotient_rimmed = halo_exchange(extended, rim_x, 2)
    cover_plane = jnp.broadcast_to(cell_cover[0].astype(jnp.float32), (share_w, depth))
    return product_gather(quotient_rimmed, backward, cover_plane, estimate, shares)


def solution(mesh):
    in_specs = (P("blk", None, None), P("view", "blk", None, None), P(), P(None, "blk", None))
    out_specs = P("blk", None, None)
    return jax.shard_map(local, mesh=mesh, in_specs=in_specs, out_specs=out_specs, check_vma=False)
```

```python
import functools

import jax
import jax.numpy as jnp
from jax import lax
from jax.experimental import pallas as pl
from jax.experimental.pallas import tpu as pltpu
from jax.sharding import PartitionSpec as P

BY = 32


def with_halo(cells, sides, width):
    for axis, dim in sides:
        count = lax.axis_size(axis)
        ends = count - 1
        head = lax.slice_in_dim(cells, 0, width, axis=dim)
        tail = lax.slice_in_dim(cells, cells.shape[dim] - width, cells.shape[dim], axis=dim)
        cells = jnp.concatenate(
            [
                lax.ppermute(tail, axis, [(i, (i + 1) % count) for i in range(ends)]),
                cells,
                lax.ppermute(head, axis, [((i + 1) % count, i) for i in range(ends)]),
            ],
            axis=dim,
        )
    return cells


def swapped(block, axis, stride):
    count = lax.axis_size(axis)
    route = []
    for low in range(count):
        high = low | 1 << stride
        if high != low and high < count:
            route += [(low, high), (high, low)]
    return lax.ppermute(block, axis, route)


def merged(part, axis, combine):
    gathered = lax.all_gather(part, axis)

    def take(source):
        return lax.dynamic_index_in_dim(gathered, source, 0, False)

    return lax.fori_loop(
        1, lax.axis_size(axis), lambda source, state: combine(state, take(source)), take(0)
    )


def product_kernel(
    n, shares, quot_ref, band_ref, cover_ref, est_ref, out_ref, cols_ref, factor_ref, held,
    send1, recv1, send2, recv2,
):
    groups = n // shares
    step, share_w, depth = held.shape[1:]
    taps_x = band_ref.shape[0]
    taps_y = quot_ref.shape[1] - share_w + 1
    me = lax.axis_index("view")
    view_id = me // shares
    part = me % shares
    mesh_kind = pl.DeviceIdType.MESH
    barrier = pltpu.get_barrier_semaphore()
    for d in range(1, groups):
        pl.semaphore_signal(
            barrier, inc=1, device_id={"view": ((view_id + d) % groups) * shares + part},
            device_id_type=mesh_kind,
        )
    for d in range(1, shares):
        pl.semaphore_signal(
            barrier, inc=1, device_id={"view": view_id * shares + (part + d) % shares},
            device_id_type=mesh_kind,
        )
    for step_y in range(taps_y):
        cols_ref[:, :, step_y * depth : (step_y + 1) * depth] = quot_ref[:, step_y : step_y + share_w, :]
    keep = cover_ref[...] > 0

    def factor_rows(target):
        acc = None
        for shift_x in range(taps_x):
            lhs = cols_ref[pl.ds(target * step + shift_x, step)].reshape(step * share_w, -1)
            part_sum = jnp.dot(lhs, band_ref[shift_x], preferred_element_type=jnp.float32)
            acc = part_sum if acc is None else acc + part_sum
        acc = acc.reshape(step, share_w, depth)
        factor_ref[pl.ds(target * step, step)] = jnp.where(keep[None], acc, 1.0)

    factor_rows(view_id)
    pl.semaphore_wait(barrier, groups + shares - 2)
    outgoing = []
    for d in range(1, groups):
        target = (view_id + d) % groups
        factor_rows(target)
        copy = pltpu.make_async_remote_copy(
            src_ref=factor_ref.at[pl.ds(target * step, step)],
            dst_ref=held.at[view_id],
            send_sem=send1.at[d],
            recv_sem=recv1.at[d],
            device_id={"view": target * shares + part},
            device_id_type=mesh_kind,
        )
        copy.start()
        outgoing.append(copy)
    acc = factor_ref[pl.ds(view_id * step, step)]
    for d in range(1, groups):
        source = (view_id - d + groups) % groups
        pltpu.make_async_remote_copy(
            src_ref=factor_ref.at[pl.ds(0, step)],
            dst_ref=held.at[source],
            send_sem=send1.at[d],
            recv_sem=recv1.at[d],
            device_id={"view": source * shares + part},
            device_id_type=mesh_kind,
        ).wait_recv()
        acc = acc * held[source]
    for copy in outgoing:
        copy.wait_send()
    rows = pl.ds(view_id * step, step)
    cols = pl.ds(part * share_w, share_w)
    out_ref[rows, cols, :] = acc * est_ref[rows, cols, :]
    outgoing = []
    for d in range(1, groups):
        target = (view_id + d) % groups
        copy = pltpu.make_async_remote_copy(
            src_ref=out_ref.at[rows, cols],
            dst_ref=out_ref.at[rows, cols],
            send_sem=send2.at[d],
            recv_sem=recv2.at[d],
            device_id={"view": target * shares + part},
            device_id_type=mesh_kind,
        )
        copy.start()
        outgoing.append(copy)
    for d in range(1, groups):
        source = (view_id - d + groups) % groups
        src_rows = pl.ds(source * step, step)
        pltpu.make_async_remote_copy(
            src_ref=out_ref.at[src_rows, cols],
            dst_ref=out_ref.at[src_rows, cols],
            send_sem=send2.at[d],
            recv_sem=recv2.at[d],
            device_id={"view": source * shares + part},
            device_id_type=mesh_kind,
        ).wait_recv()
    for copy in outgoing:
        copy.wait_send()
    outgoing = []
    for d in range(1, shares):
        other = (part + d) % shares
        copy = pltpu.make_async_remote_copy(
            src_ref=out_ref.at[:, cols],
            dst_ref=out_ref.at[:, cols],
            send_sem=send2.at[groups + d],
            recv_sem=recv2.at[groups + d],
            device_id={"view": view_id * shares + other},
            device_id_type=mesh_kind,
        )
        copy.start()
        outgoing.append(copy)
    for d in range(1, shares):
        other = (part - d + shares) % shares
        other_cols = pl.ds(other * share_w, share_w)
        pltpu.make_async_remote_copy(
            src_ref=out_ref.at[:, other_cols],
            dst_ref=out_ref.at[:, other_cols],
            send_sem=send2.at[groups + d],
            recv_sem=recv2.at[groups + d],
            device_id={"view": view_id * shares + other},
            device_id_type=mesh_kind,
        ).wait_recv()
    for copy in outgoing:
        copy.wait_send()


def product_gather(quotient_rimmed, banded, cover_plane, estimate, shares):
    n = lax.axis_size("view")
    groups = n // shares
    slab_x, width_y, depth = estimate.shape
    share_w = cover_plane.shape[0]
    step = slab_x // groups
    vmem = pl.BlockSpec(memory_space=pltpu.VMEM)
    return pl.pallas_call(
        functools.partial(product_kernel, n, shares),
        out_shape=jax.ShapeDtypeStruct(estimate.shape, jnp.float32),
        in_specs=[vmem] * 4,
        out_specs=vmem,
        scratch_shapes=[
            pltpu.VMEM((quotient_rimmed.shape[0], share_w, banded.shape[1]), jnp.bfloat16),
            pltpu.VMEM((slab_x, share_w, depth), jnp.float32),
            pltpu.VMEM((groups, step, share_w, depth), jnp.float32),
            pltpu.SemaphoreType.DMA((groups,)),
            pltpu.SemaphoreType.DMA((groups,)),
            pltpu.SemaphoreType.DMA((groups + shares,)),
            pltpu.SemaphoreType.DMA((groups + shares,)),
        ],
        compiler_params=pltpu.CompilerParams(collective_id=0, has_side_effects=True),
    )(quotient_rimmed, banded, cover_plane, estimate)


def band_tables(kernels, depth):
    count, taps_x, taps_y, taps_z = kernels.shape
    rim_z = (taps_z - 1) // 2
    shape_three = (taps_z, depth, depth)
    offset = lax.broadcasted_iota(jnp.int32, shape_three, 1) - lax.broadcasted_iota(
        jnp.int32, shape_three, 2
    )
    onehot = (offset + rim_z == lax.broadcasted_iota(jnp.int32, shape_three, 0)).astype(
        jnp.bfloat16
    )
    banded = jnp.dot(
        kernels.reshape(count * taps_x * taps_y, taps_z),
        onehot.reshape(taps_z, depth * depth),
        preferred_element_type=jnp.float32,
    ).astype(jnp.bfloat16)
    return banded.reshape(count, taps_x, taps_y * depth, depth)


def conv_kernel(tile_x, src_ref, band_ref, out_ref, cols_ref):
    rows_x, rows_y, depth = out_ref.shape
    taps_x = src_ref.shape[0] - rows_x + 1
    taps_y = src_ref.shape[1] - rows_y + 1
    for step_y in range(taps_y):
        cols_ref[:, :, step_y * depth : (step_y + 1) * depth] = src_ref[:, step_y : step_y + rows_y, :]
    for start in range(0, rows_x, tile_x):
        acc = None
        for shift_x in range(taps_x):
            lhs = cols_ref[start + shift_x : start + shift_x + tile_x].reshape(tile_x * rows_y, -1)
            part = jnp.dot(lhs, band_ref[shift_x], preferred_element_type=jnp.float32)
            acc = part if acc is None else acc + part
        out_ref[start : start + tile_x] = acc.reshape(tile_x, rows_y, depth)


def convolve(padded_part, banded, rows_x, rows_y):
    depth = padded_part.shape[2]
    vmem = pl.BlockSpec(memory_space=pltpu.VMEM)
    return pl.pallas_call(
        functools.partial(conv_kernel, 4),
        out_shape=jax.ShapeDtypeStruct((rows_x, rows_y, depth), jnp.float32),
        in_specs=[vmem, vmem],
        out_specs=vmem,
        scratch_shapes=[pltpu.VMEM((padded_part.shape[0], rows_y, banded.shape[1]), jnp.bfloat16)],
    )(padded_part, banded)


def local(estimate, images, point_spread, covered):
    slab_x, width_y, depth = estimate.shape
    share_w = images.shape[2]
    view_count, taps_x, taps_y, taps_z = point_spread.shape
    rim_x, rim_y, rim_z = ((taps_x - 1) // 2, (taps_y - 1) // 2, (taps_z - 1) // 2)
    shares = width_y // share_w
    share_blocks = share_w // BY
    group = lax.axis_index("view")
    view_id = group // shares
    part = group % shares
    y_start = part * share_w
    source = estimate.astype(jnp.bfloat16)
    rimmed = with_halo(source, (("blk", 0),), rim_x)
    padded = jnp.pad(rimmed, ((0, 0), (rim_y, rim_y), (0, 0)))
    flat = point_spread.reshape(view_count, taps_x * taps_y * taps_z)
    spread = lax.dynamic_index_in_dim(flat, view_id, 0, keepdims=False)
    kernel = (spread / jnp.sum(spread)).astype(jnp.bfloat16).reshape(taps_x, taps_y, taps_z)
    forward, backward = band_tables(jnp.stack([kernel, kernel[::-1, ::-1, ::-1]]), depth)
    coverage_row = lax.dynamic_index_in_dim(covered[:, 0, :], view_id, 0, keepdims=False) > 0
    share_cover = lax.dynamic_slice_in_dim(coverage_row, part * share_blocks, share_blocks)
    cell_cover = jnp.repeat(share_cover, BY)[None, :, None]
    image = images[0]
    region = lax.dynamic_slice(
        padded, (0, y_start, 0), (slab_x + 2 * rim_x, share_w + 2 * rim_y, depth)
    )
    blurred = convolve(region, forward, slab_x, share_w)
    quotient = jnp.where(cell_cover, image.astype(jnp.float32) / blurred, 0.0).astype(jnp.bfloat16)
    rim_zeros = jnp.zeros((slab_x, rim_y, depth), jnp.bfloat16)
    edge_rows = jnp.where(part == 0, quotient[:, share_w - rim_y :, :], quotient[:, :rim_y, :])
    partner = swapped(edge_rows, "view", 0)
    lower_rim = jnp.where(part > 0, partner, rim_zeros)
    upper_rim = jnp.where(part < shares - 1, partner, rim_zeros)
    extended = jnp.concatenate([lower_rim, quotient, upper_rim], axis=1)
    quotient_rimmed = with_halo(extended, (("blk", 0),), rim_x)
    cover_plane = jnp.broadcast_to(cell_cover[0].astype(jnp.float32), (share_w, depth))
    return product_gather(quotient_rimmed, backward, cover_plane, estimate, shares)


def solution(mesh):
    in_specs = (P("blk", None, None), P("view", "blk", None, None), P(), P(None, "blk", None))
    out_specs = P("blk", None, None)
    return jax.shard_map(local, mesh=mesh, in_specs=in_specs, out_specs=out_specs, check_vma=False)
```

```python
import functools

import jax
import jax.numpy as jnp
from jax import lax
from jax.experimental import pallas as pl
from jax.experimental.pallas import tpu as pltpu
from jax.sharding import PartitionSpec as P

BY = 32


def with_halo(cells, sides, width):
    for axis, dim in sides:
        count = lax.axis_size(axis)
        ends = count - 1
        head = lax.slice_in_dim(cells, 0, width, axis=dim)
        tail = lax.slice_in_dim(cells, cells.shape[dim] - width, cells.shape[dim], axis=dim)
        cells = jnp.concatenate(
            [
                lax.ppermute(tail, axis, [(i, (i + 1) % count) for i in range(ends)]),
                cells,
                lax.ppermute(head, axis, [((i + 1) % count, i) for i in range(ends)]),
            ],
            axis=dim,
        )
    return cells


def swapped(block, axis, stride):
    count = lax.axis_size(axis)
    route = []
    for low in range(count):
        high = low | 1 << stride
        if high != low and high < count:
            route += [(low, high), (high, low)]
    return lax.ppermute(block, axis, route)


def merged(part, axis, combine):
    gathered = lax.all_gather(part, axis)

    def take(source):
        return lax.dynamic_index_in_dim(gathered, source, 0, False)

    return lax.fori_loop(
        1, lax.axis_size(axis), lambda source, state: combine(state, take(source)), take(0)
    )


def product_kernel(
    n, shares, quot_ref, band_ref, cover_ref, est_ref, out_ref, cols_ref, factor_ref, held,
    send1, recv1, send2, recv2,
):
    groups = n // shares
    step, share_w, depth = held.shape[1:]
    taps_x = band_ref.shape[0]
    taps_y = quot_ref.shape[1] - share_w + 1
    me = lax.axis_index("view")
    view_id = me // shares
    part = me % shares
    mesh_kind = pl.DeviceIdType.MESH
    barrier = pltpu.get_barrier_semaphore()
    for d in range(1, groups):
        pl.semaphore_signal(
            barrier, inc=1, device_id={"view": ((view_id + d) % groups) * shares + part},
            device_id_type=mesh_kind,
        )
    for d in range(1, shares):
        pl.semaphore_signal(
            barrier, inc=1, device_id={"view": view_id * shares + (part + d) % shares},
            device_id_type=mesh_kind,
        )
    for step_y in range(taps_y):
        cols_ref[:, :, step_y * depth : (step_y + 1) * depth] = quot_ref[:, step_y : step_y + share_w, :]
    keep = cover_ref[...] > 0

    def factor_rows(target):
        acc = None
        for shift_x in range(taps_x):
            lhs = cols_ref[pl.ds(target * step + shift_x, step)].reshape(step * share_w, -1)
            part_sum = jnp.dot(lhs, band_ref[shift_x], preferred_element_type=jnp.float32)
            acc = part_sum if acc is None else acc + part_sum
        acc = acc.reshape(step, share_w, depth)
        factor_ref[pl.ds(target * step, step)] = jnp.where(keep[None], acc, 1.0)

    factor_rows(view_id)
    pl.semaphore_wait(barrier, groups + shares - 2)
    outgoing = []
    for d in range(1, groups):
        target = (view_id + d) % groups
        factor_rows(target)
        copy = pltpu.make_async_remote_copy(
            src_ref=factor_ref.at[pl.ds(target * step, step)],
            dst_ref=held.at[view_id],
            send_sem=send1.at[d],
            recv_sem=recv1.at[d],
            device_id={"view": target * shares + part},
            device_id_type=mesh_kind,
        )
        copy.start()
        outgoing.append(copy)
    acc = factor_ref[pl.ds(view_id * step, step)]
    for d in range(1, groups):
        source = (view_id - d + groups) % groups
        pltpu.make_async_remote_copy(
            src_ref=factor_ref.at[pl.ds(0, step)],
            dst_ref=held.at[source],
            send_sem=send1.at[d],
            recv_sem=recv1.at[d],
            device_id={"view": source * shares + part},
            device_id_type=mesh_kind,
        ).wait_recv()
        acc = acc * held[source]
    for copy in outgoing:
        copy.wait_send()
    rows = pl.ds(view_id * step, step)
    cols = pl.ds(part * share_w, share_w)
    out_ref[rows, cols, :] = acc * est_ref[rows, cols, :]
    outgoing = []
    for d in range(1, groups):
        target = (view_id + d) % groups
        copy = pltpu.make_async_remote_copy(
            src_ref=out_ref.at[rows, cols],
            dst_ref=out_ref.at[rows, cols],
            send_sem=send2.at[d],
            recv_sem=recv2.at[d],
            device_id={"view": target * shares + part},
            device_id_type=mesh_kind,
        )
        copy.start()
        outgoing.append(copy)
    for d in range(1, groups):
        source = (view_id - d + groups) % groups
        src_rows = pl.ds(source * step, step)
        pltpu.make_async_remote_copy(
            src_ref=out_ref.at[src_rows, cols],
            dst_ref=out_ref.at[src_rows, cols],
            send_sem=send2.at[d],
            recv_sem=recv2.at[d],
            device_id={"view": source * shares + part},
            device_id_type=mesh_kind,
        ).wait_recv()
    for copy in outgoing:
        copy.wait_send()
    outgoing = []
    for d in range(1, shares):
        other = (part + d) % shares
        copy = pltpu.make_async_remote_copy(
            src_ref=out_ref.at[:, cols],
            dst_ref=out_ref.at[:, cols],
            send_sem=send2.at[groups + d],
            recv_sem=recv2.at[groups + d],
            device_id={"view": view_id * shares + other},
            device_id_type=mesh_kind,
        )
        copy.start()
        outgoing.append(copy)
    for d in range(1, shares):
        other = (part - d + shares) % shares
        other_cols = pl.ds(other * share_w, share_w)
        pltpu.make_async_remote_copy(
            src_ref=out_ref.at[:, other_cols],
            dst_ref=out_ref.at[:, other_cols],
            send_sem=send2.at[groups + d],
            recv_sem=recv2.at[groups + d],
            device_id={"view": view_id * shares + other},
            device_id_type=mesh_kind,
        ).wait_recv()
    for copy in outgoing:
        copy.wait_send()


def product_gather(quotient_rimmed, banded, cover_plane, estimate, shares):
    n = lax.axis_size("view")
    groups = n // shares
    slab_x, width_y, depth = estimate.shape
    share_w = cover_plane.shape[0]
    step = slab_x // groups
    vmem = pl.BlockSpec(memory_space=pltpu.VMEM)
    return pl.pallas_call(
        functools.partial(product_kernel, n, shares),
        out_shape=jax.ShapeDtypeStruct(estimate.shape, jnp.float32),
        in_specs=[vmem] * 4,
        out_specs=vmem,
        scratch_shapes=[
            pltpu.VMEM((quotient_rimmed.shape[0], share_w, banded.shape[1]), jnp.bfloat16),
            pltpu.VMEM((slab_x, share_w, depth), jnp.float32),
            pltpu.VMEM((groups, step, share_w, depth), jnp.float32),
            pltpu.SemaphoreType.DMA((groups,)),
            pltpu.SemaphoreType.DMA((groups,)),
            pltpu.SemaphoreType.DMA((groups + shares,)),
            pltpu.SemaphoreType.DMA((groups + shares,)),
        ],
        compiler_params=pltpu.CompilerParams(collective_id=0, has_side_effects=True),
    )(quotient_rimmed, banded, cover_plane, estimate)


def band_table(kernel, depth):
    taps_x, taps_y, taps_z = kernel.shape
    rim_z = (taps_z - 1) // 2
    shape_three = (taps_z, depth, depth)
    offset = lax.broadcasted_iota(jnp.int32, shape_three, 1) - lax.broadcasted_iota(
        jnp.int32, shape_three, 2
    )
    onehot = (offset + rim_z == lax.broadcasted_iota(jnp.int32, shape_three, 0)).astype(
        jnp.bfloat16
    )
    banded = jnp.einsum("abt,tpz->abpz", kernel, onehot, preferred_element_type=jnp.float32).astype(
        jnp.bfloat16
    )
    return banded.reshape(taps_x, taps_y * depth, depth)


def conv_kernel(tile_x, src_ref, band_ref, image_ref, cover_ref, out_ref, cols_ref):
    rows_x, rows_y, depth = out_ref.shape
    taps_x = src_ref.shape[0] - rows_x + 1
    taps_y = src_ref.shape[1] - rows_y + 1
    for step_y in range(taps_y):
        cols_ref[:, :, step_y * depth : (step_y + 1) * depth] = src_ref[:, step_y : step_y + rows_y, :]
    keep = cover_ref[...] > 0
    for start in range(0, rows_x, tile_x):
        acc = None
        for shift_x in range(taps_x):
            lhs = cols_ref[start + shift_x : start + shift_x + tile_x].reshape(tile_x * rows_y, -1)
            part = jnp.dot(lhs, band_ref[shift_x], preferred_element_type=jnp.float32)
            acc = part if acc is None else acc + part
        blurred = acc.reshape(tile_x, rows_y, depth)
        ratio = image_ref[start : start + tile_x].astype(jnp.float32) / blurred
        out_ref[start : start + tile_x] = jnp.where(keep[None], ratio, 0.0).astype(out_ref.dtype)


def quotient_of(padded_part, banded, image, cover_plane):
    rows_x, rows_y, depth = image.shape
    vmem = pl.BlockSpec(memory_space=pltpu.VMEM)
    return pl.pallas_call(
        functools.partial(conv_kernel, 4),
        out_shape=jax.ShapeDtypeStruct((rows_x, rows_y, depth), jnp.bfloat16),
        in_specs=[vmem] * 4,
        out_specs=vmem,
        scratch_shapes=[pltpu.VMEM((padded_part.shape[0], rows_y, banded.shape[1]), jnp.bfloat16)],
    )(padded_part, banded, image, cover_plane)


def local(estimate, images, point_spread, covered):
    slab_x, width_y, depth = estimate.shape
    share_w = images.shape[2]
    view_count, taps_x, taps_y, taps_z = point_spread.shape
    rim_x, rim_y, rim_z = ((taps_x - 1) // 2, (taps_y - 1) // 2, (taps_z - 1) // 2)
    shares = width_y // share_w
    share_blocks = share_w // BY
    group = lax.axis_index("view")
    view_id = group // shares
    part = group % shares
    y_start = part * share_w
    source = estimate.astype(jnp.bfloat16)
    rimmed = with_halo(source, (("blk", 0),), rim_x)
    padded = jnp.pad(rimmed, ((0, 0), (rim_y, rim_y), (0, 0)))
    spread = lax.dynamic_index_in_dim(point_spread, view_id, 0, keepdims=False)
    kernel = (spread / jnp.sum(spread)).astype(jnp.bfloat16)
    forward = band_table(kernel, depth)
    backward = band_table(kernel[::-1, ::-1, ::-1], depth)
    coverage_row = lax.dynamic_index_in_dim(covered[:, 0, :], view_id, 0, keepdims=False) > 0
    share_cover = lax.dynamic_slice_in_dim(coverage_row, part * share_blocks, share_blocks)
    cell_cover = jnp.repeat(share_cover, BY)[None, :, None]
    image = images[0]
    region = lax.dynamic_slice(
        padded, (0, y_start, 0), (slab_x + 2 * rim_x, share_w + 2 * rim_y, depth)
    )
    cover_plane = jnp.broadcast_to(cell_cover[0].astype(jnp.float32), (share_w, depth))
    quotient = quotient_of(region, forward, image, cover_plane)
    rim_zeros = jnp.zeros((slab_x, rim_y, depth), jnp.bfloat16)
    edge_rows = jnp.where(part == 0, quotient[:, share_w - rim_y :, :], quotient[:, :rim_y, :])
    partner = swapped(edge_rows, "view", 0)
    lower_rim = jnp.where(part > 0, partner, rim_zeros)
    upper_rim = jnp.where(part < shares - 1, partner, rim_zeros)
    extended = jnp.concatenate([lower_rim, quotient, upper_rim], axis=1)
    quotient_rimmed = with_halo(extended, (("blk", 0),), rim_x)
    return product_gather(quotient_rimmed, backward, cover_plane, estimate, shares)


def solution(mesh):
    in_specs = (P("blk", None, None), P("view", "blk", None, None), P(), P(None, "blk", None))
    out_specs = P("blk", None, None)
    return jax.shard_map(local, mesh=mesh, in_specs=in_specs, out_specs=out_specs, check_vma=False)
```

```python
import functools

import jax
import jax.numpy as jnp
from jax import lax
from jax.experimental import pallas as pl
from jax.experimental.pallas import tpu as pltpu
from jax.sharding import PartitionSpec as P

BY = 32


def with_halo(cells, sides, width):
    for axis, dim in sides:
        count = lax.axis_size(axis)
        ends = count - 1
        head = lax.slice_in_dim(cells, 0, width, axis=dim)
        tail = lax.slice_in_dim(cells, cells.shape[dim] - width, cells.shape[dim], axis=dim)
        cells = jnp.concatenate(
            [
                lax.ppermute(tail, axis, [(i, (i + 1) % count) for i in range(ends)]),
                cells,
                lax.ppermute(head, axis, [((i + 1) % count, i) for i in range(ends)]),
            ],
            axis=dim,
        )
    return cells


def swapped(block, axis, stride):
    count = lax.axis_size(axis)
    route = []
    for low in range(count):
        high = low | 1 << stride
        if high != low and high < count:
            route += [(low, high), (high, low)]
    return lax.ppermute(block, axis, route)


def merged(part, axis, combine):
    gathered = lax.all_gather(part, axis)

    def take(source):
        return lax.dynamic_index_in_dim(gathered, source, 0, False)

    return lax.fori_loop(
        1, lax.axis_size(axis), lambda source, state: combine(state, take(source)), take(0)
    )


def product_kernel(
    n, shares, width, quot_ref, band_ref, cover_ref, est_ref, out_ref, ext_ref, cols_ref, factor_ref,
    held, send1, recv1, send2, recv2, send_halo, recv_halo,
):
    groups = n // shares
    step, share_w, depth = held.shape[1:]
    taps_x = band_ref.shape[0]
    taps_y = quot_ref.shape[1] - share_w + 1
    rows = quot_ref.shape[0]
    me = lax.axis_index("view")
    view_id = me // shares
    part = me % shares
    layers = lax.axis_size("blk")
    layer = lax.axis_index("blk")
    up = (layer + 1) % layers
    down = (layer + layers - 1) % layers
    mesh_kind = pl.DeviceIdType.MESH
    barrier = pltpu.get_barrier_semaphore()
    for d in range(1, groups):
        pl.semaphore_signal(
            barrier, inc=1, device_id={"view": ((view_id + d) % groups) * shares + part},
            device_id_type=mesh_kind,
        )
    for d in range(1, shares):
        pl.semaphore_signal(
            barrier, inc=1, device_id={"view": view_id * shares + (part + d) % shares},
            device_id_type=mesh_kind,
        )
    for other in (up, down):
        pl.semaphore_signal(barrier, inc=1, device_id={"blk": other}, device_id_type=mesh_kind)
    ext_ref[pl.ds(width, rows)] = quot_ref[...]

    def build_columns(first, count):
        for step_y in range(taps_y):
            cols_ref[pl.ds(first, count), :, step_y * depth : (step_y + 1) * depth] = ext_ref[
                pl.ds(first, count), step_y : step_y + share_w, :
            ]

    build_columns(width, rows)
    keep = cover_ref[...] > 0

    def factor_rows(target):
        acc = None
        for shift_x in range(taps_x):
            lhs = cols_ref[pl.ds(target * step + shift_x, step)].reshape(step * share_w, -1)
            part_sum = jnp.dot(lhs, band_ref[shift_x], preferred_element_type=jnp.float32)
            acc = part_sum if acc is None else acc + part_sum
        acc = acc.reshape(step, share_w, depth)
        factor_ref[pl.ds(target * step, step)] = jnp.where(keep[None], acc, 1.0)

    pl.semaphore_wait(barrier, groups + shares)
    to_up = pltpu.make_async_remote_copy(
        src_ref=quot_ref.at[pl.ds(rows - width, width)],
        dst_ref=ext_ref.at[pl.ds(0, width)],
        send_sem=send_halo.at[0],
        recv_sem=recv_halo.at[0],
        device_id={"blk": up},
        device_id_type=mesh_kind,
    )
    to_down = pltpu.make_async_remote_copy(
        src_ref=quot_ref.at[pl.ds(0, width)],
        dst_ref=ext_ref.at[pl.ds(rows + width, width)],
        send_sem=send_halo.at[1],
        recv_sem=recv_halo.at[1],
        device_id={"blk": down},
        device_id_type=mesh_kind,
    )
    to_up.start()
    to_down.start()
    reach = width // step
    inner = list(range(reach, groups - reach))
    outer = list(range(reach)) + list(range(groups - reach, groups))
    outgoing = []

    def send_chunk(target):
        factor_rows(target)
        copy = pltpu.make_async_remote_copy(
            src_ref=factor_ref.at[pl.ds(target * step, step)],
            dst_ref=held.at[view_id],
            send_sem=send1.at[target],
            recv_sem=recv1.at[view_id],
            device_id={"view": target * shares + part},
            device_id_type=mesh_kind,
        )

        @pl.when(target != view_id)
        def _():
            copy.start()

        outgoing.append((target, copy))

    for target in inner:
        send_chunk(target)
    to_up.wait()
    to_down.wait()

    @pl.when(layer == 0)
    def _():
        ext_ref[pl.ds(0, width)] = jnp.zeros((width,) + quot_ref.shape[1:], quot_ref.dtype)

    @pl.when(layer == layers - 1)
    def _():
        ext_ref[pl.ds(rows + width, width)] = jnp.zeros((width,) + quot_ref.shape[1:], quot_ref.dtype)

    build_columns(0, width)
    build_columns(rows + width, width)
    for target in outer:
        send_chunk(target)
    acc = factor_ref[pl.ds(view_id * step, step)]
    for d in range(1, groups):
        source = (view_id - d + groups) % groups
        pltpu.make_async_remote_copy(
            src_ref=factor_ref.at[pl.ds(0, step)],
            dst_ref=held.at[source],
            send_sem=send1.at[source],
            recv_sem=recv1.at[source],
            device_id={"view": source * shares + part},
            device_id_type=mesh_kind,
        ).wait_recv()
        acc = acc * held[source]
    for target, copy in outgoing:

        @pl.when(target != view_id)
        def _():
            copy.wait_send()

    mine = pl.ds(view_id * step, step)
    cols = pl.ds(part * share_w, share_w)
    out_ref[mine, cols, :] = acc * est_ref[mine, cols, :]
    outgoing = []
    for d in range(1, groups):
        target = (view_id + d) % groups
        copy = pltpu.make_async_remote_copy(
            src_ref=out_ref.at[mine, cols],
            dst_ref=out_ref.at[mine, cols],
            send_sem=send2.at[d],
            recv_sem=recv2.at[d],
            device_id={"view": target * shares + part},
            device_id_type=mesh_kind,
        )
        copy.start()
        outgoing.append(copy)
    for d in range(1, groups):
        source = (view_id - d + groups) % groups
        src_rows = pl.ds(source * step, step)
        pltpu.make_async_remote_copy(
            src_ref=out_ref.at[src_rows, cols],
            dst_ref=out_ref.at[src_rows, cols],
            send_sem=send2.at[d],
            recv_sem=recv2.at[d],
            device_id={"view": source * shares + part},
            device_id_type=mesh_kind,
        ).wait_recv()
    for copy in outgoing:
        copy.wait_send()
    outgoing = []
    for d in range(1, shares):
        other = (part + d) % shares
        copy = pltpu.make_async_remote_copy(
            src_ref=out_ref.at[:, cols],
            dst_ref=out_ref.at[:, cols],
            send_sem=send2.at[groups + d],
            recv_sem=recv2.at[groups + d],
            device_id={"view": view_id * shares + other},
            device_id_type=mesh_kind,
        )
        copy.start()
        outgoing.append(copy)
    for d in range(1, shares):
        other = (part - d + shares) % shares
        other_cols = pl.ds(other * share_w, share_w)
        pltpu.make_async_remote_copy(
            src_ref=out_ref.at[:, other_cols],
            dst_ref=out_ref.at[:, other_cols],
            send_sem=send2.at[groups + d],
            recv_sem=recv2.at[groups + d],
            device_id={"view": view_id * shares + other},
            device_id_type=mesh_kind,
        ).wait_recv()
    for copy in outgoing:
        copy.wait_send()


def product_gather(extended, banded, cover_plane, estimate, shares, width):
    n = lax.axis_size("view")
    groups = n // shares
    slab_x, width_y, depth = estimate.shape
    share_w = cover_plane.shape[0]
    step = slab_x // groups
    padded_rows = extended.shape[0] + 2 * width
    vmem = pl.BlockSpec(memory_space=pltpu.VMEM)
    return pl.pallas_call(
        functools.partial(product_kernel, n, shares, width),
        out_shape=jax.ShapeDtypeStruct(estimate.shape, jnp.float32),
        in_specs=[vmem] * 4,
        out_specs=vmem,
        scratch_shapes=[
            pltpu.VMEM((padded_rows,) + extended.shape[1:], extended.dtype),
            pltpu.VMEM((padded_rows, share_w, banded.shape[1]), jnp.bfloat16),
            pltpu.VMEM((slab_x, share_w, depth), jnp.float32),
            pltpu.VMEM((groups, step, share_w, depth), jnp.float32),
            pltpu.SemaphoreType.DMA((groups,)),
            pltpu.SemaphoreType.DMA((groups,)),
            pltpu.SemaphoreType.DMA((groups + shares,)),
            pltpu.SemaphoreType.DMA((groups + shares,)),
            pltpu.SemaphoreType.DMA((2,)),
            pltpu.SemaphoreType.DMA((2,)),
        ],
        compiler_params=pltpu.CompilerParams(collective_id=0, has_side_effects=True),
    )(extended, banded, cover_plane, estimate)


def band_table(kernel, depth):
    taps_x, taps_y, taps_z = kernel.shape
    rim_z = (taps_z - 1) // 2
    shape_three = (taps_z, depth, depth)
    offset = lax.broadcasted_iota(jnp.int32, shape_three, 1) - lax.broadcasted_iota(
        jnp.int32, shape_three, 2
    )
    onehot = (offset + rim_z == lax.broadcasted_iota(jnp.int32, shape_three, 0)).astype(
        jnp.bfloat16
    )
    banded = jnp.einsum("abt,tpz->abpz", kernel, onehot, preferred_element_type=jnp.float32).astype(
        jnp.bfloat16
    )
    return banded.reshape(taps_x, taps_y * depth, depth)


def conv_kernel(tile_x, src_ref, band_ref, image_ref, cover_ref, out_ref, cols_ref):
    rows_x, rows_y, depth = out_ref.shape
    taps_x = src_ref.shape[0] - rows_x + 1
    taps_y = src_ref.shape[1] - rows_y + 1
    for step_y in range(taps_y):
        cols_ref[:, :, step_y * depth : (step_y + 1) * depth] = src_ref[:, step_y : step_y + rows_y, :]
    keep = cover_ref[...] > 0
    for start in range(0, rows_x, tile_x):
        acc = None
        for shift_x in range(taps_x):
            lhs = cols_ref[start + shift_x : start + shift_x + tile_x].reshape(tile_x * rows_y, -1)
            part = jnp.dot(lhs, band_ref[shift_x], preferred_element_type=jnp.float32)
            acc = part if acc is None else acc + part
        blurred = acc.reshape(tile_x, rows_y, depth)
        ratio = image_ref[start : start + tile_x].astype(jnp.float32) / blurred
        out_ref[start : start + tile_x] = jnp.where(keep[None], ratio, 0.0).astype(out_ref.dtype)


def quotient_of(padded_part, banded, image, cover_plane):
    rows_x, rows_y, depth = image.shape
    vmem = pl.BlockSpec(memory_space=pltpu.VMEM)
    return pl.pallas_call(
        functools.partial(conv_kernel, 4),
        out_shape=jax.ShapeDtypeStruct((rows_x, rows_y, depth), jnp.bfloat16),
        in_specs=[vmem] * 4,
        out_specs=vmem,
        scratch_shapes=[pltpu.VMEM((padded_part.shape[0], rows_y, banded.shape[1]), jnp.bfloat16)],
    )(padded_part, banded, image, cover_plane)


def local(estimate, images, point_spread, covered):
    slab_x, width_y, depth = estimate.shape
    share_w = images.shape[2]
    view_count, taps_x, taps_y, taps_z = point_spread.shape
    rim_x, rim_y, rim_z = ((taps_x - 1) // 2, (taps_y - 1) // 2, (taps_z - 1) // 2)
    shares = width_y // share_w
    share_blocks = share_w // BY
    group = lax.axis_index("view")
    view_id = group // shares
    part = group % shares
    y_start = part * share_w
    source = estimate.astype(jnp.bfloat16)
    rimmed = with_halo(source, (("blk", 0),), rim_x)
    padded = jnp.pad(rimmed, ((0, 0), (rim_y, rim_y), (0, 0)))
    spread = lax.dynamic_index_in_dim(point_spread, view_id, 0, keepdims=False)
    kernel = (spread / jnp.sum(spread)).astype(jnp.bfloat16)
    forward = band_table(kernel, depth)
    backward = band_table(kernel[::-1, ::-1, ::-1], depth)
    coverage_row = lax.dynamic_index_in_dim(covered[:, 0, :], view_id, 0, keepdims=False) > 0
    share_cover = lax.dynamic_slice_in_dim(coverage_row, part * share_blocks, share_blocks)
    cell_cover = jnp.repeat(share_cover, BY)[None, :, None]
    image = images[0]
    region = lax.dynamic_slice(
        padded, (0, y_start, 0), (slab_x + 2 * rim_x, share_w + 2 * rim_y, depth)
    )
    cover_plane = jnp.broadcast_to(cell_cover[0].astype(jnp.float32), (share_w, depth))
    quotient = quotient_of(region, forward, image, cover_plane)
    rim_zeros = jnp.zeros((slab_x, rim_y, depth), jnp.bfloat16)
    edge_rows = jnp.where(part == 0, quotient[:, share_w - rim_y :, :], quotient[:, :rim_y, :])
    partner = swapped(edge_rows, "view", 0)
    lower_rim = jnp.where(part > 0, partner, rim_zeros)
    upper_rim = jnp.where(part < shares - 1, partner, rim_zeros)
    extended = jnp.concatenate([lower_rim, quotient, upper_rim], axis=1)
    return product_gather(extended, backward, cover_plane, estimate, shares, rim_x)


def solution(mesh):
    in_specs = (P("blk", None, None), P("view", "blk", None, None), P(), P(None, "blk", None))
    out_specs = P("blk", None, None)
    return jax.shard_map(local, mesh=mesh, in_specs=in_specs, out_specs=out_specs, check_vma=False)
```

```python
import functools

import jax
import jax.numpy as jnp
from jax import lax
from jax.experimental import pallas as pl
from jax.experimental.pallas import tpu as pltpu
from jax.sharding import PartitionSpec as P

BY = 32


def with_halo(cells, sides, width):
    for axis, dim in sides:
        count = lax.axis_size(axis)
        ends = count - 1
        head = lax.slice_in_dim(cells, 0, width, axis=dim)
        tail = lax.slice_in_dim(cells, cells.shape[dim] - width, cells.shape[dim], axis=dim)
        cells = jnp.concatenate(
            [
                lax.ppermute(tail, axis, [(i, (i + 1) % count) for i in range(ends)]),
                cells,
                lax.ppermute(head, axis, [((i + 1) % count, i) for i in range(ends)]),
            ],
            axis=dim,
        )
    return cells


def swapped(block, axis, stride):
    count = lax.axis_size(axis)
    route = []
    for low in range(count):
        high = low | 1 << stride
        if high != low and high < count:
            route += [(low, high), (high, low)]
    return lax.ppermute(block, axis, route)


def merged(part, axis, combine):
    gathered = lax.all_gather(part, axis)

    def take(source):
        return lax.dynamic_index_in_dim(gathered, source, 0, False)

    return lax.fori_loop(
        1, lax.axis_size(axis), lambda source, state: combine(state, take(source)), take(0)
    )


def product_kernel(
    n, shares, width, quot_ref, band_ref, cover_ref, est_ref, out_ref, ext_ref, cols_ref, factor_ref,
    held, send1, recv1, send2, recv2, send_halo, recv_halo,
):
    groups = n // shares
    step, share_w, depth = held.shape[1:]
    taps_x = band_ref.shape[0]
    taps_y = quot_ref.shape[1] - share_w + 1
    rows = quot_ref.shape[0]
    me = lax.axis_index("view")
    view_id = me // shares
    part = me % shares
    layers = lax.axis_size("blk")
    layer = lax.axis_index("blk")
    up = (layer + 1) % layers
    down = (layer + layers - 1) % layers
    mesh_kind = pl.DeviceIdType.MESH
    barrier = pltpu.get_barrier_semaphore()
    for d in range(1, groups):
        pl.semaphore_signal(
            barrier, inc=1, device_id={"view": ((view_id + d) % groups) * shares + part},
            device_id_type=mesh_kind,
        )
    for d in range(1, shares):
        pl.semaphore_signal(
            barrier, inc=1, device_id={"view": view_id * shares + (part + d) % shares},
            device_id_type=mesh_kind,
        )
    has_up = layer < layers - 1
    has_down = layer > 0

    @pl.when(has_up)
    def _():
        pl.semaphore_signal(barrier, inc=1, device_id={"blk": up}, device_id_type=mesh_kind)

    @pl.when(has_down)
    def _():
        pl.semaphore_signal(barrier, inc=1, device_id={"blk": down}, device_id_type=mesh_kind)

    ext_ref[pl.ds(width, rows)] = quot_ref[...]

    def build_columns(first, count):
        for step_y in range(taps_y):
            cols_ref[pl.ds(first, count), :, step_y * depth : (step_y + 1) * depth] = ext_ref[
                pl.ds(first, count), step_y : step_y + share_w, :
            ]

    build_columns(width, rows)
    keep = cover_ref[...] > 0

    def factor_rows(target):
        acc = None
        for shift_x in range(taps_x):
            lhs = cols_ref[pl.ds(target * step + shift_x, step)].reshape(step * share_w, -1)
            part_sum = jnp.dot(lhs, band_ref[shift_x], preferred_element_type=jnp.float32)
            acc = part_sum if acc is None else acc + part_sum
        acc = acc.reshape(step, share_w, depth)
        factor_ref[pl.ds(target * step, step)] = jnp.where(keep[None], acc, 1.0)

    pl.semaphore_wait(
        barrier, groups + shares - 2 + has_up.astype(jnp.int32) + has_down.astype(jnp.int32)
    )
    to_up = pltpu.make_async_remote_copy(
        src_ref=quot_ref.at[pl.ds(rows - width, width)],
        dst_ref=ext_ref.at[pl.ds(0, width)],
        send_sem=send_halo.at[0],
        recv_sem=recv_halo.at[0],
        device_id={"blk": up},
        device_id_type=mesh_kind,
    )
    to_down = pltpu.make_async_remote_copy(
        src_ref=quot_ref.at[pl.ds(0, width)],
        dst_ref=ext_ref.at[pl.ds(rows + width, width)],
        send_sem=send_halo.at[1],
        recv_sem=recv_halo.at[1],
        device_id={"blk": down},
        device_id_type=mesh_kind,
    )
    @pl.when(has_up)
    def _():
        to_up.start()

    @pl.when(has_down)
    def _():
        to_down.start()

    reach = width // step
    inner = list(range(reach, groups - reach))
    outer = list(range(reach)) + list(range(groups - reach, groups))
    outgoing = []

    def send_chunk(target):
        factor_rows(target)
        copy = pltpu.make_async_remote_copy(
            src_ref=factor_ref.at[pl.ds(target * step, step)],
            dst_ref=held.at[view_id],
            send_sem=send1.at[target],
            recv_sem=recv1.at[view_id],
            device_id={"view": target * shares + part},
            device_id_type=mesh_kind,
        )

        @pl.when(target != view_id)
        def _():
            copy.start()

        outgoing.append((target, copy))

    for target in inner:
        send_chunk(target)
    @pl.when(has_up)
    def _():
        to_up.wait_send()
        to_down.wait_recv()

    @pl.when(has_down)
    def _():
        to_down.wait_send()
        to_up.wait_recv()

    @pl.when(layer == 0)
    def _():
        ext_ref[pl.ds(0, width)] = jnp.zeros((width,) + quot_ref.shape[1:], quot_ref.dtype)

    @pl.when(layer == layers - 1)
    def _():
        ext_ref[pl.ds(rows + width, width)] = jnp.zeros((width,) + quot_ref.shape[1:], quot_ref.dtype)

    build_columns(0, width)
    build_columns(rows + width, width)
    for target in outer:
        send_chunk(target)
    acc = factor_ref[pl.ds(view_id * step, step)]
    for d in range(1, groups):
        source = (view_id - d + groups) % groups
        pltpu.make_async_remote_copy(
            src_ref=factor_ref.at[pl.ds(0, step)],
            dst_ref=held.at[source],
            send_sem=send1.at[source],
            recv_sem=recv1.at[source],
            device_id={"view": source * shares + part},
            device_id_type=mesh_kind,
        ).wait_recv()
        acc = acc * held[source]
    for target, copy in outgoing:

        @pl.when(target != view_id)
        def _():
            copy.wait_send()

    mine = pl.ds(view_id * step, step)
    cols = pl.ds(part * share_w, share_w)
    out_ref[mine, cols, :] = acc * est_ref[mine, cols, :]
    outgoing = []
    for d in range(1, groups):
        target = (view_id + d) % groups
        copy = pltpu.make_async_remote_copy(
            src_ref=out_ref.at[mine, cols],
            dst_ref=out_ref.at[mine, cols],
            send_sem=send2.at[d],
            recv_sem=recv2.at[d],
            device_id={"view": target * shares + part},
            device_id_type=mesh_kind,
        )
        copy.start()
        outgoing.append(copy)
    for d in range(1, groups):
        source = (view_id - d + groups) % groups
        src_rows = pl.ds(source * step, step)
        pltpu.make_async_remote_copy(
            src_ref=out_ref.at[src_rows, cols],
            dst_ref=out_ref.at[src_rows, cols],
            send_sem=send2.at[d],
            recv_sem=recv2.at[d],
            device_id={"view": source * shares + part},
            device_id_type=mesh_kind,
        ).wait_recv()
    for copy in outgoing:
        copy.wait_send()
    outgoing = []
    for d in range(1, shares):
        other = (part + d) % shares
        copy = pltpu.make_async_remote_copy(
            src_ref=out_ref.at[:, cols],
            dst_ref=out_ref.at[:, cols],
            send_sem=send2.at[groups + d],
            recv_sem=recv2.at[groups + d],
            device_id={"view": view_id * shares + other},
            device_id_type=mesh_kind,
        )
        copy.start()
        outgoing.append(copy)
    for d in range(1, shares):
        other = (part - d + shares) % shares
        other_cols = pl.ds(other * share_w, share_w)
        pltpu.make_async_remote_copy(
            src_ref=out_ref.at[:, other_cols],
            dst_ref=out_ref.at[:, other_cols],
            send_sem=send2.at[groups + d],
            recv_sem=recv2.at[groups + d],
            device_id={"view": view_id * shares + other},
            device_id_type=mesh_kind,
        ).wait_recv()
    for copy in outgoing:
        copy.wait_send()


def product_gather(extended, banded, cover_plane, estimate, shares, width):
    n = lax.axis_size("view")
    groups = n // shares
    slab_x, width_y, depth = estimate.shape
    share_w = cover_plane.shape[0]
    step = slab_x // groups
    padded_rows = extended.shape[0] + 2 * width
    vmem = pl.BlockSpec(memory_space=pltpu.VMEM)
    return pl.pallas_call(
        functools.partial(product_kernel, n, shares, width),
        out_shape=jax.ShapeDtypeStruct(estimate.shape, jnp.float32),
        in_specs=[vmem] * 4,
        out_specs=vmem,
        scratch_shapes=[
            pltpu.VMEM((padded_rows,) + extended.shape[1:], extended.dtype),
            pltpu.VMEM((padded_rows, share_w, banded.shape[1]), jnp.bfloat16),
            pltpu.VMEM((slab_x, share_w, depth), jnp.float32),
            pltpu.VMEM((groups, step, share_w, depth), jnp.float32),
            pltpu.SemaphoreType.DMA((groups,)),
            pltpu.SemaphoreType.DMA((groups,)),
            pltpu.SemaphoreType.DMA((groups + shares,)),
            pltpu.SemaphoreType.DMA((groups + shares,)),
            pltpu.SemaphoreType.DMA((2,)),
            pltpu.SemaphoreType.DMA((2,)),
        ],
        compiler_params=pltpu.CompilerParams(collective_id=0, has_side_effects=True),
    )(extended, banded, cover_plane, estimate)


def band_table(kernel, depth):
    taps_x, taps_y, taps_z = kernel.shape
    rim_z = (taps_z - 1) // 2
    shape_three = (taps_z, depth, depth)
    offset = lax.broadcasted_iota(jnp.int32, shape_three, 1) - lax.broadcasted_iota(
        jnp.int32, shape_three, 2
    )
    onehot = (offset + rim_z == lax.broadcasted_iota(jnp.int32, shape_three, 0)).astype(
        jnp.bfloat16
    )
    banded = jnp.einsum("abt,tpz->abpz", kernel, onehot, preferred_element_type=jnp.float32).astype(
        jnp.bfloat16
    )
    return banded.reshape(taps_x, taps_y * depth, depth)


def conv_kernel(tile_x, src_ref, band_ref, image_ref, cover_ref, out_ref, cols_ref):
    rows_x, rows_y, depth = out_ref.shape
    taps_x = src_ref.shape[0] - rows_x + 1
    taps_y = src_ref.shape[1] - rows_y + 1
    for step_y in range(taps_y):
        cols_ref[:, :, step_y * depth : (step_y + 1) * depth] = src_ref[:, step_y : step_y + rows_y, :]
    keep = cover_ref[...] > 0
    for start in range(0, rows_x, tile_x):
        acc = None
        for shift_x in range(taps_x):
            lhs = cols_ref[start + shift_x : start + shift_x + tile_x].reshape(tile_x * rows_y, -1)
            part = jnp.dot(lhs, band_ref[shift_x], preferred_element_type=jnp.float32)
            acc = part if acc is None else acc + part
        blurred = acc.reshape(tile_x, rows_y, depth)
        ratio = image_ref[start : start + tile_x].astype(jnp.float32) / blurred
        out_ref[start : start + tile_x] = jnp.where(keep[None], ratio, 0.0).astype(out_ref.dtype)


def quotient_of(padded_part, banded, image, cover_plane):
    rows_x, rows_y, depth = image.shape
    vmem = pl.BlockSpec(memory_space=pltpu.VMEM)
    return pl.pallas_call(
        functools.partial(conv_kernel, 4),
        out_shape=jax.ShapeDtypeStruct((rows_x, rows_y, depth), jnp.bfloat16),
        in_specs=[vmem] * 4,
        out_specs=vmem,
        scratch_shapes=[pltpu.VMEM((padded_part.shape[0], rows_y, banded.shape[1]), jnp.bfloat16)],
    )(padded_part, banded, image, cover_plane)


def local(estimate, images, point_spread, covered):
    slab_x, width_y, depth = estimate.shape
    share_w = images.shape[2]
    view_count, taps_x, taps_y, taps_z = point_spread.shape
    rim_x, rim_y, rim_z = ((taps_x - 1) // 2, (taps_y - 1) // 2, (taps_z - 1) // 2)
    shares = width_y // share_w
    share_blocks = share_w // BY
    group = lax.axis_index("view")
    view_id = group // shares
    part = group % shares
    y_start = part * share_w
    source = estimate.astype(jnp.bfloat16)
    rimmed = with_halo(source, (("blk", 0),), rim_x)
    padded = jnp.pad(rimmed, ((0, 0), (rim_y, rim_y), (0, 0)))
    spread = lax.dynamic_index_in_dim(point_spread, view_id, 0, keepdims=False)
    kernel = (spread / jnp.sum(spread)).astype(jnp.bfloat16)
    forward = band_table(kernel, depth)
    backward = band_table(kernel[::-1, ::-1, ::-1], depth)
    coverage_row = lax.dynamic_index_in_dim(covered[:, 0, :], view_id, 0, keepdims=False) > 0
    share_cover = lax.dynamic_slice_in_dim(coverage_row, part * share_blocks, share_blocks)
    cell_cover = jnp.repeat(share_cover, BY)[None, :, None]
    image = images[0]
    region = lax.dynamic_slice(
        padded, (0, y_start, 0), (slab_x + 2 * rim_x, share_w + 2 * rim_y, depth)
    )
    cover_plane = jnp.broadcast_to(cell_cover[0].astype(jnp.float32), (share_w, depth))
    quotient = quotient_of(region, forward, image, cover_plane)
    rim_zeros = jnp.zeros((slab_x, rim_y, depth), jnp.bfloat16)
    edge_rows = jnp.where(part == 0, quotient[:, share_w - rim_y :, :], quotient[:, :rim_y, :])
    partner = swapped(edge_rows, "view", 0)
    lower_rim = jnp.where(part > 0, partner, rim_zeros)
    upper_rim = jnp.where(part < shares - 1, partner, rim_zeros)
    extended = jnp.concatenate([lower_rim, quotient, upper_rim], axis=1)
    return product_gather(extended, backward, cover_plane, estimate, shares, rim_x)


def solution(mesh):
    in_specs = (P("blk", None, None), P("view", "blk", None, None), P(), P(None, "blk", None))
    out_specs = P("blk", None, None)
    return jax.shard_map(local, mesh=mesh, in_specs=in_specs, out_specs=out_specs, check_vma=False)
```

```python
import functools

import jax
import jax.numpy as jnp
from jax import lax
from jax.experimental import pallas as pl
from jax.experimental.pallas import tpu as pltpu
from jax.sharding import PartitionSpec as P

BY = 32


def with_halo(cells, sides, width):
    for axis, dim in sides:
        count = lax.axis_size(axis)
        ends = count - 1
        head = lax.slice_in_dim(cells, 0, width, axis=dim)
        tail = lax.slice_in_dim(cells, cells.shape[dim] - width, cells.shape[dim], axis=dim)
        cells = jnp.concatenate(
            [
                lax.ppermute(tail, axis, [(i, (i + 1) % count) for i in range(ends)]),
                cells,
                lax.ppermute(head, axis, [((i + 1) % count, i) for i in range(ends)]),
            ],
            axis=dim,
        )
    return cells


def swapped(block, axis, stride):
    count = lax.axis_size(axis)
    route = []
    for low in range(count):
        high = low | 1 << stride
        if high != low and high < count:
            route += [(low, high), (high, low)]
    return lax.ppermute(block, axis, route)


def merged(part, axis, combine):
    gathered = lax.all_gather(part, axis)

    def take(source):
        return lax.dynamic_index_in_dim(gathered, source, 0, False)

    return lax.fori_loop(
        1, lax.axis_size(axis), lambda source, state: combine(state, take(source)), take(0)
    )


def product_kernel(
    n, shares, width, quot_ref, band_ref, cover_ref, est_ref, out_ref, ext_ref, cols_ref, factor_ref,
    held, send1, recv1, send2, recv2, send3, recv3, send_halo, recv_halo,
):
    groups = n // shares
    step, share_w, depth = held.shape[1:]
    taps_x = band_ref.shape[0]
    taps_y = quot_ref.shape[1] - share_w + 1
    rows = quot_ref.shape[0]
    me = lax.axis_index("view")
    view_id = me // shares
    part = me % shares
    layers = lax.axis_size("blk")
    layer = lax.axis_index("blk")
    up = (layer + 1) % layers
    down = (layer + layers - 1) % layers
    mesh_kind = pl.DeviceIdType.MESH
    barrier = pltpu.get_barrier_semaphore()
    for d in range(1, groups):
        pl.semaphore_signal(
            barrier, inc=1, device_id={"view": ((view_id + d) % groups) * shares + part},
            device_id_type=mesh_kind,
        )
    for d in range(1, shares):
        pl.semaphore_signal(
            barrier, inc=1, device_id={"view": view_id * shares + (part + d) % shares},
            device_id_type=mesh_kind,
        )
    has_up = layer < layers - 1
    has_down = layer > 0

    @pl.when(has_up)
    def _():
        pl.semaphore_signal(barrier, inc=1, device_id={"blk": up}, device_id_type=mesh_kind)

    @pl.when(has_down)
    def _():
        pl.semaphore_signal(barrier, inc=1, device_id={"blk": down}, device_id_type=mesh_kind)

    ext_ref[pl.ds(width, rows)] = quot_ref[...]

    def build_columns(first, count):
        for step_y in range(taps_y):
            cols_ref[pl.ds(first, count), :, step_y * depth : (step_y + 1) * depth] = ext_ref[
                pl.ds(first, count), step_y : step_y + share_w, :
            ]

    build_columns(width, rows)
    keep = cover_ref[...] > 0

    def factor_rows(target):
        acc = None
        for shift_x in range(taps_x):
            lhs = cols_ref[pl.ds(target * step + shift_x, step)].reshape(step * share_w, -1)
            part_sum = jnp.dot(lhs, band_ref[shift_x], preferred_element_type=jnp.float32)
            acc = part_sum if acc is None else acc + part_sum
        acc = acc.reshape(step, share_w, depth)
        factor_ref[pl.ds(target * step, step)] = jnp.where(keep[None], acc, 1.0)

    pl.semaphore_wait(
        barrier, groups + shares - 2 + has_up.astype(jnp.int32) + has_down.astype(jnp.int32)
    )
    to_up = pltpu.make_async_remote_copy(
        src_ref=quot_ref.at[pl.ds(rows - width, width)],
        dst_ref=ext_ref.at[pl.ds(0, width)],
        send_sem=send_halo.at[0],
        recv_sem=recv_halo.at[0],
        device_id={"blk": up},
        device_id_type=mesh_kind,
    )
    to_down = pltpu.make_async_remote_copy(
        src_ref=quot_ref.at[pl.ds(0, width)],
        dst_ref=ext_ref.at[pl.ds(rows + width, width)],
        send_sem=send_halo.at[1],
        recv_sem=recv_halo.at[1],
        device_id={"blk": down},
        device_id_type=mesh_kind,
    )
    @pl.when(has_up)
    def _():
        to_up.start()

    @pl.when(has_down)
    def _():
        to_down.start()

    reach = width // step
    inner = list(range(reach, groups - reach))
    outer = list(range(reach)) + list(range(groups - reach, groups))
    outgoing = []

    def send_chunk(target):
        factor_rows(target)
        copy = pltpu.make_async_remote_copy(
            src_ref=factor_ref.at[pl.ds(target * step, step)],
            dst_ref=held.at[view_id],
            send_sem=send1.at[target],
            recv_sem=recv1.at[view_id],
            device_id={"view": target * shares + part},
            device_id_type=mesh_kind,
        )

        @pl.when(target != view_id)
        def _():
            copy.start()

        outgoing.append((target, copy))

    for target in inner:
        send_chunk(target)
    @pl.when(has_up)
    def _():
        to_up.wait_send()
        to_down.wait_recv()

    @pl.when(has_down)
    def _():
        to_down.wait_send()
        to_up.wait_recv()

    @pl.when(layer == 0)
    def _():
        ext_ref[pl.ds(0, width)] = jnp.zeros((width,) + quot_ref.shape[1:], quot_ref.dtype)

    @pl.when(layer == layers - 1)
    def _():
        ext_ref[pl.ds(rows + width, width)] = jnp.zeros((width,) + quot_ref.shape[1:], quot_ref.dtype)

    build_columns(0, width)
    build_columns(rows + width, width)
    for target in outer:
        send_chunk(target)
    acc = factor_ref[pl.ds(view_id * step, step)]
    for d in range(1, groups):
        source = (view_id - d + groups) % groups
        pltpu.make_async_remote_copy(
            src_ref=factor_ref.at[pl.ds(0, step)],
            dst_ref=held.at[source],
            send_sem=send1.at[source],
            recv_sem=recv1.at[source],
            device_id={"view": source * shares + part},
            device_id_type=mesh_kind,
        ).wait_recv()
        acc = acc * held[source]
    for target, copy in outgoing:

        @pl.when(target != view_id)
        def _():
            copy.wait_send()

    mine = pl.ds(view_id * step, step)
    cols = pl.ds(part * share_w, share_w)
    out_ref[mine, cols, :] = acc * est_ref[mine, cols, :]
    other = (part + 1) % shares
    partner = view_id * shares + other
    other_cols = pl.ds(other * share_w, share_w)
    outgoing = []
    for d in range(1, groups):
        target = (view_id + d) % groups
        copy = pltpu.make_async_remote_copy(
            src_ref=out_ref.at[mine, cols],
            dst_ref=out_ref.at[mine, cols],
            send_sem=send2.at[d],
            recv_sem=recv2.at[d],
            device_id={"view": target * shares + part},
            device_id_type=mesh_kind,
        )
        copy.start()
        outgoing.append(copy)

    def forward(chunk):
        copy = pltpu.make_async_remote_copy(
            src_ref=out_ref.at[pl.ds(chunk * step, step), cols],
            dst_ref=out_ref.at[pl.ds(chunk * step, step), cols],
            send_sem=send3.at[chunk],
            recv_sem=recv3.at[chunk],
            device_id={"view": partner},
            device_id_type=mesh_kind,
        )
        copy.start()
        outgoing.append(copy)

    forward(view_id)
    for d in range(1, groups):
        source = (view_id - d + groups) % groups
        src_rows = pl.ds(source * step, step)
        pltpu.make_async_remote_copy(
            src_ref=out_ref.at[src_rows, cols],
            dst_ref=out_ref.at[src_rows, cols],
            send_sem=send2.at[d],
            recv_sem=recv2.at[d],
            device_id={"view": source * shares + part},
            device_id_type=mesh_kind,
        ).wait_recv()
        forward(source)
    for chunk in range(groups):
        chunk_rows = pl.ds(chunk * step, step)
        pltpu.make_async_remote_copy(
            src_ref=out_ref.at[chunk_rows, other_cols],
            dst_ref=out_ref.at[chunk_rows, other_cols],
            send_sem=send3.at[chunk],
            recv_sem=recv3.at[chunk],
            device_id={"view": partner},
            device_id_type=mesh_kind,
        ).wait_recv()
    for copy in outgoing:
        copy.wait_send()


def product_gather(extended, banded, cover_plane, estimate, shares, width):
    n = lax.axis_size("view")
    groups = n // shares
    slab_x, width_y, depth = estimate.shape
    share_w = cover_plane.shape[0]
    step = slab_x // groups
    padded_rows = extended.shape[0] + 2 * width
    vmem = pl.BlockSpec(memory_space=pltpu.VMEM)
    return pl.pallas_call(
        functools.partial(product_kernel, n, shares, width),
        out_shape=jax.ShapeDtypeStruct(estimate.shape, jnp.float32),
        in_specs=[vmem] * 4,
        out_specs=vmem,
        scratch_shapes=[
            pltpu.VMEM((padded_rows,) + extended.shape[1:], extended.dtype),
            pltpu.VMEM((padded_rows, share_w, banded.shape[1]), jnp.bfloat16),
            pltpu.VMEM((slab_x, share_w, depth), jnp.float32),
            pltpu.VMEM((groups, step, share_w, depth), jnp.float32),
            pltpu.SemaphoreType.DMA((groups,)),
            pltpu.SemaphoreType.DMA((groups,)),
            pltpu.SemaphoreType.DMA((groups,)),
            pltpu.SemaphoreType.DMA((groups,)),
            pltpu.SemaphoreType.DMA((groups,)),
            pltpu.SemaphoreType.DMA((groups,)),
            pltpu.SemaphoreType.DMA((2,)),
            pltpu.SemaphoreType.DMA((2,)),
        ],
        compiler_params=pltpu.CompilerParams(collective_id=0, has_side_effects=True),
    )(extended, banded, cover_plane, estimate)


def band_table(kernel, depth):
    taps_x, taps_y, taps_z = kernel.shape
    rim_z = (taps_z - 1) // 2
    shape_three = (taps_z, depth, depth)
    offset = lax.broadcasted_iota(jnp.int32, shape_three, 1) - lax.broadcasted_iota(
        jnp.int32, shape_three, 2
    )
    onehot = (offset + rim_z == lax.broadcasted_iota(jnp.int32, shape_three, 0)).astype(
        jnp.bfloat16
    )
    banded = jnp.einsum("abt,tpz->abpz", kernel, onehot, preferred_element_type=jnp.float32).astype(
        jnp.bfloat16
    )
    return banded.reshape(taps_x, taps_y * depth, depth)


def conv_kernel(tile_x, src_ref, band_ref, image_ref, cover_ref, out_ref, cols_ref):
    rows_x, rows_y, depth = out_ref.shape
    taps_x = src_ref.shape[0] - rows_x + 1
    taps_y = src_ref.shape[1] - rows_y + 1
    for step_y in range(taps_y):
        cols_ref[:, :, step_y * depth : (step_y + 1) * depth] = src_ref[:, step_y : step_y + rows_y, :]
    keep = cover_ref[...] > 0
    for start in range(0, rows_x, tile_x):
        acc = None
        for shift_x in range(taps_x):
            lhs = cols_ref[start + shift_x : start + shift_x + tile_x].reshape(tile_x * rows_y, -1)
            part = jnp.dot(lhs, band_ref[shift_x], preferred_element_type=jnp.float32)
            acc = part if acc is None else acc + part
        blurred = acc.reshape(tile_x, rows_y, depth)
        ratio = image_ref[start : start + tile_x].astype(jnp.float32) / blurred
        out_ref[start : start + tile_x] = jnp.where(keep[None], ratio, 0.0).astype(out_ref.dtype)


def quotient_of(padded_part, banded, image, cover_plane):
    rows_x, rows_y, depth = image.shape
    vmem = pl.BlockSpec(memory_space=pltpu.VMEM)
    return pl.pallas_call(
        functools.partial(conv_kernel, 4),
        out_shape=jax.ShapeDtypeStruct((rows_x, rows_y, depth), jnp.bfloat16),
        in_specs=[vmem] * 4,
        out_specs=vmem,
        scratch_shapes=[pltpu.VMEM((padded_part.shape[0], rows_y, banded.shape[1]), jnp.bfloat16)],
    )(padded_part, banded, image, cover_plane)


def local(estimate, images, point_spread, covered):
    slab_x, width_y, depth = estimate.shape
    share_w = images.shape[2]
    view_count, taps_x, taps_y, taps_z = point_spread.shape
    rim_x, rim_y, rim_z = ((taps_x - 1) // 2, (taps_y - 1) // 2, (taps_z - 1) // 2)
    shares = width_y // share_w
    share_blocks = share_w // BY
    group = lax.axis_index("view")
    view_id = group // shares
    part = group % shares
    y_start = part * share_w
    source = estimate.astype(jnp.bfloat16)
    rimmed = with_halo(source, (("blk", 0),), rim_x)
    padded = jnp.pad(rimmed, ((0, 0), (rim_y, rim_y), (0, 0)))
    spread = lax.dynamic_index_in_dim(point_spread, view_id, 0, keepdims=False)
    kernel = (spread / jnp.sum(spread)).astype(jnp.bfloat16)
    forward = band_table(kernel, depth)
    backward = band_table(kernel[::-1, ::-1, ::-1], depth)
    coverage_row = lax.dynamic_index_in_dim(covered[:, 0, :], view_id, 0, keepdims=False) > 0
    share_cover = lax.dynamic_slice_in_dim(coverage_row, part * share_blocks, share_blocks)
    cell_cover = jnp.repeat(share_cover, BY)[None, :, None]
    image = images[0]
    region = lax.dynamic_slice(
        padded, (0, y_start, 0), (slab_x + 2 * rim_x, share_w + 2 * rim_y, depth)
    )
    cover_plane = jnp.broadcast_to(cell_cover[0].astype(jnp.float32), (share_w, depth))
    quotient = quotient_of(region, forward, image, cover_plane)
    rim_zeros = jnp.zeros((slab_x, rim_y, depth), jnp.bfloat16)
    edge_rows = jnp.where(part == 0, quotient[:, share_w - rim_y :, :], quotient[:, :rim_y, :])
    partner = swapped(edge_rows, "view", 0)
    lower_rim = jnp.where(part > 0, partner, rim_zeros)
    upper_rim = jnp.where(part < shares - 1, partner, rim_zeros)
    extended = jnp.concatenate([lower_rim, quotient, upper_rim], axis=1)
    return product_gather(extended, backward, cover_plane, estimate, shares, rim_x)


def solution(mesh):
    in_specs = (P("blk", None, None), P("view", "blk", None, None), P(), P(None, "blk", None))
    out_specs = P("blk", None, None)
    return jax.shard_map(local, mesh=mesh, in_specs=in_specs, out_specs=out_specs, check_vma=False)
```

```python
import functools

import jax
import jax.numpy as jnp
from jax import lax
from jax.experimental import pallas as pl
from jax.experimental.pallas import tpu as pltpu
from jax.sharding import PartitionSpec as P

BY = 32


def with_halo(cells, sides, width):
    for axis, dim in sides:
        count = lax.axis_size(axis)
        ends = count - 1
        head = lax.slice_in_dim(cells, 0, width, axis=dim)
        tail = lax.slice_in_dim(cells, cells.shape[dim] - width, cells.shape[dim], axis=dim)
        cells = jnp.concatenate(
            [
                lax.ppermute(tail, axis, [(i, (i + 1) % count) for i in range(ends)]),
                cells,
                lax.ppermute(head, axis, [((i + 1) % count, i) for i in range(ends)]),
            ],
            axis=dim,
        )
    return cells


def swapped(block, axis, stride):
    count = lax.axis_size(axis)
    route = []
    for low in range(count):
        high = low | 1 << stride
        if high != low and high < count:
            route += [(low, high), (high, low)]
    return lax.ppermute(block, axis, route)


def merged(part, axis, combine):
    gathered = lax.all_gather(part, axis)

    def take(source):
        return lax.dynamic_index_in_dim(gathered, source, 0, False)

    return lax.fori_loop(
        1, lax.axis_size(axis), lambda source, state: combine(state, take(source)), take(0)
    )


def product_kernel(
    n, shares, width, quot_ref, band_ref, cover_ref, out_ref, ext_ref, cols_ref, factor_ref,
    held, send1, recv1, send2, recv2, send_halo, recv_halo,
):
    groups = n // shares
    step, share_w, depth = held.shape[1:]
    taps_x = band_ref.shape[0]
    taps_y = quot_ref.shape[1] - share_w + 1
    rows = quot_ref.shape[0]
    me = lax.axis_index("view")
    view_id = me // shares
    part = me % shares
    layers = lax.axis_size("blk")
    layer = lax.axis_index("blk")
    up = (layer + 1) % layers
    down = (layer + layers - 1) % layers
    mesh_kind = pl.DeviceIdType.MESH
    barrier = pltpu.get_barrier_semaphore()
    for d in range(1, groups):
        pl.semaphore_signal(
            barrier, inc=1, device_id={"view": ((view_id + d) % groups) * shares + part},
            device_id_type=mesh_kind,
        )
    for d in range(1, shares):
        pl.semaphore_signal(
            barrier, inc=1, device_id={"view": view_id * shares + (part + d) % shares},
            device_id_type=mesh_kind,
        )
    has_up = layer < layers - 1
    has_down = layer > 0

    @pl.when(has_up)
    def _():
        pl.semaphore_signal(barrier, inc=1, device_id={"blk": up}, device_id_type=mesh_kind)

    @pl.when(has_down)
    def _():
        pl.semaphore_signal(barrier, inc=1, device_id={"blk": down}, device_id_type=mesh_kind)

    ext_ref[pl.ds(width, rows)] = quot_ref[...]

    def build_columns(first, count):
        for step_y in range(taps_y):
            cols_ref[pl.ds(first, count), :, step_y * depth : (step_y + 1) * depth] = ext_ref[
                pl.ds(first, count), step_y : step_y + share_w, :
            ]

    build_columns(width, rows)
    keep = cover_ref[...] > 0

    def factor_rows(target):
        acc = None
        for shift_x in range(taps_x):
            lhs = cols_ref[pl.ds(target * step + shift_x, step)].reshape(step * share_w, -1)
            part_sum = jnp.dot(lhs, band_ref[shift_x], preferred_element_type=jnp.float32)
            acc = part_sum if acc is None else acc + part_sum
        acc = acc.reshape(step, share_w, depth)
        factor_ref[pl.ds(target * step, step)] = jnp.where(keep[None], acc, 1.0)

    pl.semaphore_wait(
        barrier, groups + shares - 2 + has_up.astype(jnp.int32) + has_down.astype(jnp.int32)
    )
    to_up = pltpu.make_async_remote_copy(
        src_ref=quot_ref.at[pl.ds(rows - width, width)],
        dst_ref=ext_ref.at[pl.ds(0, width)],
        send_sem=send_halo.at[0],
        recv_sem=recv_halo.at[0],
        device_id={"blk": up},
        device_id_type=mesh_kind,
    )
    to_down = pltpu.make_async_remote_copy(
        src_ref=quot_ref.at[pl.ds(0, width)],
        dst_ref=ext_ref.at[pl.ds(rows + width, width)],
        send_sem=send_halo.at[1],
        recv_sem=recv_halo.at[1],
        device_id={"blk": down},
        device_id_type=mesh_kind,
    )
    @pl.when(has_up)
    def _():
        to_up.start()

    @pl.when(has_down)
    def _():
        to_down.start()

    reach = width // step
    inner = list(range(reach, groups - reach))
    outer = list(range(reach)) + list(range(groups - reach, groups))
    outgoing = []

    def send_chunk(target):
        factor_rows(target)
        copy = pltpu.make_async_remote_copy(
            src_ref=factor_ref.at[pl.ds(target * step, step)],
            dst_ref=held.at[view_id],
            send_sem=send1.at[target],
            recv_sem=recv1.at[view_id],
            device_id={"view": target * shares + part},
            device_id_type=mesh_kind,
        )

        @pl.when(target != view_id)
        def _():
            copy.start()

        outgoing.append((target, copy))

    for target in inner:
        send_chunk(target)
    @pl.when(has_up)
    def _():
        to_up.wait_send()
        to_down.wait_recv()

    @pl.when(has_down)
    def _():
        to_down.wait_send()
        to_up.wait_recv()

    @pl.when(layer == 0)
    def _():
        ext_ref[pl.ds(0, width)] = jnp.zeros((width,) + quot_ref.shape[1:], quot_ref.dtype)

    @pl.when(layer == layers - 1)
    def _():
        ext_ref[pl.ds(rows + width, width)] = jnp.zeros((width,) + quot_ref.shape[1:], quot_ref.dtype)

    build_columns(0, width)
    build_columns(rows + width, width)
    for target in outer:
        send_chunk(target)
    acc = factor_ref[pl.ds(view_id * step, step)]
    for d in range(1, groups):
        source = (view_id - d + groups) % groups
        pltpu.make_async_remote_copy(
            src_ref=factor_ref.at[pl.ds(0, step)],
            dst_ref=held.at[source],
            send_sem=send1.at[source],
            recv_sem=recv1.at[source],
            device_id={"view": source * shares + part},
            device_id_type=mesh_kind,
        ).wait_recv()
        acc = acc * held[source]
    for target, copy in outgoing:

        @pl.when(target != view_id)
        def _():
            copy.wait_send()

    mine = pl.ds(view_id * step, step)
    cols = pl.ds(part * share_w, share_w)
    out_ref[mine, cols, :] = acc
    outgoing = []
    for d in range(1, groups):
        target = (view_id + d) % groups
        copy = pltpu.make_async_remote_copy(
            src_ref=out_ref.at[mine, cols],
            dst_ref=out_ref.at[mine, cols],
            send_sem=send2.at[d],
            recv_sem=recv2.at[d],
            device_id={"view": target * shares + part},
            device_id_type=mesh_kind,
        )
        copy.start()
        outgoing.append(copy)
    for d in range(1, groups):
        source = (view_id - d + groups) % groups
        src_rows = pl.ds(source * step, step)
        pltpu.make_async_remote_copy(
            src_ref=out_ref.at[src_rows, cols],
            dst_ref=out_ref.at[src_rows, cols],
            send_sem=send2.at[d],
            recv_sem=recv2.at[d],
            device_id={"view": source * shares + part},
            device_id_type=mesh_kind,
        ).wait_recv()
    for copy in outgoing:
        copy.wait_send()
    outgoing = []
    for d in range(1, shares):
        other = (part + d) % shares
        copy = pltpu.make_async_remote_copy(
            src_ref=out_ref.at[:, cols],
            dst_ref=out_ref.at[:, cols],
            send_sem=send2.at[groups + d],
            recv_sem=recv2.at[groups + d],
            device_id={"view": view_id * shares + other},
            device_id_type=mesh_kind,
        )
        copy.start()
        outgoing.append(copy)
    for d in range(1, shares):
        other = (part - d + shares) % shares
        other_cols = pl.ds(other * share_w, share_w)
        pltpu.make_async_remote_copy(
            src_ref=out_ref.at[:, other_cols],
            dst_ref=out_ref.at[:, other_cols],
            send_sem=send2.at[groups + d],
            recv_sem=recv2.at[groups + d],
            device_id={"view": view_id * shares + other},
            device_id_type=mesh_kind,
        ).wait_recv()
    for copy in outgoing:
        copy.wait_send()


def product_gather(extended, banded, cover_plane, estimate, shares, width):
    n = lax.axis_size("view")
    groups = n // shares
    slab_x, width_y, depth = estimate.shape
    share_w = cover_plane.shape[0]
    step = slab_x // groups
    padded_rows = extended.shape[0] + 2 * width
    vmem = pl.BlockSpec(memory_space=pltpu.VMEM)
    return pl.pallas_call(
        functools.partial(product_kernel, n, shares, width),
        out_shape=jax.ShapeDtypeStruct(estimate.shape, jnp.float32),
        in_specs=[vmem] * 3,
        out_specs=vmem,
        scratch_shapes=[
            pltpu.VMEM((padded_rows,) + extended.shape[1:], extended.dtype),
            pltpu.VMEM((padded_rows, share_w, banded.shape[1]), jnp.bfloat16),
            pltpu.VMEM((slab_x, share_w, depth), jnp.float32),
            pltpu.VMEM((groups, step, share_w, depth), jnp.float32),
            pltpu.SemaphoreType.DMA((groups,)),
            pltpu.SemaphoreType.DMA((groups,)),
            pltpu.SemaphoreType.DMA((groups + shares,)),
            pltpu.SemaphoreType.DMA((groups + shares,)),
            pltpu.SemaphoreType.DMA((2,)),
            pltpu.SemaphoreType.DMA((2,)),
        ],
        compiler_params=pltpu.CompilerParams(collective_id=0, has_side_effects=True),
    )(extended, banded, cover_plane)


def band_table(kernel, depth):
    taps_x, taps_y, taps_z = kernel.shape
    rim_z = (taps_z - 1) // 2
    shape_three = (taps_z, depth, depth)
    offset = lax.broadcasted_iota(jnp.int32, shape_three, 1) - lax.broadcasted_iota(
        jnp.int32, shape_three, 2
    )
    onehot = (offset + rim_z == lax.broadcasted_iota(jnp.int32, shape_three, 0)).astype(
        jnp.bfloat16
    )
    banded = jnp.einsum("abt,tpz->abpz", kernel, onehot, preferred_element_type=jnp.float32).astype(
        jnp.bfloat16
    )
    return banded.reshape(taps_x, taps_y * depth, depth)


def conv_kernel(tile_x, src_ref, band_ref, image_ref, cover_ref, out_ref, cols_ref):
    rows_x, rows_y, depth = out_ref.shape
    taps_x = src_ref.shape[0] - rows_x + 1
    taps_y = src_ref.shape[1] - rows_y + 1
    for step_y in range(taps_y):
        cols_ref[:, :, step_y * depth : (step_y + 1) * depth] = src_ref[:, step_y : step_y + rows_y, :]
    keep = cover_ref[...] > 0
    for start in range(0, rows_x, tile_x):
        acc = None
        for shift_x in range(taps_x):
            lhs = cols_ref[start + shift_x : start + shift_x + tile_x].reshape(tile_x * rows_y, -1)
            part = jnp.dot(lhs, band_ref[shift_x], preferred_element_type=jnp.float32)
            acc = part if acc is None else acc + part
        blurred = acc.reshape(tile_x, rows_y, depth)
        ratio = image_ref[start : start + tile_x].astype(jnp.float32) / blurred
        out_ref[start : start + tile_x] = jnp.where(keep[None], ratio, 0.0).astype(out_ref.dtype)


def quotient_of(padded_part, banded, image, cover_plane):
    rows_x, rows_y, depth = image.shape
    vmem = pl.BlockSpec(memory_space=pltpu.VMEM)
    return pl.pallas_call(
        functools.partial(conv_kernel, 4),
        out_shape=jax.ShapeDtypeStruct((rows_x, rows_y, depth), jnp.bfloat16),
        in_specs=[vmem] * 4,
        out_specs=vmem,
        scratch_shapes=[pltpu.VMEM((padded_part.shape[0], rows_y, banded.shape[1]), jnp.bfloat16)],
    )(padded_part, banded, image, cover_plane)


def local(estimate, images, point_spread, covered):
    slab_x, width_y, depth = estimate.shape
    share_w = images.shape[2]
    view_count, taps_x, taps_y, taps_z = point_spread.shape
    rim_x, rim_y, rim_z = ((taps_x - 1) // 2, (taps_y - 1) // 2, (taps_z - 1) // 2)
    shares = width_y // share_w
    share_blocks = share_w // BY
    group = lax.axis_index("view")
    view_id = group // shares
    part = group % shares
    y_start = part * share_w
    source = estimate.astype(jnp.bfloat16)
    rimmed = with_halo(source, (("blk", 0),), rim_x)
    padded = jnp.pad(rimmed, ((0, 0), (rim_y, rim_y), (0, 0)))
    spread = lax.dynamic_index_in_dim(point_spread, view_id, 0, keepdims=False)
    kernel = (spread / jnp.sum(spread)).astype(jnp.bfloat16)
    forward = band_table(kernel, depth)
    backward = band_table(kernel[::-1, ::-1, ::-1], depth)
    coverage_row = lax.dynamic_index_in_dim(covered[:, 0, :], view_id, 0, keepdims=False) > 0
    share_cover = lax.dynamic_slice_in_dim(coverage_row, part * share_blocks, share_blocks)
    cell_cover = jnp.repeat(share_cover, BY)[None, :, None]
    image = images[0]
    region = lax.dynamic_slice(
        padded, (0, y_start, 0), (slab_x + 2 * rim_x, share_w + 2 * rim_y, depth)
    )
    cover_plane = jnp.broadcast_to(cell_cover[0].astype(jnp.float32), (share_w, depth))
    quotient = quotient_of(region, forward, image, cover_plane)
    rim_zeros = jnp.zeros((slab_x, rim_y, depth), jnp.bfloat16)
    edge_rows = jnp.where(part == 0, quotient[:, share_w - rim_y :, :], quotient[:, :rim_y, :])
    partner = swapped(edge_rows, "view", 0)
    lower_rim = jnp.where(part > 0, partner, rim_zeros)
    upper_rim = jnp.where(part < shares - 1, partner, rim_zeros)
    extended = jnp.concatenate([lower_rim, quotient, upper_rim], axis=1)
    return estimate * product_gather(extended, backward, cover_plane, estimate, shares, rim_x)


def solution(mesh):
    in_specs = (P("blk", None, None), P("view", "blk", None, None), P(), P(None, "blk", None))
    out_specs = P("blk", None, None)
    return jax.shard_map(local, mesh=mesh, in_specs=in_specs, out_specs=out_specs, check_vma=False)
```

```python
import functools

import jax
import jax.numpy as jnp
from jax import lax
from jax.experimental import pallas as pl
from jax.experimental.pallas import tpu as pltpu
from jax.sharding import PartitionSpec as P

BY = 32


def with_halo(cells, sides, width):
    for axis, dim in sides:
        count = lax.axis_size(axis)
        ends = count - 1
        head = lax.slice_in_dim(cells, 0, width, axis=dim)
        tail = lax.slice_in_dim(cells, cells.shape[dim] - width, cells.shape[dim], axis=dim)
        cells = jnp.concatenate(
            [
                lax.ppermute(tail, axis, [(i, (i + 1) % count) for i in range(ends)]),
                cells,
                lax.ppermute(head, axis, [((i + 1) % count, i) for i in range(ends)]),
            ],
            axis=dim,
        )
    return cells


def swapped(block, axis, stride):
    count = lax.axis_size(axis)
    route = []
    for low in range(count):
        high = low | 1 << stride
        if high != low and high < count:
            route += [(low, high), (high, low)]
    return lax.ppermute(block, axis, route)


def merged(part, axis, combine):
    gathered = lax.all_gather(part, axis)

    def take(source):
        return lax.dynamic_index_in_dim(gathered, source, 0, False)

    return lax.fori_loop(
        1, lax.axis_size(axis), lambda source, state: combine(state, take(source)), take(0)
    )


def product_kernel(
    n, shares, width, quot_ref, band_ref, cover_ref, out_ref, ext_ref, cols_ref, factor_ref,
    held, send1, recv1, send2, recv2, send_halo, recv_halo,
):
    groups = n // shares
    step, share_w, depth = held.shape[1:]
    taps_x = band_ref.shape[0]
    taps_y = quot_ref.shape[1] - share_w + 1
    rows = quot_ref.shape[0]
    me = lax.axis_index("view")
    view_id = me // shares
    part = me % shares
    layers = lax.axis_size("blk")
    layer = lax.axis_index("blk")
    up = (layer + 1) % layers
    down = (layer + layers - 1) % layers
    mesh_kind = pl.DeviceIdType.MESH
    barrier = pltpu.get_barrier_semaphore()
    for d in range(1, groups):
        pl.semaphore_signal(
            barrier, inc=1, device_id={"view": ((view_id + d) % groups) * shares + part},
            device_id_type=mesh_kind,
        )
    for d in range(1, shares):
        pl.semaphore_signal(
            barrier, inc=1, device_id={"view": view_id * shares + (part + d) % shares},
            device_id_type=mesh_kind,
        )
    has_up = layer < layers - 1
    has_down = layer > 0

    @pl.when(has_up)
    def _():
        pl.semaphore_signal(barrier, inc=1, device_id={"blk": up}, device_id_type=mesh_kind)

    @pl.when(has_down)
    def _():
        pl.semaphore_signal(barrier, inc=1, device_id={"blk": down}, device_id_type=mesh_kind)

    ext_ref[pl.ds(width, rows)] = quot_ref[...]

    def build_columns(first, count):
        for step_y in range(taps_y):
            cols_ref[pl.ds(first, count), :, step_y * depth : (step_y + 1) * depth] = ext_ref[
                pl.ds(first, count), step_y : step_y + share_w, :
            ]

    build_columns(width, rows)
    keep = cover_ref[...] > 0

    def factor_rows(target):
        acc = None
        for shift_x in range(taps_x):
            lhs = cols_ref[pl.ds(target * step + shift_x, step)].reshape(step * share_w, -1)
            part_sum = jnp.dot(lhs, band_ref[shift_x], preferred_element_type=jnp.float32)
            acc = part_sum if acc is None else acc + part_sum
        acc = acc.reshape(step, share_w, depth)
        factor_ref[pl.ds(target * step, step)] = jnp.where(keep[None], acc, 1.0)

    pl.semaphore_wait(
        barrier, groups + shares - 2 + has_up.astype(jnp.int32) + has_down.astype(jnp.int32)
    )
    to_up = pltpu.make_async_remote_copy(
        src_ref=quot_ref.at[pl.ds(rows - width, width)],
        dst_ref=ext_ref.at[pl.ds(0, width)],
        send_sem=send_halo.at[0],
        recv_sem=recv_halo.at[0],
        device_id={"blk": up},
        device_id_type=mesh_kind,
    )
    to_down = pltpu.make_async_remote_copy(
        src_ref=quot_ref.at[pl.ds(0, width)],
        dst_ref=ext_ref.at[pl.ds(rows + width, width)],
        send_sem=send_halo.at[1],
        recv_sem=recv_halo.at[1],
        device_id={"blk": down},
        device_id_type=mesh_kind,
    )
    @pl.when(has_up)
    def _():
        to_up.start()

    @pl.when(has_down)
    def _():
        to_down.start()

    reach = width // step
    inner = list(range(reach, groups - reach))
    outer = list(range(reach)) + list(range(groups - reach, groups))
    outgoing = []

    def send_chunk(target):
        factor_rows(target)
        copy = pltpu.make_async_remote_copy(
            src_ref=factor_ref.at[pl.ds(target * step, step)],
            dst_ref=held.at[view_id],
            send_sem=send1.at[target],
            recv_sem=recv1.at[view_id],
            device_id={"view": target * shares + part},
            device_id_type=mesh_kind,
        )

        @pl.when(target != view_id)
        def _():
            copy.start()

        outgoing.append((target, copy))

    for target in inner:
        send_chunk(target)
    @pl.when(has_up)
    def _():
        to_up.wait_send()
        to_down.wait_recv()

    @pl.when(has_down)
    def _():
        to_down.wait_send()
        to_up.wait_recv()

    @pl.when(layer == 0)
    def _():
        ext_ref[pl.ds(0, width)] = jnp.zeros((width,) + quot_ref.shape[1:], quot_ref.dtype)

    @pl.when(layer == layers - 1)
    def _():
        ext_ref[pl.ds(rows + width, width)] = jnp.zeros((width,) + quot_ref.shape[1:], quot_ref.dtype)

    build_columns(0, width)
    build_columns(rows + width, width)
    for target in outer:
        send_chunk(target)
    acc = factor_ref[pl.ds(view_id * step, step)]
    for d in range(1, groups):
        source = (view_id - d + groups) % groups
        pltpu.make_async_remote_copy(
            src_ref=factor_ref.at[pl.ds(0, step)],
            dst_ref=held.at[source],
            send_sem=send1.at[source],
            recv_sem=recv1.at[source],
            device_id={"view": source * shares + part},
            device_id_type=mesh_kind,
        ).wait_recv()
        acc = acc * held[source]
    for target, copy in outgoing:

        @pl.when(target != view_id)
        def _():
            copy.wait_send()

    mine = pl.ds(view_id * step, step)
    cols = pl.ds(part * share_w, share_w)
    out_ref[mine, cols, :] = acc
    outgoing = []
    for d in range(1, groups):
        target = (view_id + d) % groups
        copy = pltpu.make_async_remote_copy(
            src_ref=out_ref.at[mine, cols],
            dst_ref=out_ref.at[mine, cols],
            send_sem=send2.at[d],
            recv_sem=recv2.at[d],
            device_id={"view": target * shares + part},
            device_id_type=mesh_kind,
        )
        copy.start()
        outgoing.append(copy)
    for d in range(1, groups):
        source = (view_id - d + groups) % groups
        src_rows = pl.ds(source * step, step)
        pltpu.make_async_remote_copy(
            src_ref=out_ref.at[src_rows, cols],
            dst_ref=out_ref.at[src_rows, cols],
            send_sem=send2.at[d],
            recv_sem=recv2.at[d],
            device_id={"view": source * shares + part},
            device_id_type=mesh_kind,
        ).wait_recv()
    for copy in outgoing:
        copy.wait_send()
    outgoing = []
    for d in range(1, shares):
        other = (part + d) % shares
        copy = pltpu.make_async_remote_copy(
            src_ref=out_ref.at[:, cols],
            dst_ref=out_ref.at[:, cols],
            send_sem=send2.at[groups + d],
            recv_sem=recv2.at[groups + d],
            device_id={"view": view_id * shares + other},
            device_id_type=mesh_kind,
        )
        copy.start()
        outgoing.append(copy)
    for d in range(1, shares):
        other = (part - d + shares) % shares
        other_cols = pl.ds(other * share_w, share_w)
        pltpu.make_async_remote_copy(
            src_ref=out_ref.at[:, other_cols],
            dst_ref=out_ref.at[:, other_cols],
            send_sem=send2.at[groups + d],
            recv_sem=recv2.at[groups + d],
            device_id={"view": view_id * shares + other},
            device_id_type=mesh_kind,
        ).wait_recv()
    for copy in outgoing:
        copy.wait_send()


def product_gather(extended, banded, cover_plane, estimate, shares, width):
    n = lax.axis_size("view")
    groups = n // shares
    slab_x, width_y, depth = estimate.shape
    share_w = cover_plane.shape[0]
    step = slab_x // groups
    padded_rows = extended.shape[0] + 2 * width
    vmem = pl.BlockSpec(memory_space=pltpu.VMEM)
    return pl.pallas_call(
        functools.partial(product_kernel, n, shares, width),
        out_shape=jax.ShapeDtypeStruct(estimate.shape, jnp.float32),
        in_specs=[vmem] * 3,
        out_specs=vmem,
        scratch_shapes=[
            pltpu.VMEM((padded_rows,) + extended.shape[1:], extended.dtype),
            pltpu.VMEM((padded_rows, share_w, banded.shape[1]), jnp.bfloat16),
            pltpu.VMEM((slab_x, share_w, depth), jnp.float32),
            pltpu.VMEM((groups, step, share_w, depth), jnp.float32),
            pltpu.SemaphoreType.DMA((groups,)),
            pltpu.SemaphoreType.DMA((groups,)),
            pltpu.SemaphoreType.DMA((groups + shares,)),
            pltpu.SemaphoreType.DMA((groups + shares,)),
            pltpu.SemaphoreType.DMA((2,)),
            pltpu.SemaphoreType.DMA((2,)),
        ],
        compiler_params=pltpu.CompilerParams(collective_id=0, has_side_effects=True),
    )(extended, banded, cover_plane)


def band_table(kernel, depth):
    taps_x, taps_y, taps_z = kernel.shape
    rim_z = (taps_z - 1) // 2
    shape_three = (taps_z, depth, depth)
    offset = lax.broadcasted_iota(jnp.int32, shape_three, 1) - lax.broadcasted_iota(
        jnp.int32, shape_three, 2
    )
    onehot = (offset + rim_z == lax.broadcasted_iota(jnp.int32, shape_three, 0)).astype(
        jnp.bfloat16
    )
    banded = jnp.einsum("abt,tpz->abpz", kernel, onehot, preferred_element_type=jnp.float32).astype(
        jnp.bfloat16
    )
    return banded.reshape(taps_x, taps_y * depth, depth)


def conv_kernel(tile_x, src_ref, band_ref, image_ref, cover_ref, out_ref, cols_ref):
    rows_x, rows_y, depth = out_ref.shape
    taps_x = src_ref.shape[0] - rows_x + 1
    taps_y = src_ref.shape[1] - rows_y + 1
    for step_y in range(taps_y):
        cols_ref[:, :, step_y * depth : (step_y + 1) * depth] = src_ref[:, step_y : step_y + rows_y, :]
    keep = cover_ref[...] > 0
    for start in range(0, rows_x, tile_x):
        acc = None
        for shift_x in range(taps_x):
            lhs = cols_ref[start + shift_x : start + shift_x + tile_x].reshape(tile_x * rows_y, -1)
            part = jnp.dot(lhs, band_ref[shift_x], preferred_element_type=jnp.float32)
            acc = part if acc is None else acc + part
        blurred = acc.reshape(tile_x, rows_y, depth)
        ratio = image_ref[start : start + tile_x].astype(jnp.float32) / blurred
        out_ref[start : start + tile_x] = jnp.where(keep[None], ratio, 0.0).astype(out_ref.dtype)


def quotient_of(padded_part, banded, image, cover_plane):
    rows_x, rows_y, depth = image.shape
    vmem = pl.BlockSpec(memory_space=pltpu.VMEM)
    return pl.pallas_call(
        functools.partial(conv_kernel, 4),
        out_shape=jax.ShapeDtypeStruct((rows_x, rows_y, depth), jnp.bfloat16),
        in_specs=[vmem] * 4,
        out_specs=vmem,
        scratch_shapes=[pltpu.VMEM((padded_part.shape[0], rows_y, banded.shape[1]), jnp.bfloat16)],
    )(padded_part, banded, image, cover_plane)


def local(estimate, images, point_spread, covered):
    slab_x, width_y, depth = estimate.shape
    share_w = images.shape[2]
    view_count, taps_x, taps_y, taps_z = point_spread.shape
    rim_x, rim_y, rim_z = ((taps_x - 1) // 2, (taps_y - 1) // 2, (taps_z - 1) // 2)
    shares = width_y // share_w
    share_blocks = share_w // BY
    group = lax.axis_index("view")
    view_id = group // shares
    part = group % shares
    y_start = part * share_w
    source = estimate.astype(jnp.bfloat16)
    padded = jnp.pad(source, ((0, 0), (rim_y, rim_y), (0, 0)))
    spread = lax.dynamic_index_in_dim(point_spread, view_id, 0, keepdims=False)
    kernel = (spread / jnp.sum(spread)).astype(jnp.bfloat16)
    forward = band_table(kernel, depth)
    backward = band_table(kernel[::-1, ::-1, ::-1], depth)
    coverage_row = lax.dynamic_index_in_dim(covered[:, 0, :], view_id, 0, keepdims=False) > 0
    share_cover = lax.dynamic_slice_in_dim(coverage_row, part * share_blocks, share_blocks)
    cell_cover = jnp.repeat(share_cover, BY)[None, :, None]
    image = images[0]
    local_region = lax.dynamic_slice(padded, (0, y_start, 0), (slab_x, share_w + 2 * rim_y, depth))
    region = with_halo(local_region, (("blk", 0),), rim_x)
    cover_plane = jnp.broadcast_to(cell_cover[0].astype(jnp.float32), (share_w, depth))
    quotient = quotient_of(region, forward, image, cover_plane)
    rim_zeros = jnp.zeros((slab_x, rim_y, depth), jnp.bfloat16)
    edge_rows = jnp.where(part == 0, quotient[:, share_w - rim_y :, :], quotient[:, :rim_y, :])
    partner = swapped(edge_rows, "view", 0)
    lower_rim = jnp.where(part > 0, partner, rim_zeros)
    upper_rim = jnp.where(part < shares - 1, partner, rim_zeros)
    extended = jnp.concatenate([lower_rim, quotient, upper_rim], axis=1)
    return estimate * product_gather(extended, backward, cover_plane, estimate, shares, rim_x)


def solution(mesh):
    in_specs = (P("blk", None, None), P("view", "blk", None, None), P(), P(None, "blk", None))
    out_specs = P("blk", None, None)
    return jax.shard_map(local, mesh=mesh, in_specs=in_specs, out_specs=out_specs, check_vma=False)
```

```python
import functools

import jax
import jax.numpy as jnp
from jax import lax
from jax.experimental import pallas as pl
from jax.experimental.pallas import tpu as pltpu
from jax.sharding import PartitionSpec as P

BY = 32


def with_halo(cells, sides, width):
    for axis, dim in sides:
        count = lax.axis_size(axis)
        ends = count - 1
        head = lax.slice_in_dim(cells, 0, width, axis=dim)
        tail = lax.slice_in_dim(cells, cells.shape[dim] - width, cells.shape[dim], axis=dim)
        cells = jnp.concatenate(
            [
                lax.ppermute(tail, axis, [(i, (i + 1) % count) for i in range(ends)]),
                cells,
                lax.ppermute(head, axis, [((i + 1) % count, i) for i in range(ends)]),
            ],
            axis=dim,
        )
    return cells


def swapped(block, axis, stride):
    count = lax.axis_size(axis)
    route = []
    for low in range(count):
        high = low | 1 << stride
        if high != low and high < count:
            route += [(low, high), (high, low)]
    return lax.ppermute(block, axis, route)


def merged(part, axis, combine):
    gathered = lax.all_gather(part, axis)

    def take(source):
        return lax.dynamic_index_in_dim(gathered, source, 0, False)

    return lax.fori_loop(
        1, lax.axis_size(axis), lambda source, state: combine(state, take(source)), take(0)
    )


def product_kernel(
    n, shares, width, quot_ref, band_ref, cover_ref, out_ref, ext_ref, cols_ref, factor_ref,
    held, send1, recv1, send2, recv2, send_halo, recv_halo,
):
    groups = n // shares
    step, share_w, depth = held.shape[1:]
    taps_x = band_ref.shape[0]
    taps_y = quot_ref.shape[1] - share_w + 1
    rows = quot_ref.shape[0]
    me = lax.axis_index("view")
    view_id = me // shares
    part = me % shares
    layers = lax.axis_size("blk")
    layer = lax.axis_index("blk")
    up = (layer + 1) % layers
    down = (layer + layers - 1) % layers
    mesh_kind = pl.DeviceIdType.MESH
    barrier = pltpu.get_barrier_semaphore()
    for d in range(1, groups):
        pl.semaphore_signal(
            barrier, inc=1, device_id={"view": ((view_id + d) % groups) * shares + part},
            device_id_type=mesh_kind,
        )
    for d in range(1, shares):
        pl.semaphore_signal(
            barrier, inc=1, device_id={"view": view_id * shares + (part + d) % shares},
            device_id_type=mesh_kind,
        )
    has_up = layer < layers - 1
    has_down = layer > 0

    @pl.when(has_up)
    def _():
        pl.semaphore_signal(barrier, inc=1, device_id={"blk": up}, device_id_type=mesh_kind)

    @pl.when(has_down)
    def _():
        pl.semaphore_signal(barrier, inc=1, device_id={"blk": down}, device_id_type=mesh_kind)

    ext_ref[pl.ds(width, rows)] = quot_ref[...]

    def build_columns(first, count):
        for step_y in range(taps_y):
            cols_ref[pl.ds(first, count), :, step_y * depth : (step_y + 1) * depth] = ext_ref[
                pl.ds(first, count), step_y : step_y + share_w, :
            ]

    build_columns(width, rows)
    keep = cover_ref[...] > 0

    def factor_rows(target):
        acc = None
        for shift_x in range(taps_x):
            lhs = cols_ref[pl.ds(target * step + shift_x, step)].reshape(step * share_w, -1)
            part_sum = jnp.dot(lhs, band_ref[shift_x], preferred_element_type=jnp.float32)
            acc = part_sum if acc is None else acc + part_sum
        acc = acc.reshape(step, share_w, depth)
        factor_ref[pl.ds(target * step, step)] = jnp.where(keep[None], acc, 1.0)

    pl.semaphore_wait(
        barrier, groups + shares - 2 + has_up.astype(jnp.int32) + has_down.astype(jnp.int32)
    )
    to_up = pltpu.make_async_remote_copy(
        src_ref=quot_ref.at[pl.ds(rows - width, width)],
        dst_ref=ext_ref.at[pl.ds(0, width)],
        send_sem=send_halo.at[0],
        recv_sem=recv_halo.at[0],
        device_id={"blk": up},
        device_id_type=mesh_kind,
    )
    to_down = pltpu.make_async_remote_copy(
        src_ref=quot_ref.at[pl.ds(0, width)],
        dst_ref=ext_ref.at[pl.ds(rows + width, width)],
        send_sem=send_halo.at[1],
        recv_sem=recv_halo.at[1],
        device_id={"blk": down},
        device_id_type=mesh_kind,
    )
    @pl.when(has_up)
    def _():
        to_up.start()

    @pl.when(has_down)
    def _():
        to_down.start()

    reach = width // step
    inner = list(range(reach, groups - reach))
    outer = list(range(reach)) + list(range(groups - reach, groups))
    outgoing = []

    def send_chunk(target):
        factor_rows(target)
        copy = pltpu.make_async_remote_copy(
            src_ref=factor_ref.at[pl.ds(target * step, step)],
            dst_ref=held.at[view_id],
            send_sem=send1.at[target],
            recv_sem=recv1.at[view_id],
            device_id={"view": target * shares + part},
            device_id_type=mesh_kind,
        )

        @pl.when(target != view_id)
        def _():
            copy.start()

        outgoing.append((target, copy))

    for target in inner:
        send_chunk(target)
    @pl.when(has_up)
    def _():
        to_up.wait_send()
        to_down.wait_recv()

    @pl.when(has_down)
    def _():
        to_down.wait_send()
        to_up.wait_recv()

    @pl.when(layer == 0)
    def _():
        ext_ref[pl.ds(0, width)] = jnp.zeros((width,) + quot_ref.shape[1:], quot_ref.dtype)

    @pl.when(layer == layers - 1)
    def _():
        ext_ref[pl.ds(rows + width, width)] = jnp.zeros((width,) + quot_ref.shape[1:], quot_ref.dtype)

    build_columns(0, width)
    build_columns(rows + width, width)
    for target in outer:
        send_chunk(target)
    acc = factor_ref[pl.ds(view_id * step, step)]
    for d in range(1, groups):
        source = (view_id - d + groups) % groups
        pltpu.make_async_remote_copy(
            src_ref=factor_ref.at[pl.ds(0, step)],
            dst_ref=held.at[source],
            send_sem=send1.at[source],
            recv_sem=recv1.at[source],
            device_id={"view": source * shares + part},
            device_id_type=mesh_kind,
        ).wait_recv()
        acc = acc * held[source]
    for target, copy in outgoing:

        @pl.when(target != view_id)
        def _():
            copy.wait_send()

    mine = pl.ds(view_id * step, step)
    cols = pl.ds(part * share_w, share_w)
    out_ref[mine, cols, :] = acc
    outgoing = []
    for d in range(1, groups):
        target = (view_id + d) % groups
        copy = pltpu.make_async_remote_copy(
            src_ref=out_ref.at[mine, cols],
            dst_ref=out_ref.at[mine, cols],
            send_sem=send2.at[d],
            recv_sem=recv2.at[d],
            device_id={"view": target * shares + part},
            device_id_type=mesh_kind,
        )
        copy.start()
        outgoing.append(copy)
    for d in range(1, groups):
        source = (view_id - d + groups) % groups
        src_rows = pl.ds(source * step, step)
        pltpu.make_async_remote_copy(
            src_ref=out_ref.at[src_rows, cols],
            dst_ref=out_ref.at[src_rows, cols],
            send_sem=send2.at[d],
            recv_sem=recv2.at[d],
            device_id={"view": source * shares + part},
            device_id_type=mesh_kind,
        ).wait_recv()
    for copy in outgoing:
        copy.wait_send()
    outgoing = []
    for d in range(1, shares):
        other = (part + d) % shares
        copy = pltpu.make_async_remote_copy(
            src_ref=out_ref.at[:, cols],
            dst_ref=out_ref.at[:, cols],
            send_sem=send2.at[groups + d],
            recv_sem=recv2.at[groups + d],
            device_id={"view": view_id * shares + other},
            device_id_type=mesh_kind,
        )
        copy.start()
        outgoing.append(copy)
    for d in range(1, shares):
        other = (part - d + shares) % shares
        other_cols = pl.ds(other * share_w, share_w)
        pltpu.make_async_remote_copy(
            src_ref=out_ref.at[:, other_cols],
            dst_ref=out_ref.at[:, other_cols],
            send_sem=send2.at[groups + d],
            recv_sem=recv2.at[groups + d],
            device_id={"view": view_id * shares + other},
            device_id_type=mesh_kind,
        ).wait_recv()
    for copy in outgoing:
        copy.wait_send()


def product_gather(extended, banded, cover_plane, estimate, shares, width):
    n = lax.axis_size("view")
    groups = n // shares
    slab_x, width_y, depth = estimate.shape
    share_w = cover_plane.shape[0]
    step = slab_x // groups
    padded_rows = extended.shape[0] + 2 * width
    vmem = pl.BlockSpec(memory_space=pltpu.VMEM)
    return pl.pallas_call(
        functools.partial(product_kernel, n, shares, width),
        out_shape=jax.ShapeDtypeStruct(estimate.shape, jnp.float32),
        in_specs=[vmem] * 3,
        out_specs=vmem,
        scratch_shapes=[
            pltpu.VMEM((padded_rows,) + extended.shape[1:], extended.dtype),
            pltpu.VMEM((padded_rows, share_w, banded.shape[1]), jnp.bfloat16),
            pltpu.VMEM((slab_x, share_w, depth), jnp.float32),
            pltpu.VMEM((groups, step, share_w, depth), jnp.float32),
            pltpu.SemaphoreType.DMA((groups,)),
            pltpu.SemaphoreType.DMA((groups,)),
            pltpu.SemaphoreType.DMA((groups + shares,)),
            pltpu.SemaphoreType.DMA((groups + shares,)),
            pltpu.SemaphoreType.DMA((2,)),
            pltpu.SemaphoreType.DMA((2,)),
        ],
        compiler_params=pltpu.CompilerParams(collective_id=0, has_side_effects=True),
    )(extended, banded, cover_plane)


def band_table(kernel, depth):
    taps_x, taps_y, taps_z = kernel.shape
    rim_z = (taps_z - 1) // 2
    shape_three = (taps_z, depth, depth)
    offset = lax.broadcasted_iota(jnp.int32, shape_three, 1) - lax.broadcasted_iota(
        jnp.int32, shape_three, 2
    )
    onehot = (offset + rim_z == lax.broadcasted_iota(jnp.int32, shape_three, 0)).astype(
        jnp.bfloat16
    )
    banded = jnp.dot(
        kernel.reshape(taps_x * taps_y, taps_z),
        onehot.reshape(taps_z, depth * depth),
        preferred_element_type=jnp.float32,
    ).astype(jnp.bfloat16)
    return banded.reshape(taps_x, taps_y * depth, depth)


def conv_kernel(tile_x, src_ref, band_ref, image_ref, cover_ref, out_ref, cols_ref):
    rows_x, rows_y, depth = out_ref.shape
    taps_x = src_ref.shape[0] - rows_x + 1
    taps_y = src_ref.shape[1] - rows_y + 1
    for step_y in range(taps_y):
        cols_ref[:, :, step_y * depth : (step_y + 1) * depth] = src_ref[:, step_y : step_y + rows_y, :]
    keep = cover_ref[...] > 0
    for start in range(0, rows_x, tile_x):
        acc = None
        for shift_x in range(taps_x):
            lhs = cols_ref[start + shift_x : start + shift_x + tile_x].reshape(tile_x * rows_y, -1)
            part = jnp.dot(lhs, band_ref[shift_x], preferred_element_type=jnp.float32)
            acc = part if acc is None else acc + part
        blurred = acc.reshape(tile_x, rows_y, depth)
        ratio = image_ref[start : start + tile_x].astype(jnp.float32) / blurred
        out_ref[start : start + tile_x] = jnp.where(keep[None], ratio, 0.0).astype(out_ref.dtype)


def quotient_of(padded_part, banded, image, cover_plane):
    rows_x, rows_y, depth = image.shape
    vmem = pl.BlockSpec(memory_space=pltpu.VMEM)
    return pl.pallas_call(
        functools.partial(conv_kernel, 4),
        out_shape=jax.ShapeDtypeStruct((rows_x, rows_y, depth), jnp.bfloat16),
        in_specs=[vmem] * 4,
        out_specs=vmem,
        scratch_shapes=[pltpu.VMEM((padded_part.shape[0], rows_y, banded.shape[1]), jnp.bfloat16)],
    )(padded_part, banded, image, cover_plane)


def local(estimate, images, point_spread, covered):
    slab_x, width_y, depth = estimate.shape
    share_w = images.shape[2]
    view_count, taps_x, taps_y, taps_z = point_spread.shape
    rim_x, rim_y, rim_z = ((taps_x - 1) // 2, (taps_y - 1) // 2, (taps_z - 1) // 2)
    shares = width_y // share_w
    share_blocks = share_w // BY
    group = lax.axis_index("view")
    view_id = group // shares
    part = group % shares
    y_start = part * share_w
    source = estimate.astype(jnp.bfloat16)
    rimmed = with_halo(source, (("blk", 0),), rim_x)
    padded = jnp.pad(rimmed, ((0, 0), (rim_y, rim_y), (0, 0)))
    spread = lax.dynamic_index_in_dim(point_spread, view_id, 0, keepdims=False)
    kernel = (spread / jnp.sum(spread)).astype(jnp.bfloat16)
    forward = band_table(kernel, depth)
    backward = band_table(kernel[::-1, ::-1, ::-1], depth)
    coverage_row = lax.dynamic_index_in_dim(covered[:, 0, :], view_id, 0, keepdims=False) > 0
    share_cover = lax.dynamic_slice_in_dim(coverage_row, part * share_blocks, share_blocks)
    cell_cover = jnp.repeat(share_cover, BY)[None, :, None]
    image = images[0]
    region = lax.dynamic_slice(
        padded, (0, y_start, 0), (slab_x + 2 * rim_x, share_w + 2 * rim_y, depth)
    )
    cover_plane = jnp.broadcast_to(cell_cover[0].astype(jnp.float32), (share_w, depth))
    quotient = quotient_of(region, forward, image, cover_plane)
    rim_zeros = jnp.zeros((slab_x, rim_y, depth), jnp.bfloat16)
    edge_rows = jnp.where(part == 0, quotient[:, share_w - rim_y :, :], quotient[:, :rim_y, :])
    partner = swapped(edge_rows, "view", 0)
    lower_rim = jnp.where(part > 0, partner, rim_zeros)
    upper_rim = jnp.where(part < shares - 1, partner, rim_zeros)
    extended = jnp.concatenate([lower_rim, quotient, upper_rim], axis=1)
    return estimate * product_gather(extended, backward, cover_plane, estimate, shares, rim_x)


def solution(mesh):
    in_specs = (P("blk", None, None), P("view", "blk", None, None), P(), P(None, "blk", None))
    out_specs = P("blk", None, None)
    return jax.shard_map(local, mesh=mesh, in_specs=in_specs, out_specs=out_specs, check_vma=False)
```

```python
import functools

import jax
import jax.numpy as jnp
from jax import lax
from jax.experimental import pallas as pl
from jax.experimental.pallas import tpu as pltpu
from jax.sharding import PartitionSpec as P

BY = 32


def with_halo(cells, sides, width):
    for axis, dim in sides:
        count = lax.axis_size(axis)
        ends = count - 1
        head = lax.slice_in_dim(cells, 0, width, axis=dim)
        tail = lax.slice_in_dim(cells, cells.shape[dim] - width, cells.shape[dim], axis=dim)
        cells = jnp.concatenate(
            [
                lax.ppermute(tail, axis, [(i, (i + 1) % count) for i in range(ends)]),
                cells,
                lax.ppermute(head, axis, [((i + 1) % count, i) for i in range(ends)]),
            ],
            axis=dim,
        )
    return cells


def swapped(block, axis, stride):
    count = lax.axis_size(axis)
    route = []
    for low in range(count):
        high = low | 1 << stride
        if high != low and high < count:
            route += [(low, high), (high, low)]
    return lax.ppermute(block, axis, route)


def merged(part, axis, combine):
    gathered = lax.all_gather(part, axis)

    def take(source):
        return lax.dynamic_index_in_dim(gathered, source, 0, False)

    return lax.fori_loop(
        1, lax.axis_size(axis), lambda source, state: combine(state, take(source)), take(0)
    )


def product_kernel(
    n, shares, width, quot_ref, band_ref, cover_ref, out_ref, ext_ref, cols_ref, factor_ref,
    held, send1, recv1, send2, recv2, send_halo, recv_halo,
):
    groups = n // shares
    step, share_w, depth = held.shape[1:]
    taps_x = band_ref.shape[0]
    taps_y = quot_ref.shape[1] - share_w + 1
    rows = quot_ref.shape[0]
    me = lax.axis_index("view")
    view_id = me // shares
    part = me % shares
    layers = lax.axis_size("blk")
    layer = lax.axis_index("blk")
    up = (layer + 1) % layers
    down = (layer + layers - 1) % layers
    mesh_kind = pl.DeviceIdType.MESH
    barrier = pltpu.get_barrier_semaphore()
    for d in range(1, groups):
        pl.semaphore_signal(
            barrier, inc=1, device_id={"view": ((view_id + d) % groups) * shares + part},
            device_id_type=mesh_kind,
        )
    for d in range(1, shares):
        pl.semaphore_signal(
            barrier, inc=1, device_id={"view": view_id * shares + (part + d) % shares},
            device_id_type=mesh_kind,
        )
    has_up = layer < layers - 1
    has_down = layer > 0

    @pl.when(has_up)
    def _():
        pl.semaphore_signal(barrier, inc=1, device_id={"blk": up}, device_id_type=mesh_kind)

    @pl.when(has_down)
    def _():
        pl.semaphore_signal(barrier, inc=1, device_id={"blk": down}, device_id_type=mesh_kind)

    ext_ref[pl.ds(width, rows)] = quot_ref[...]

    def build_columns(first, count):
        for step_y in range(taps_y):
            cols_ref[pl.ds(first, count), :, step_y * depth : (step_y + 1) * depth] = ext_ref[
                pl.ds(first, count), step_y : step_y + share_w, :
            ]

    build_columns(width, rows)
    keep = cover_ref[...] > 0

    def factor_rows(target):
        acc = None
        for shift_x in range(taps_x):
            lhs = cols_ref[pl.ds(target * step + shift_x, step)].reshape(step * share_w, -1)
            part_sum = jnp.dot(lhs, band_ref[shift_x], preferred_element_type=jnp.float32)
            acc = part_sum if acc is None else acc + part_sum
        acc = acc.reshape(step, share_w, depth)
        factor_ref[pl.ds(target * step, step)] = jnp.where(keep[None], acc, 1.0)

    pl.semaphore_wait(
        barrier, groups + shares - 2 + has_up.astype(jnp.int32) + has_down.astype(jnp.int32)
    )
    to_up = pltpu.make_async_remote_copy(
        src_ref=quot_ref.at[pl.ds(rows - width, width)],
        dst_ref=ext_ref.at[pl.ds(0, width)],
        send_sem=send_halo.at[0],
        recv_sem=recv_halo.at[0],
        device_id={"blk": up},
        device_id_type=mesh_kind,
    )
    to_down = pltpu.make_async_remote_copy(
        src_ref=quot_ref.at[pl.ds(0, width)],
        dst_ref=ext_ref.at[pl.ds(rows + width, width)],
        send_sem=send_halo.at[1],
        recv_sem=recv_halo.at[1],
        device_id={"blk": down},
        device_id_type=mesh_kind,
    )
    @pl.when(has_up)
    def _():
        to_up.start()

    @pl.when(has_down)
    def _():
        to_down.start()

    reach = width // step
    inner = list(range(reach, groups - reach))
    outer = list(range(reach)) + list(range(groups - reach, groups))
    outgoing = []

    def send_chunk(target):
        factor_rows(target)
        copy = pltpu.make_async_remote_copy(
            src_ref=factor_ref.at[pl.ds(target * step, step)],
            dst_ref=held.at[view_id],
            send_sem=send1.at[target],
            recv_sem=recv1.at[view_id],
            device_id={"view": target * shares + part},
            device_id_type=mesh_kind,
        )

        @pl.when(target != view_id)
        def _():
            copy.start()

        outgoing.append((target, copy))

    for target in inner:
        send_chunk(target)
    @pl.when(has_up)
    def _():
        to_up.wait_send()
        to_down.wait_recv()

    @pl.when(has_down)
    def _():
        to_down.wait_send()
        to_up.wait_recv()

    @pl.when(layer == 0)
    def _():
        ext_ref[pl.ds(0, width)] = jnp.zeros((width,) + quot_ref.shape[1:], quot_ref.dtype)

    @pl.when(layer == layers - 1)
    def _():
        ext_ref[pl.ds(rows + width, width)] = jnp.zeros((width,) + quot_ref.shape[1:], quot_ref.dtype)

    build_columns(0, width)
    build_columns(rows + width, width)
    for target in outer:
        send_chunk(target)
    acc = factor_ref[pl.ds(view_id * step, step)]
    for d in range(1, groups):
        source = (view_id - d + groups) % groups
        pltpu.make_async_remote_copy(
            src_ref=factor_ref.at[pl.ds(0, step)],
            dst_ref=held.at[source],
            send_sem=send1.at[source],
            recv_sem=recv1.at[source],
            device_id={"view": source * shares + part},
            device_id_type=mesh_kind,
        ).wait_recv()
        acc = acc * held[source]
    for target, copy in outgoing:

        @pl.when(target != view_id)
        def _():
            copy.wait_send()

    mine = pl.ds(view_id * step, step)
    cols = pl.ds(part * share_w, share_w)
    out_ref[mine, cols, :] = acc
    outgoing = []
    for d in range(1, groups):
        target = (view_id + d) % groups
        copy = pltpu.make_async_remote_copy(
            src_ref=out_ref.at[mine, cols],
            dst_ref=out_ref.at[mine, cols],
            send_sem=send2.at[d],
            recv_sem=recv2.at[d],
            device_id={"view": target * shares + part},
            device_id_type=mesh_kind,
        )
        copy.start()
        outgoing.append(copy)
    for d in range(1, groups):
        source = (view_id - d + groups) % groups
        src_rows = pl.ds(source * step, step)
        pltpu.make_async_remote_copy(
            src_ref=out_ref.at[src_rows, cols],
            dst_ref=out_ref.at[src_rows, cols],
            send_sem=send2.at[d],
            recv_sem=recv2.at[d],
            device_id={"view": source * shares + part},
            device_id_type=mesh_kind,
        ).wait_recv()
    for copy in outgoing:
        copy.wait_send()
    outgoing = []
    for d in range(1, shares):
        other = (part + d) % shares
        copy = pltpu.make_async_remote_copy(
            src_ref=out_ref.at[:, cols],
            dst_ref=out_ref.at[:, cols],
            send_sem=send2.at[groups + d],
            recv_sem=recv2.at[groups + d],
            device_id={"view": view_id * shares + other},
            device_id_type=mesh_kind,
        )
        copy.start()
        outgoing.append(copy)
    for d in range(1, shares):
        other = (part - d + shares) % shares
        other_cols = pl.ds(other * share_w, share_w)
        pltpu.make_async_remote_copy(
            src_ref=out_ref.at[:, other_cols],
            dst_ref=out_ref.at[:, other_cols],
            send_sem=send2.at[groups + d],
            recv_sem=recv2.at[groups + d],
            device_id={"view": view_id * shares + other},
            device_id_type=mesh_kind,
        ).wait_recv()
    for copy in outgoing:
        copy.wait_send()


def product_gather(extended, banded, cover_plane, estimate, shares, width):
    n = lax.axis_size("view")
    groups = n // shares
    slab_x, width_y, depth = estimate.shape
    share_w = cover_plane.shape[0]
    step = slab_x // groups
    padded_rows = extended.shape[0] + 2 * width
    vmem = pl.BlockSpec(memory_space=pltpu.VMEM)
    return pl.pallas_call(
        functools.partial(product_kernel, n, shares, width),
        out_shape=jax.ShapeDtypeStruct(estimate.shape, jnp.float32),
        in_specs=[vmem] * 3,
        out_specs=vmem,
        scratch_shapes=[
            pltpu.VMEM((padded_rows,) + extended.shape[1:], extended.dtype),
            pltpu.VMEM((padded_rows, share_w, banded.shape[1]), jnp.bfloat16),
            pltpu.VMEM((slab_x, share_w, depth), jnp.float32),
            pltpu.VMEM((groups, step, share_w, depth), jnp.float32),
            pltpu.SemaphoreType.DMA((groups,)),
            pltpu.SemaphoreType.DMA((groups,)),
            pltpu.SemaphoreType.DMA((groups + shares,)),
            pltpu.SemaphoreType.DMA((groups + shares,)),
            pltpu.SemaphoreType.DMA((2,)),
            pltpu.SemaphoreType.DMA((2,)),
        ],
        compiler_params=pltpu.CompilerParams(collective_id=0, has_side_effects=True),
    )(extended, banded, cover_plane)


def band_table(kernel, depth):
    taps_x, taps_y, taps_z = kernel.shape
    rim_z = (taps_z - 1) // 2
    shape_three = (taps_z, depth, depth)
    offset = lax.broadcasted_iota(jnp.int32, shape_three, 1) - lax.broadcasted_iota(
        jnp.int32, shape_three, 2
    )
    onehot = (offset + rim_z == lax.broadcasted_iota(jnp.int32, shape_three, 0)).astype(
        jnp.bfloat16
    )
    banded = jnp.einsum("abt,tpz->abpz", kernel, onehot, preferred_element_type=jnp.float32).astype(
        jnp.bfloat16
    )
    return banded.reshape(taps_x, taps_y * depth, depth)


def conv_kernel(tile_x, src_ref, band_ref, image_ref, cover_ref, out_ref, cols_ref):
    rows_x, rows_y, depth = out_ref.shape
    taps_x = src_ref.shape[0] - rows_x + 1
    taps_y = src_ref.shape[1] - rows_y + 1
    for step_y in range(taps_y):
        cols_ref[:, :, step_y * depth : (step_y + 1) * depth] = src_ref[:, step_y : step_y + rows_y, :]
    keep = cover_ref[...] > 0
    for start in range(0, rows_x, tile_x):
        acc = None
        for shift_x in range(taps_x):
            lhs = cols_ref[start + shift_x : start + shift_x + tile_x].reshape(tile_x * rows_y, -1)
            part = jnp.dot(lhs, band_ref[shift_x], preferred_element_type=jnp.float32)
            acc = part if acc is None else acc + part
        blurred = acc.reshape(tile_x, rows_y, depth)
        ratio = image_ref[start : start + tile_x].astype(jnp.float32) / blurred
        out_ref[start : start + tile_x] = jnp.where(keep[None], ratio, 0.0).astype(out_ref.dtype)


def quotient_of(padded_part, banded, image, cover_plane):
    rows_x, rows_y, depth = image.shape
    vmem = pl.BlockSpec(memory_space=pltpu.VMEM)
    return pl.pallas_call(
        functools.partial(conv_kernel, 4),
        out_shape=jax.ShapeDtypeStruct((rows_x, rows_y, depth), jnp.bfloat16),
        in_specs=[vmem] * 4,
        out_specs=vmem,
        scratch_shapes=[pltpu.VMEM((padded_part.shape[0], rows_y, banded.shape[1]), jnp.bfloat16)],
    )(padded_part, banded, image, cover_plane)


def local(estimate, images, point_spread, covered):
    slab_x, width_y, depth = estimate.shape
    share_w = images.shape[2]
    view_count, taps_x, taps_y, taps_z = point_spread.shape
    rim_x, rim_y, rim_z = ((taps_x - 1) // 2, (taps_y - 1) // 2, (taps_z - 1) // 2)
    shares = width_y // share_w
    share_blocks = share_w // BY
    group = lax.axis_index("view")
    view_id = group // shares
    part = group % shares
    y_start = part * share_w
    source = estimate.astype(jnp.bfloat16)
    rimmed = with_halo(source, (("blk", 0),), rim_x)
    padded = jnp.pad(rimmed, ((0, 0), (rim_y, rim_y), (0, 0)))
    spread = lax.dynamic_index_in_dim(point_spread, view_id, 0, keepdims=False)
    totals = jnp.sum(point_spread, axis=(1, 2, 3))
    kernel = (spread / lax.dynamic_index_in_dim(totals, view_id, 0, keepdims=False)).astype(jnp.bfloat16)
    forward = band_table(kernel, depth)
    backward = band_table(kernel[::-1, ::-1, ::-1], depth)
    coverage_row = lax.dynamic_index_in_dim(covered[:, 0, :], view_id, 0, keepdims=False) > 0
    share_cover = lax.dynamic_slice_in_dim(coverage_row, part * share_blocks, share_blocks)
    cell_cover = jnp.repeat(share_cover, BY)[None, :, None]
    image = images[0]
    region = lax.dynamic_slice(
        padded, (0, y_start, 0), (slab_x + 2 * rim_x, share_w + 2 * rim_y, depth)
    )
    cover_plane = jnp.broadcast_to(cell_cover[0].astype(jnp.float32), (share_w, depth))
    quotient = quotient_of(region, forward, image, cover_plane)
    rim_zeros = jnp.zeros((slab_x, rim_y, depth), jnp.bfloat16)
    edge_rows = jnp.where(part == 0, quotient[:, share_w - rim_y :, :], quotient[:, :rim_y, :])
    partner = swapped(edge_rows, "view", 0)
    lower_rim = jnp.where(part > 0, partner, rim_zeros)
    upper_rim = jnp.where(part < shares - 1, partner, rim_zeros)
    extended = jnp.concatenate([lower_rim, quotient, upper_rim], axis=1)
    return estimate * product_gather(extended, backward, cover_plane, estimate, shares, rim_x)


def solution(mesh):
    in_specs = (P("blk", None, None), P("view", "blk", None, None), P(), P(None, "blk", None))
    out_specs = P("blk", None, None)
    return jax.shard_map(local, mesh=mesh, in_specs=in_specs, out_specs=out_specs, check_vma=False)
```

```python
import functools

import jax
import jax.numpy as jnp
from jax import lax
from jax.experimental import pallas as pl
from jax.experimental.pallas import tpu as pltpu
from jax.sharding import PartitionSpec as P

BY = 32


def with_halo(cells, sides, width):
    for axis, dim in sides:
        count = lax.axis_size(axis)
        ends = count - 1
        head = lax.slice_in_dim(cells, 0, width, axis=dim)
        tail = lax.slice_in_dim(cells, cells.shape[dim] - width, cells.shape[dim], axis=dim)
        cells = jnp.concatenate(
            [
                lax.ppermute(tail, axis, [(i, (i + 1) % count) for i in range(ends)]),
                cells,
                lax.ppermute(head, axis, [((i + 1) % count, i) for i in range(ends)]),
            ],
            axis=dim,
        )
    return cells


def swapped(block, axis, stride):
    count = lax.axis_size(axis)
    route = []
    for low in range(count):
        high = low | 1 << stride
        if high != low and high < count:
            route += [(low, high), (high, low)]
    return lax.ppermute(block, axis, route)


def merged(part, axis, combine):
    gathered = lax.all_gather(part, axis)

    def take(source):
        return lax.dynamic_index_in_dim(gathered, source, 0, False)

    return lax.fori_loop(
        1, lax.axis_size(axis), lambda source, state: combine(state, take(source)), take(0)
    )


def cover_mask(cover_ref, shares, share_w, depth):
    me = lax.axis_index("view")
    view_id = me // shares
    part = me % shares
    blocks = cover_ref.shape[1] // shares
    block_of = lax.broadcasted_iota(jnp.int32, (share_w, depth), 0) // (share_w // blocks)
    keep = block_of < 0
    for j in range(blocks):
        keep = keep | ((block_of == j) & (cover_ref[view_id, part * blocks + j] > 0))
    return keep


def product_kernel(
    n, shares, width, quot_ref, band_ref, cover_ref, out_ref, ext_ref, cols_ref, factor_ref,
    held, send1, recv1, send2, recv2, send_halo, recv_halo,
):
    groups = n // shares
    step, share_w, depth = held.shape[1:]
    taps_x = band_ref.shape[0]
    taps_y = quot_ref.shape[1] - share_w + 1
    rows = quot_ref.shape[0]
    me = lax.axis_index("view")
    view_id = me // shares
    part = me % shares
    layers = lax.axis_size("blk")
    layer = lax.axis_index("blk")
    up = (layer + 1) % layers
    down = (layer + layers - 1) % layers
    mesh_kind = pl.DeviceIdType.MESH
    barrier = pltpu.get_barrier_semaphore()
    for d in range(1, groups):
        pl.semaphore_signal(
            barrier, inc=1, device_id={"view": ((view_id + d) % groups) * shares + part},
            device_id_type=mesh_kind,
        )
    for d in range(1, shares):
        pl.semaphore_signal(
            barrier, inc=1, device_id={"view": view_id * shares + (part + d) % shares},
            device_id_type=mesh_kind,
        )
    has_up = layer < layers - 1
    has_down = layer > 0

    @pl.when(has_up)
    def _():
        pl.semaphore_signal(barrier, inc=1, device_id={"blk": up}, device_id_type=mesh_kind)

    @pl.when(has_down)
    def _():
        pl.semaphore_signal(barrier, inc=1, device_id={"blk": down}, device_id_type=mesh_kind)

    ext_ref[pl.ds(width, rows)] = quot_ref[...]

    def build_columns(first, count):
        for step_y in range(taps_y):
            cols_ref[pl.ds(first, count), :, step_y * depth : (step_y + 1) * depth] = ext_ref[
                pl.ds(first, count), step_y : step_y + share_w, :
            ]

    build_columns(width, rows)
    keep = cover_mask(cover_ref, shares, share_w, depth)

    def factor_rows(target):
        acc = None
        for shift_x in range(taps_x):
            lhs = cols_ref[pl.ds(target * step + shift_x, step)].reshape(step * share_w, -1)
            part_sum = jnp.dot(lhs, band_ref[shift_x], preferred_element_type=jnp.float32)
            acc = part_sum if acc is None else acc + part_sum
        acc = acc.reshape(step, share_w, depth)
        factor_ref[pl.ds(target * step, step)] = jnp.where(keep[None], acc, 1.0)

    pl.semaphore_wait(
        barrier, groups + shares - 2 + has_up.astype(jnp.int32) + has_down.astype(jnp.int32)
    )
    to_up = pltpu.make_async_remote_copy(
        src_ref=quot_ref.at[pl.ds(rows - width, width)],
        dst_ref=ext_ref.at[pl.ds(0, width)],
        send_sem=send_halo.at[0],
        recv_sem=recv_halo.at[0],
        device_id={"blk": up},
        device_id_type=mesh_kind,
    )
    to_down = pltpu.make_async_remote_copy(
        src_ref=quot_ref.at[pl.ds(0, width)],
        dst_ref=ext_ref.at[pl.ds(rows + width, width)],
        send_sem=send_halo.at[1],
        recv_sem=recv_halo.at[1],
        device_id={"blk": down},
        device_id_type=mesh_kind,
    )
    @pl.when(has_up)
    def _():
        to_up.start()

    @pl.when(has_down)
    def _():
        to_down.start()

    reach = width // step
    inner = list(range(reach, groups - reach))
    outer = list(range(reach)) + list(range(groups - reach, groups))
    outgoing = []

    def send_chunk(target):
        factor_rows(target)
        copy = pltpu.make_async_remote_copy(
            src_ref=factor_ref.at[pl.ds(target * step, step)],
            dst_ref=held.at[view_id],
            send_sem=send1.at[target],
            recv_sem=recv1.at[view_id],
            device_id={"view": target * shares + part},
            device_id_type=mesh_kind,
        )

        @pl.when(target != view_id)
        def _():
            copy.start()

        outgoing.append((target, copy))

    for target in inner:
        send_chunk(target)
    @pl.when(has_up)
    def _():
        to_up.wait_send()
        to_down.wait_recv()

    @pl.when(has_down)
    def _():
        to_down.wait_send()
        to_up.wait_recv()

    @pl.when(layer == 0)
    def _():
        ext_ref[pl.ds(0, width)] = jnp.zeros((width,) + quot_ref.shape[1:], quot_ref.dtype)

    @pl.when(layer == layers - 1)
    def _():
        ext_ref[pl.ds(rows + width, width)] = jnp.zeros((width,) + quot_ref.shape[1:], quot_ref.dtype)

    build_columns(0, width)
    build_columns(rows + width, width)
    for target in outer:
        send_chunk(target)
    acc = factor_ref[pl.ds(view_id * step, step)]
    for d in range(1, groups):
        source = (view_id - d + groups) % groups
        pltpu.make_async_remote_copy(
            src_ref=factor_ref.at[pl.ds(0, step)],
            dst_ref=held.at[source],
            send_sem=send1.at[source],
            recv_sem=recv1.at[source],
            device_id={"view": source * shares + part},
            device_id_type=mesh_kind,
        ).wait_recv()
        acc = acc * held[source]
    for target, copy in outgoing:

        @pl.when(target != view_id)
        def _():
            copy.wait_send()

    mine = pl.ds(view_id * step, step)
    cols = pl.ds(part * share_w, share_w)
    out_ref[mine, cols, :] = acc
    outgoing = []
    for d in range(1, groups):
        target = (view_id + d) % groups
        copy = pltpu.make_async_remote_copy(
            src_ref=out_ref.at[mine, cols],
            dst_ref=out_ref.at[mine, cols],
            send_sem=send2.at[d],
            recv_sem=recv2.at[d],
            device_id={"view": target * shares + part},
            device_id_type=mesh_kind,
        )
        copy.start()
        outgoing.append(copy)
    for d in range(1, groups):
        source = (view_id - d + groups) % groups
        src_rows = pl.ds(source * step, step)
        pltpu.make_async_remote_copy(
            src_ref=out_ref.at[src_rows, cols],
            dst_ref=out_ref.at[src_rows, cols],
            send_sem=send2.at[d],
            recv_sem=recv2.at[d],
            device_id={"view": source * shares + part},
            device_id_type=mesh_kind,
        ).wait_recv()
    for copy in outgoing:
        copy.wait_send()
    outgoing = []
    for d in range(1, shares):
        other = (part + d) % shares
        copy = pltpu.make_async_remote_copy(
            src_ref=out_ref.at[:, cols],
            dst_ref=out_ref.at[:, cols],
            send_sem=send2.at[groups + d],
            recv_sem=recv2.at[groups + d],
            device_id={"view": view_id * shares + other},
            device_id_type=mesh_kind,
        )
        copy.start()
        outgoing.append(copy)
    for d in range(1, shares):
        other = (part - d + shares) % shares
        other_cols = pl.ds(other * share_w, share_w)
        pltpu.make_async_remote_copy(
            src_ref=out_ref.at[:, other_cols],
            dst_ref=out_ref.at[:, other_cols],
            send_sem=send2.at[groups + d],
            recv_sem=recv2.at[groups + d],
            device_id={"view": view_id * shares + other},
            device_id_type=mesh_kind,
        ).wait_recv()
    for copy in outgoing:
        copy.wait_send()


def product_gather(extended, banded, cover_plane, estimate, shares, width):
    n = lax.axis_size("view")
    groups = n // shares
    slab_x, width_y, depth = estimate.shape
    share_w = extended.shape[1] - banded.shape[1] // depth + 1
    step = slab_x // groups
    padded_rows = extended.shape[0] + 2 * width
    vmem = pl.BlockSpec(memory_space=pltpu.VMEM)
    return pl.pallas_call(
        functools.partial(product_kernel, n, shares, width),
        out_shape=jax.ShapeDtypeStruct(estimate.shape, jnp.float32),
        in_specs=[vmem, vmem, pl.BlockSpec(memory_space=pltpu.SMEM)],
        out_specs=vmem,
        scratch_shapes=[
            pltpu.VMEM((padded_rows,) + extended.shape[1:], extended.dtype),
            pltpu.VMEM((padded_rows, share_w, banded.shape[1]), jnp.bfloat16),
            pltpu.VMEM((slab_x, share_w, depth), jnp.float32),
            pltpu.VMEM((groups, step, share_w, depth), jnp.float32),
            pltpu.SemaphoreType.DMA((groups,)),
            pltpu.SemaphoreType.DMA((groups,)),
            pltpu.SemaphoreType.DMA((groups + shares,)),
            pltpu.SemaphoreType.DMA((groups + shares,)),
            pltpu.SemaphoreType.DMA((2,)),
            pltpu.SemaphoreType.DMA((2,)),
        ],
        compiler_params=pltpu.CompilerParams(collective_id=0, has_side_effects=True),
    )(extended, banded, cover_plane)


def band_table(kernel, depth):
    taps_x, taps_y, taps_z = kernel.shape
    rim_z = (taps_z - 1) // 2
    shape_three = (taps_z, depth, depth)
    offset = lax.broadcasted_iota(jnp.int32, shape_three, 1) - lax.broadcasted_iota(
        jnp.int32, shape_three, 2
    )
    onehot = (offset + rim_z == lax.broadcasted_iota(jnp.int32, shape_three, 0)).astype(
        jnp.bfloat16
    )
    banded = jnp.einsum("abt,tpz->abpz", kernel, onehot, preferred_element_type=jnp.float32).astype(
        jnp.bfloat16
    )
    return banded.reshape(taps_x, taps_y * depth, depth)


def conv_kernel(tile_x, shares, src_ref, band_ref, image_ref, cover_ref, out_ref, cols_ref):
    rows_x, rows_y, depth = out_ref.shape
    taps_x = src_ref.shape[0] - rows_x + 1
    taps_y = src_ref.shape[1] - rows_y + 1
    for step_y in range(taps_y):
        cols_ref[:, :, step_y * depth : (step_y + 1) * depth] = src_ref[:, step_y : step_y + rows_y, :]
    keep = cover_mask(cover_ref, shares, rows_y, depth)
    for start in range(0, rows_x, tile_x):
        acc = None
        for shift_x in range(taps_x):
            lhs = cols_ref[start + shift_x : start + shift_x + tile_x].reshape(tile_x * rows_y, -1)
            part = jnp.dot(lhs, band_ref[shift_x], preferred_element_type=jnp.float32)
            acc = part if acc is None else acc + part
        blurred = acc.reshape(tile_x, rows_y, depth)
        ratio = image_ref[start : start + tile_x].astype(jnp.float32) / blurred
        out_ref[start : start + tile_x] = jnp.where(keep[None], ratio, 0.0).astype(out_ref.dtype)


def quotient_of(padded_part, banded, image, cover_plane, shares):
    rows_x, rows_y, depth = image.shape
    vmem = pl.BlockSpec(memory_space=pltpu.VMEM)
    return pl.pallas_call(
        functools.partial(conv_kernel, 4, shares),
        out_shape=jax.ShapeDtypeStruct((rows_x, rows_y, depth), jnp.bfloat16),
        in_specs=[vmem, vmem, vmem, pl.BlockSpec(memory_space=pltpu.SMEM)],
        out_specs=vmem,
        scratch_shapes=[pltpu.VMEM((padded_part.shape[0], rows_y, banded.shape[1]), jnp.bfloat16)],
    )(padded_part, banded, image, cover_plane)


def local(estimate, images, point_spread, covered):
    slab_x, width_y, depth = estimate.shape
    share_w = images.shape[2]
    view_count, taps_x, taps_y, taps_z = point_spread.shape
    rim_x, rim_y, rim_z = ((taps_x - 1) // 2, (taps_y - 1) // 2, (taps_z - 1) // 2)
    shares = width_y // share_w
    share_blocks = share_w // BY
    group = lax.axis_index("view")
    view_id = group // shares
    part = group % shares
    y_start = part * share_w
    source = estimate.astype(jnp.bfloat16)
    rimmed = with_halo(source, (("blk", 0),), rim_x)
    padded = jnp.pad(rimmed, ((0, 0), (rim_y, rim_y), (0, 0)))
    spread = lax.dynamic_index_in_dim(point_spread, view_id, 0, keepdims=False)
    kernel = (spread / jnp.sum(spread)).astype(jnp.bfloat16)
    forward = band_table(kernel, depth)
    backward = band_table(kernel[::-1, ::-1, ::-1], depth)
    coverage_row = lax.dynamic_index_in_dim(covered[:, 0, :], view_id, 0, keepdims=False) > 0
    share_cover = lax.dynamic_slice_in_dim(coverage_row, part * share_blocks, share_blocks)
    cell_cover = jnp.repeat(share_cover, BY)[None, :, None]
    image = images[0]
    region = lax.dynamic_slice(
        padded, (0, y_start, 0), (slab_x + 2 * rim_x, share_w + 2 * rim_y, depth)
    )
    cover_plane = covered[:, 0, :]
    quotient = quotient_of(region, forward, image, cover_plane, shares)
    rim_zeros = jnp.zeros((slab_x, rim_y, depth), jnp.bfloat16)
    edge_rows = jnp.where(part == 0, quotient[:, share_w - rim_y :, :], quotient[:, :rim_y, :])
    partner = swapped(edge_rows, "view", 0)
    lower_rim = jnp.where(part > 0, partner, rim_zeros)
    upper_rim = jnp.where(part < shares - 1, partner, rim_zeros)
    extended = jnp.concatenate([lower_rim, quotient, upper_rim], axis=1)
    return estimate * product_gather(extended, backward, cover_plane, estimate, shares, rim_x)


def solution(mesh):
    in_specs = (P("blk", None, None), P("view", "blk", None, None), P(), P(None, "blk", None))
    out_specs = P("blk", None, None)
    return jax.shard_map(local, mesh=mesh, in_specs=in_specs, out_specs=out_specs, check_vma=False)
```

```python
import functools

import jax
import jax.numpy as jnp
from jax import lax
from jax.experimental import pallas as pl
from jax.experimental.pallas import tpu as pltpu
from jax.sharding import PartitionSpec as P

BY = 32


def with_halo(cells, sides, width):
    for axis, dim in sides:
        count = lax.axis_size(axis)
        ends = count - 1
        head = lax.slice_in_dim(cells, 0, width, axis=dim)
        tail = lax.slice_in_dim(cells, cells.shape[dim] - width, cells.shape[dim], axis=dim)
        cells = jnp.concatenate(
            [
                lax.ppermute(tail, axis, [(i, (i + 1) % count) for i in range(ends)]),
                cells,
                lax.ppermute(head, axis, [((i + 1) % count, i) for i in range(ends)]),
            ],
            axis=dim,
        )
    return cells


def swapped(block, axis, stride):
    count = lax.axis_size(axis)
    route = []
    for low in range(count):
        high = low | 1 << stride
        if high != low and high < count:
            route += [(low, high), (high, low)]
    return lax.ppermute(block, axis, route)


def merged(part, axis, combine):
    gathered = lax.all_gather(part, axis)

    def take(source):
        return lax.dynamic_index_in_dim(gathered, source, 0, False)

    return lax.fori_loop(
        1, lax.axis_size(axis), lambda source, state: combine(state, take(source)), take(0)
    )


def cover_mask(cover_ref, shares, share_w, depth):
    me = lax.axis_index("view")
    view_id = me // shares
    part = me % shares
    blocks = cover_ref.shape[1] // shares
    block_of = lax.broadcasted_iota(jnp.int32, (share_w, depth), 0) // (share_w // blocks)
    keep = block_of < 0
    for j in range(blocks):
        keep = keep | ((block_of == j) & (cover_ref[view_id, part * blocks + j] > 0))
    return keep


def product_kernel(
    n, shares, width, quot_ref, band_ref, cover_ref, out_ref, ext_ref, cols_ref, factor_ref,
    held, send1, recv1, send2, recv2, send_halo, recv_halo,
):
    groups = n // shares
    step, share_w, depth = held.shape[1:]
    taps_x = band_ref.shape[0]
    taps_y = quot_ref.shape[1] - share_w + 1
    rows = quot_ref.shape[0]
    me = lax.axis_index("view")
    view_id = me // shares
    part = me % shares
    layers = lax.axis_size("blk")
    layer = lax.axis_index("blk")
    up = (layer + 1) % layers
    down = (layer + layers - 1) % layers
    mesh_kind = pl.DeviceIdType.MESH
    barrier = pltpu.get_barrier_semaphore()
    for d in range(1, groups):
        pl.semaphore_signal(
            barrier, inc=1, device_id={"view": ((view_id + d) % groups) * shares + part},
            device_id_type=mesh_kind,
        )
    for d in range(1, shares):
        pl.semaphore_signal(
            barrier, inc=1, device_id={"view": view_id * shares + (part + d) % shares},
            device_id_type=mesh_kind,
        )
    has_up = layer < layers - 1
    has_down = layer > 0

    @pl.when(has_up)
    def _():
        pl.semaphore_signal(barrier, inc=1, device_id={"blk": up}, device_id_type=mesh_kind)

    @pl.when(has_down)
    def _():
        pl.semaphore_signal(barrier, inc=1, device_id={"blk": down}, device_id_type=mesh_kind)


    def build_columns(first, count):
        for step_y in range(taps_y):
            cols_ref[pl.ds(first, count), :, step_y * depth : (step_y + 1) * depth] = ext_ref[
                pl.ds(first, count), step_y : step_y + share_w, :
            ]

    for step_y in range(taps_y):
        cols_ref[pl.ds(width, rows), :, step_y * depth : (step_y + 1) * depth] = quot_ref[
            :, step_y : step_y + share_w, :
        ]
    keep = cover_mask(cover_ref, shares, share_w, depth)

    def factor_rows(target):
        acc = None
        for shift_x in range(taps_x):
            lhs = cols_ref[pl.ds(target * step + shift_x, step)].reshape(step * share_w, -1)
            part_sum = jnp.dot(lhs, band_ref[shift_x], preferred_element_type=jnp.float32)
            acc = part_sum if acc is None else acc + part_sum
        acc = acc.reshape(step, share_w, depth)
        factor_ref[pl.ds(target * step, step)] = jnp.where(keep[None], acc, 1.0)

    pl.semaphore_wait(
        barrier, groups + shares - 2 + has_up.astype(jnp.int32) + has_down.astype(jnp.int32)
    )
    to_up = pltpu.make_async_remote_copy(
        src_ref=quot_ref.at[pl.ds(rows - width, width)],
        dst_ref=ext_ref.at[pl.ds(0, width)],
        send_sem=send_halo.at[0],
        recv_sem=recv_halo.at[0],
        device_id={"blk": up},
        device_id_type=mesh_kind,
    )
    to_down = pltpu.make_async_remote_copy(
        src_ref=quot_ref.at[pl.ds(0, width)],
        dst_ref=ext_ref.at[pl.ds(rows + width, width)],
        send_sem=send_halo.at[1],
        recv_sem=recv_halo.at[1],
        device_id={"blk": down},
        device_id_type=mesh_kind,
    )
    @pl.when(has_up)
    def _():
        to_up.start()

    @pl.when(has_down)
    def _():
        to_down.start()

    reach = width // step
    inner = list(range(reach, groups - reach))
    outer = list(range(reach)) + list(range(groups - reach, groups))
    outgoing = []

    def send_chunk(target):
        factor_rows(target)
        copy = pltpu.make_async_remote_copy(
            src_ref=factor_ref.at[pl.ds(target * step, step)],
            dst_ref=held.at[view_id],
            send_sem=send1.at[target],
            recv_sem=recv1.at[view_id],
            device_id={"view": target * shares + part},
            device_id_type=mesh_kind,
        )

        @pl.when(target != view_id)
        def _():
            copy.start()

        outgoing.append((target, copy))

    for target in inner:
        send_chunk(target)
    @pl.when(has_up)
    def _():
        to_up.wait_send()
        to_down.wait_recv()

    @pl.when(has_down)
    def _():
        to_down.wait_send()
        to_up.wait_recv()

    @pl.when(layer == 0)
    def _():
        ext_ref[pl.ds(0, width)] = jnp.zeros((width,) + quot_ref.shape[1:], quot_ref.dtype)

    @pl.when(layer == layers - 1)
    def _():
        ext_ref[pl.ds(rows + width, width)] = jnp.zeros((width,) + quot_ref.shape[1:], quot_ref.dtype)

    build_columns(0, width)
    build_columns(rows + width, width)
    for target in outer:
        send_chunk(target)
    acc = factor_ref[pl.ds(view_id * step, step)]
    for d in range(1, groups):
        source = (view_id - d + groups) % groups
        pltpu.make_async_remote_copy(
            src_ref=factor_ref.at[pl.ds(0, step)],
            dst_ref=held.at[source],
            send_sem=send1.at[source],
            recv_sem=recv1.at[source],
            device_id={"view": source * shares + part},
            device_id_type=mesh_kind,
        ).wait_recv()
        acc = acc * held[source]
    for target, copy in outgoing:

        @pl.when(target != view_id)
        def _():
            copy.wait_send()

    mine = pl.ds(view_id * step, step)
    cols = pl.ds(part * share_w, share_w)
    out_ref[mine, cols, :] = acc
    outgoing = []
    for d in range(1, groups):
        target = (view_id + d) % groups
        copy = pltpu.make_async_remote_copy(
            src_ref=out_ref.at[mine, cols],
            dst_ref=out_ref.at[mine, cols],
            send_sem=send2.at[d],
            recv_sem=recv2.at[d],
            device_id={"view": target * shares + part},
            device_id_type=mesh_kind,
        )
        copy.start()
        outgoing.append(copy)
    for d in range(1, groups):
        source = (view_id - d + groups) % groups
        src_rows = pl.ds(source * step, step)
        pltpu.make_async_remote_copy(
            src_ref=out_ref.at[src_rows, cols],
            dst_ref=out_ref.at[src_rows, cols],
            send_sem=send2.at[d],
            recv_sem=recv2.at[d],
            device_id={"view": source * shares + part},
            device_id_type=mesh_kind,
        ).wait_recv()
    for copy in outgoing:
        copy.wait_send()
    outgoing = []
    for d in range(1, shares):
        other = (part + d) % shares
        copy = pltpu.make_async_remote_copy(
            src_ref=out_ref.at[:, cols],
            dst_ref=out_ref.at[:, cols],
            send_sem=send2.at[groups + d],
            recv_sem=recv2.at[groups + d],
            device_id={"view": view_id * shares + other},
            device_id_type=mesh_kind,
        )
        copy.start()
        outgoing.append(copy)
    for d in range(1, shares):
        other = (part - d + shares) % shares
        other_cols = pl.ds(other * share_w, share_w)
        pltpu.make_async_remote_copy(
            src_ref=out_ref.at[:, other_cols],
            dst_ref=out_ref.at[:, other_cols],
            send_sem=send2.at[groups + d],
            recv_sem=recv2.at[groups + d],
            device_id={"view": view_id * shares + other},
            device_id_type=mesh_kind,
        ).wait_recv()
    for copy in outgoing:
        copy.wait_send()


def product_gather(extended, banded, cover_plane, estimate, shares, width):
    n = lax.axis_size("view")
    groups = n // shares
    slab_x, width_y, depth = estimate.shape
    share_w = extended.shape[1] - banded.shape[1] // depth + 1
    step = slab_x // groups
    padded_rows = extended.shape[0] + 2 * width
    vmem = pl.BlockSpec(memory_space=pltpu.VMEM)
    return pl.pallas_call(
        functools.partial(product_kernel, n, shares, width),
        out_shape=jax.ShapeDtypeStruct(estimate.shape, jnp.float32),
        in_specs=[vmem, vmem, pl.BlockSpec(memory_space=pltpu.SMEM)],
        out_specs=vmem,
        scratch_shapes=[
            pltpu.VMEM((padded_rows,) + extended.shape[1:], extended.dtype),
            pltpu.VMEM((padded_rows, share_w, banded.shape[1]), jnp.bfloat16),
            pltpu.VMEM((slab_x, share_w, depth), jnp.float32),
            pltpu.VMEM((groups, step, share_w, depth), jnp.float32),
            pltpu.SemaphoreType.DMA((groups,)),
            pltpu.SemaphoreType.DMA((groups,)),
            pltpu.SemaphoreType.DMA((groups + shares,)),
            pltpu.SemaphoreType.DMA((groups + shares,)),
            pltpu.SemaphoreType.DMA((2,)),
            pltpu.SemaphoreType.DMA((2,)),
        ],
        compiler_params=pltpu.CompilerParams(collective_id=0, has_side_effects=True),
    )(extended, banded, cover_plane)


def band_table(kernel, depth):
    taps_x, taps_y, taps_z = kernel.shape
    rim_z = (taps_z - 1) // 2
    shape_three = (taps_z, depth, depth)
    offset = lax.broadcasted_iota(jnp.int32, shape_three, 1) - lax.broadcasted_iota(
        jnp.int32, shape_three, 2
    )
    onehot = (offset + rim_z == lax.broadcasted_iota(jnp.int32, shape_three, 0)).astype(
        jnp.bfloat16
    )
    banded = jnp.einsum("abt,tpz->abpz", kernel, onehot, preferred_element_type=jnp.float32).astype(
        jnp.bfloat16
    )
    return banded.reshape(taps_x, taps_y * depth, depth)


def conv_kernel(tile_x, shares, src_ref, band_ref, image_ref, cover_ref, out_ref, cols_ref):
    rows_x, rows_y, depth = out_ref.shape
    taps_x = src_ref.shape[0] - rows_x + 1
    taps_y = src_ref.shape[1] - rows_y + 1
    for step_y in range(taps_y):
        cols_ref[:, :, step_y * depth : (step_y + 1) * depth] = src_ref[:, step_y : step_y + rows_y, :]
    keep = cover_mask(cover_ref, shares, rows_y, depth)
    for start in range(0, rows_x, tile_x):
        acc = None
        for shift_x in range(taps_x):
            lhs = cols_ref[start + shift_x : start + shift_x + tile_x].reshape(tile_x * rows_y, -1)
            part = jnp.dot(lhs, band_ref[shift_x], preferred_element_type=jnp.float32)
            acc = part if acc is None else acc + part
        blurred = acc.reshape(tile_x, rows_y, depth)
        ratio = image_ref[start : start + tile_x].astype(jnp.float32) / blurred
        out_ref[start : start + tile_x] = jnp.where(keep[None], ratio, 0.0).astype(out_ref.dtype)


def quotient_of(padded_part, banded, image, cover_plane, shares):
    rows_x, rows_y, depth = image.shape
    vmem = pl.BlockSpec(memory_space=pltpu.VMEM)
    return pl.pallas_call(
        functools.partial(conv_kernel, 4, shares),
        out_shape=jax.ShapeDtypeStruct((rows_x, rows_y, depth), jnp.bfloat16),
        in_specs=[vmem, vmem, vmem, pl.BlockSpec(memory_space=pltpu.SMEM)],
        out_specs=vmem,
        scratch_shapes=[pltpu.VMEM((padded_part.shape[0], rows_y, banded.shape[1]), jnp.bfloat16)],
    )(padded_part, banded, image, cover_plane)


def local(estimate, images, point_spread, covered):
    slab_x, width_y, depth = estimate.shape
    share_w = images.shape[2]
    view_count, taps_x, taps_y, taps_z = point_spread.shape
    rim_x, rim_y, rim_z = ((taps_x - 1) // 2, (taps_y - 1) // 2, (taps_z - 1) // 2)
    shares = width_y // share_w
    share_blocks = share_w // BY
    group = lax.axis_index("view")
    view_id = group // shares
    part = group % shares
    y_start = part * share_w
    source = estimate.astype(jnp.bfloat16)
    rimmed = with_halo(source, (("blk", 0),), rim_x)
    padded = jnp.pad(rimmed, ((0, 0), (rim_y, rim_y), (0, 0)))
    spread = lax.dynamic_index_in_dim(point_spread, view_id, 0, keepdims=False)
    kernel = (spread / jnp.sum(spread)).astype(jnp.bfloat16)
    forward = band_table(kernel, depth)
    backward = band_table(kernel[::-1, ::-1, ::-1], depth)
    coverage_row = lax.dynamic_index_in_dim(covered[:, 0, :], view_id, 0, keepdims=False) > 0
    share_cover = lax.dynamic_slice_in_dim(coverage_row, part * share_blocks, share_blocks)
    cell_cover = jnp.repeat(share_cover, BY)[None, :, None]
    image = images[0]
    region = lax.dynamic_slice(
        padded, (0, y_start, 0), (slab_x + 2 * rim_x, share_w + 2 * rim_y, depth)
    )
    cover_plane = covered[:, 0, :]
    quotient = quotient_of(region, forward, image, cover_plane, shares)
    rim_zeros = jnp.zeros((slab_x, rim_y, depth), jnp.bfloat16)
    edge_rows = jnp.where(part == 0, quotient[:, share_w - rim_y :, :], quotient[:, :rim_y, :])
    partner = swapped(edge_rows, "view", 0)
    lower_rim = jnp.where(part > 0, partner, rim_zeros)
    upper_rim = jnp.where(part < shares - 1, partner, rim_zeros)
    extended = jnp.concatenate([lower_rim, quotient, upper_rim], axis=1)
    return estimate * product_gather(extended, backward, cover_plane, estimate, shares, rim_x)


def solution(mesh):
    in_specs = (P("blk", None, None), P("view", "blk", None, None), P(), P(None, "blk", None))
    out_specs = P("blk", None, None)
    return jax.shard_map(local, mesh=mesh, in_specs=in_specs, out_specs=out_specs, check_vma=False)
```
